128 devices in a mesh: wide: 8 (over x, core), narrow: 16 (over z, y).
Axes of the slice: x: 4, y: 4, z: 4, core: 2. Of those that a mesh axis runs over, the one named last changes fastest.
Arguments:
- basis_t: bfloat16 [8192, 64, 256], P(('wide', 'narrow')), may hold values from -0.375 to 0.375
- nested_transfer_matrices: float32 [64, 64, 16384], P(None, None, ('wide', 'narrow')), may hold values from -0.22 to 0.93
- leaf_coupling: float32 [64, 64, 65536], P(None, None, ('wide', 'narrow')), may hold values from -6 to 6
- leaf_columns: int32 [65536], P(('wide', 'narrow')), may hold values from 0 to 8191, as said below
- far_coupling: float32 [64, 64, 2048], P(None, None, ('wide', 'narrow')), may hold values from -6 to 6
- far_columns: int32 [2048], P(('wide', 'narrow')), may hold values from 0 to 7, as said below
Outputs:
- leaf_coupled: float32 [64, 64, 65536], P(None, None, ('wide', 'narrow'))
- far_coupled: float32 [64, 64, 2048], P(None, None, ('wide', 'narrow'))
- group_factors: float32 [128, 64, 64], P(('wide', 'narrow'))
The draws below stay inside these ranges and needn't reach their ends.
Inputs may be any that keep to these rules, and one draw needn't show every extreme that they name: `leaf_columns`: block b's column leaf lies 2 to 64 leaves away from its row leaf b // 8; on every device some block lies exactly 64 leaves away. `far_columns`: block f's column branch differs from its row branch f // 256.
All inputs are finite; a program needn't handle non-finite values.
Results may differ from the reference program's by a relative error of at most 0.0003.
Values sent between devices are 32-bit elements; how exact they have to be, the bound alone decides.
No kernel may reach another device: no remote copies, remote signals or barrier semaphores. Data moves between devices by JAX's collectives and lax.ppermute only.
A program may use at most 192 MiB of HBM per device.

```python
import jax
import jax.numpy as jnp
from jax import lax

BASIS_RANK = 64
LEAF_SIZE = 256
LEAF_DEV = 64
NB = 8
BRANCH_COUPLINGS = 16
BRANCHES = 8
GROUP = 16
NLEAF = 8192
NBLK = 65536
NFAR = 2048
TRANSFER_SLOTS = 16384


def draw_nested_transfer_matrices(key, part):
    diagonal_jitter = jnp.clip(jax.random.normal(key, (BASIS_RANK, BASIS_RANK, TRANSFER_SLOTS), jnp.float32), -4.0, 4.0) * 0.3
    identity = jnp.eye(BASIS_RANK, dtype=jnp.float32)[:, :, None]
    return (identity + diagonal_jitter * BASIS_RANK ** (-0.5)) * 0.7071


def draw_leaf_columns(key, part):
    block_ids = jnp.arange(NBLK)
    row_leaf = block_ids // NB
    slot_index = block_ids % NB
    position = row_leaf % LEAF_DEV
    distance = jax.random.randint(key, (NBLK,), 2, LEAF_DEV + 1)
    distance = jnp.where((position == 0) & (slot_index == 0), LEAF_DEV, distance)
    distance = jnp.where((position == LEAF_DEV - 1) & (slot_index == 1), LEAF_DEV, distance)
    early_col = row_leaf - distance
    later_col = row_leaf + distance
    column = jnp.where(slot_index % 2 == 0, early_col, later_col)
    column = jnp.where(column < 0, later_col, column)
    column = jnp.where(column >= NLEAF, early_col, column)
    return column.astype(jnp.int32)


def draw_far_columns(key, part):
    block_ids = jnp.arange(NFAR)
    branch = block_ids // (GROUP * BRANCH_COUPLINGS)
    offset = jax.random.randint(key, (NFAR,), 0, BRANCHES - 1)
    return ((branch + 1 + offset) % BRANCHES).astype(jnp.int32)


def block_levels(own_key, extent, cuts, least, top_value):
    loudness, own = 1.0, jax.random.fold_in(own_key, 6)
    for dim, parts in cuts:
        steps = jnp.exp(jax.random.uniform(jax.random.fold_in(own, dim), (parts,), jnp.float32, least / len(cuts), top_value / len(cuts)))
        loudness = loudness * jnp.repeat(steps, extent[dim] // parts).reshape([-1 if axis == dim else 1 for axis in range(len(extent))])
    return loudness


def bell_draw(key, shape, spread, bound, split=(), kind=jnp.bfloat16):
    factor_of = block_levels(key, shape, split, -0.22, 0.18) if split else 1.0
    array = jax.random.normal(key, shape, jnp.float32) * spread * factor_of
    return jnp.minimum(jnp.maximum(array, -bound), bound).astype(kind)


def setup_inputs(seed: int = 0) -> dict:
    splits = jax.random.split(jax.random.key(seed), 7)
    return {
        "basis_t": bell_draw(splits[0], (NLEAF, BASIS_RANK, LEAF_SIZE), LEAF_SIZE ** -0.5, 0.375, ((0, 128),)),
        "nested_transfer_matrices": draw_nested_transfer_matrices(jax.random.fold_in(splits[6], 71), 0),
        "leaf_coupling": bell_draw(splits[2], (BASIS_RANK, BASIS_RANK, NBLK), 1.0, 6.0, ((2, 128),), jnp.float32),
        "leaf_columns": draw_leaf_columns(jax.random.fold_in(splits[6], 71), 0),
        "far_coupling": bell_draw(splits[4], (BASIS_RANK, BASIS_RANK, NFAR), 1.0, 6.0, ((2, 128),), jnp.float32),
        "far_columns": draw_far_columns(jax.random.fold_in(splits[6], 71), 0),
    }


HIGHEST = lax.Precision.HIGHEST

def cholesky_lower(gram_stack):
    full_shape = gram_stack.shape
    rank_size = full_shape[0]
    flat = gram_stack.reshape(rank_size, rank_size, -1)
    row_ids = jnp.arange(rank_size)

    def column_step(column, lower_now):
        row_part = lax.dynamic_index_in_dim(lower_now, column, 0, keepdims=False)
        target = lax.dynamic_index_in_dim(flat, column, 1, keepdims=False) - jnp.einsum('ikb,kb->ib', lower_now, row_part, precision=HIGHEST)
        pivot = jnp.sqrt(lax.dynamic_index_in_dim(target, column, 0, keepdims=False))
        update = jnp.where((row_ids >= column)[:, None], target / pivot[None, :], jnp.zeros_like(target))
        return lax.dynamic_update_index_in_dim(lower_now, update, column, 1)
    result = lax.fori_loop(0, rank_size, column_step, jnp.zeros_like(flat))
    return result.reshape(full_shape)

def join_term(gram_part, transfer_part):
    product = jnp.einsum('kl...,lj...->kj...', gram_part, transfer_part, precision=HIGHEST)
    return jnp.einsum('ki...,kj...->ij...', transfer_part, product, precision=HIGHEST)

def climb_local(gram_leaves, transfer):
    count_now = gram_leaves.shape[-1]
    current = gram_leaves
    while count_now > 1:
        terms_pair = join_term(current, transfer[..., count_now:2 * count_now])
        current = terms_pair[..., 0::2] + terms_pair[..., 1::2]
        count_now = count_now // 2
    return current

def reference(basis_t, nested_transfer_matrices, leaf_coupling, leaf_columns, far_coupling, far_columns):
    basis_wide = basis_t.astype(jnp.float32)
    leaf_gram = jnp.einsum('bkl,bml->kmb', basis_wide, basis_wide, precision=HIGHEST)
    leaf_lower = cholesky_lower(leaf_gram)
    device_count = NLEAF // LEAF_DEV
    transfer_dev = nested_transfer_matrices.reshape(BASIS_RANK, BASIS_RANK, device_count, 2 * LEAF_DEV)
    device_top = climb_local(leaf_gram.reshape(BASIS_RANK, BASIS_RANK, device_count, LEAF_DEV), transfer_dev)[..., 0]
    root_grams = device_top.reshape(BASIS_RANK, BASIS_RANK, BRANCHES, GROUP)
    root_trans = transfer_dev[..., 1].reshape(BASIS_RANK, BASIS_RANK, BRANCHES, GROUP)
    inner_trans = transfer_dev[..., 0].reshape(BASIS_RANK, BASIS_RANK, BRANCHES, GROUP)
    level_list = [root_grams]
    current = root_grams
    count_now = GROUP
    level = 0
    while count_now > 1:
        table = root_trans if level == 0 else inner_trans[..., count_now:2 * count_now]
        terms_pair = join_term(current, table)
        current = terms_pair[..., 0::2] + terms_pair[..., 1::2]
        level_list.append(current)
        count_now = count_now // 2
        level = level + 1
    top_level = len(level_list) - 1
    chosen_list = []
    for narrow_pos in range(GROUP):
        trailing = 0
        while narrow_pos >> trailing & 1 == 1:
            trailing = trailing + 1
        selected_level = trailing + 1
        if selected_level > top_level:
            chosen_list.append(level_list[0][..., narrow_pos])
        else:
            chosen_list.append(level_list[selected_level][..., narrow_pos >> selected_level])
    chosen = jnp.stack(chosen_list, axis=-1)
    group_lower = cholesky_lower(chosen)
    group_factors = jnp.transpose(group_lower, (2, 3, 1, 0)).reshape(device_count, BASIS_RANK, BASIS_RANK)
    branch_lower = cholesky_lower(level_list[top_level][..., 0])
    far_rows = jnp.arange(NFAR) // (GROUP * BRANCH_COUPLINGS)
    row_far_blocks = jnp.take(branch_lower, far_rows.astype(jnp.int32), axis=2)
    col_far = jnp.take(branch_lower, far_columns, axis=2)
    half_far = jnp.einsum('kif,kjf->ijf', row_far_blocks, far_coupling, precision=HIGHEST)
    far_coupled = jnp.einsum('ikf,kjf->ijf', half_far, col_far, precision=HIGHEST)
    blocks_four = leaf_coupling.reshape(BASIS_RANK, BASIS_RANK, NLEAF, NB)
    half_leaf = jnp.einsum('kib,kjbn->ijbn', leaf_lower, blocks_four, precision=HIGHEST)
    col_leaf = jnp.take(leaf_lower, leaf_columns, axis=2).reshape(BASIS_RANK, BASIS_RANK, NLEAF, NB)
    leaf_coupled = jnp.einsum('ikbn,kjbn->ijbn', half_leaf, col_leaf, precision=HIGHEST).reshape(BASIS_RANK, BASIS_RANK, NBLK)
    return (leaf_coupled, far_coupled, group_factors)
```

```python
import functools

import jax
import jax.numpy as jnp
from jax import lax
from jax.experimental import pallas as pl
from jax.experimental.pallas import tpu as pltpu
from jax.sharding import PartitionSpec as P

F32 = jnp.float32
BF16 = jnp.bfloat16


def split(x):
    hi = x.astype(BF16)
    lo = (x - hi.astype(F32)).astype(BF16)
    return hi, lo


def mm(a, b):
    return lax.dot_general(a, b, (((1,), (0,)), ((), ())), preferred_element_type=F32)


def mm_nt(a, b):
    return lax.dot_general(a, b, (((1,), (1,)), ((), ())), preferred_element_type=F32)


def half_kernel(c_ref, lt_ref, y_ref, s_ref):
    def turn(k, _):
        slab = jnp.concatenate([c_ref[k, :, 0:128], c_ref[k, :, 128:256]], axis=0)
        s_ref[:, k, :] = slab.T
        return 0

    lax.fori_loop(0, 64, turn, 0, unroll=4)
    lane = lax.broadcasted_iota(jnp.int32, (64, 1024), 1)
    first = (lane % 128) < 64

    def leaf(tp, _):
        w = jnp.concatenate([s_ref[tp * 8 + n] for n in range(8)], axis=1)
        wh, wl = split(w)
        lt = jnp.concatenate([lt_ref[tp], lt_ref[tp + 16]], axis=0)
        lh, ll = split(lt)
        left = jnp.concatenate([lh, ll, lh], axis=1)
        right = jnp.concatenate([wh, wh, wl], axis=0)
        z = mm(left, right)
        y = jnp.where(first, z[0:64], z[64:128])
        yh, yl = split(y)
        for n in range(8):
            y_ref[tp * 8 + n, :, 0:128] = yh[:, n * 128 : n * 128 + 128]
            y_ref[tp * 8 + n, :, 128:256] = yl[:, n * 128 : n * 128 + 128]
        return 0

    lax.fori_loop(0, 16, leaf, 0)


def half_leaf(coupling, lt):
    steps = coupling.shape[2] // 256
    return pl.pallas_call(
        half_kernel,
        out_shape=jax.ShapeDtypeStruct((steps * 128, 64, 256), BF16),
        grid=(steps,),
        in_specs=[
            pl.BlockSpec((64, 64, 256), lambda s: (0, 0, s)),
            pl.BlockSpec((32, 64, 64), lambda s: (s, 0, 0)),
        ],
        out_specs=pl.BlockSpec((128, 64, 256), lambda s: (s, 0, 0)),
        scratch_shapes=[pltpu.VMEM((128, 64, 128), F32)],
        compiler_params=pltpu.CompilerParams(vmem_limit_bytes=24 * 2**20),
        name="half_leaf",
    )(coupling, lt)


def full_kernel(cols_ref, y_ref, before_ref, own_ref, after_ref, o_ref, w_ref, s_ref):
    step = pl.program_id(0)

    @pl.when(step == 0)
    def _():
        lane = lax.broadcasted_iota(jnp.int32, (64, 128), 1)
        first = lane < 64
        zero = jnp.zeros((64, 128), BF16)

        def prep(q, _, low_ref, group):
            x = low_ref[q]
            h, l = split(x)
            hf = h.astype(F32)
            lf = l.astype(F32)
            hr = pltpu.roll(hf, 64, 1)
            lr = pltpu.roll(lf, 64, 1)
            base = group * 64 + q
            for c in range(2):
                t = base + 32 * c
                a_h, b_h = (hf, hr) if c == 0 else (hr, hf)
                a_l, b_l = (lf, lr) if c == 0 else (lr, lf)
                w_ref[t, 0:64, 0:128] = jnp.where(first, a_h, 0.0).astype(BF16)
                w_ref[t, 0:64, 128:256] = jnp.where(first, a_l, 0.0).astype(BF16)
                w_ref[t, 64:128, 0:128] = jnp.where(first, 0.0, b_h).astype(BF16)
                w_ref[t, 64:128, 128:256] = jnp.where(first, 0.0, b_l).astype(BF16)
            return 0

        for group, low_ref in enumerate((before_ref, own_ref, after_ref)):
            step_fn = functools.partial(prep, low_ref=low_ref, group=group)
            lax.fori_loop(0, 32, step_fn, 0, unroll=2)

    zero = jnp.zeros((128, 128), BF16)

    def pair(p, _):
        sa = cols_ref[step * 256 + p]
        sb = cols_ref[step * 256 + 128 + p]
        r = jnp.concatenate([w_ref[sa, 0:64, :], w_ref[sb, 64:128, :]], axis=0)
        bottom = jnp.concatenate([r[:, 0:128], zero], axis=1)
        right = jnp.concatenate([r, bottom], axis=0)
        z = mm(y_ref[p], right)
        s_ref[p] = z[:, 0:128] + z[:, 128:256]
        return 0

    lax.fori_loop(0, 128, pair, 0, unroll=4)

    def turn(i, _):
        x = s_ref[:, i, :].T
        o_ref[i, :, 0:128] = x[0:64]
        o_ref[i, :, 128:256] = x[64:128]
        return 0

    lax.fori_loop(0, 64, turn, 0, unroll=4)


def full_leaf(cols, y, before, own, after):
    steps = y.shape[0] // 128
    return pl.pallas_call(
        full_kernel,
        out_shape=jax.ShapeDtypeStruct((64, 64, steps * 256), F32),
        grid_spec=pltpu.PrefetchScalarGridSpec(
            num_scalar_prefetch=1,
            grid=(steps,),
            in_specs=[
                pl.BlockSpec((128, 64, 256), lambda s, c: (s, 0, 0)),
                pl.BlockSpec((32, 64, 128), lambda s, c: (0, 0, 0)),
                pl.BlockSpec((32, 64, 128), lambda s, c: (0, 0, 0)),
                pl.BlockSpec((32, 64, 128), lambda s, c: (0, 0, 0)),
            ],
            out_specs=pl.BlockSpec((64, 64, 256), lambda s, c: (0, 0, s)),
            scratch_shapes=[
                pltpu.VMEM((192, 128, 256), BF16),
                pltpu.VMEM((128, 64, 128), F32),
            ],
        ),
        compiler_params=pltpu.CompilerParams(vmem_limit_bytes=36 * 2**20),
        name="full_leaf",
    )(cols, y, before, own, after)


def chol_lanes(a_ref, count=64, panel=8):
    sub = lax.broadcasted_iota(jnp.int32, (8, 128), 0)
    for p in range(count // panel):
        base = p * panel
        if p > 0:
            for it in range(p, count // 8):

                def body(k, accs):
                    lv = a_ref[k, it * 8 : it * 8 + 8, :]
                    return tuple(
                        accs[j] - lv * a_ref[k, pl.ds(base + j, 8, stride=0), :]
                        for j in range(panel)
                    )

                accs = tuple(
                    a_ref[base + j, it * 8 : it * 8 + 8, :] for j in range(panel)
                )
                accs = lax.fori_loop(0, base, body, accs, unroll=8)
                for j in range(panel):
                    a_ref[base + j, it * 8 : it * 8 + 8, :] = accs[j]
        d = [a_ref[base + j, base : base + 8, :] for j in range(8)]
        invs = []
        for j in range(8):
            piv = jnp.broadcast_to(d[j][j : j + 1, :], (8, 128))
            inv = lax.rsqrt(piv)
            invs.append(inv)
            d[j] = jnp.where(sub >= j, d[j] * inv, 0.0)
            for m in range(j + 1, 8):
                d[m] = d[m] - d[j] * jnp.broadcast_to(d[j][m : m + 1, :], (8, 128))
            a_ref[base + j, base : base + 8, :] = d[j]
            if base > 0:
                a_ref[base + j, 0:base, :] = jnp.zeros((base, 128), F32)
        bc = {}
        for j in range(8):
            for m in range(j + 1, 8):
                bc[j, m] = jnp.broadcast_to(d[j][m : m + 1, :], (8, 128))
        for it in range(p + 1, count // 8):
            v = [a_ref[base + j, it * 8 : it * 8 + 8, :] for j in range(8)]
            for j in range(8):
                v[j] = v[j] * invs[j]
                for m in range(j + 1, 8):
                    v[m] = v[m] - v[j] * bc[j, m]
                a_ref[base + j, it * 8 : it * 8 + 8, :] = v[j]


def leaf_chol_kernel(g_ref, lt_ref, low_ref, a_ref):
    def load(k, _):
        x = g_ref[:, k, :]
        xx = jnp.concatenate([x[:, 0:64], x[:, 64:128]], axis=0)
        xp = jnp.concatenate([xx, jnp.zeros((64, 64), F32)], axis=0)
        a_ref[k] = xp.T
        return 0

    lax.fori_loop(0, 64, load, 0, unroll=4)
    chol_lanes(a_ref)

    def store_t(k, _):
        x = a_ref[k].T
        lt_ref[:, k, :] = x[0:64]
        return 0

    lax.fori_loop(0, 64, store_t, 0, unroll=4)

    def store_l(i, _):
        x = a_ref[:, i, :]
        slab = jnp.concatenate([x, pltpu.roll(x, 96, 1)], axis=0)
        low_ref[:, i, :] = slab.T[0:32]
        return 0

    lax.fori_loop(0, 64, store_l, 0, unroll=4)


def leaf_chol(gram):
    return pl.pallas_call(
        leaf_chol_kernel,
        out_shape=(
            jax.ShapeDtypeStruct((64, 64, 64), F32),
            jax.ShapeDtypeStruct((32, 64, 128), F32),
        ),
        scratch_shapes=[pltpu.VMEM((64, 64, 128), F32)],
        compiler_params=pltpu.CompilerParams(vmem_limit_bytes=12 * 2**20),
        name="leaf_chol",
    )(gram)


def climb_kernel(b_ref, t_ref, g_ref, top_ref, pay_ref, e_ref, n_ref):
    def turn(k, _):
        slab = jnp.concatenate([t_ref[k], t_ref[k + 32]], axis=0)
        x = slab.T
        e_ref[:, k, :] = x
        return 0

    lax.fori_loop(0, 32, turn, 0, unroll=4)

    def gram(t, _):
        b0 = b_ref[t]
        b1 = b_ref[t + 32]
        g0 = mm_nt(b0, b0)
        g1 = mm_nt(b1, b1)
        g_ref[t] = jnp.concatenate([g0, g1], axis=1)
        n_ref[64 + t] = g0
        n_ref[96 + t] = g1
        return 0

    lax.fori_loop(0, 32, gram, 0, unroll=4)

    def transfer(h):
        e = e_ref[h]
        return jnp.concatenate([e[:, 0:64], e[:, 64:128]], axis=0)

    def term(h):
        g = n_ref[h]
        e = transfer(h)
        gh, gl = split(g)
        eh, el = split(e)
        prod = mm(
            jnp.concatenate([gh, gl, gh], axis=1), jnp.concatenate([eh, eh, el], axis=0)
        )
        et = e.T
        th, tl = split(et)
        ph, pl_ = split(prod)
        return mm(
            jnp.concatenate([th, tl, th], axis=1), jnp.concatenate([ph, ph, pl_], axis=0)
        )

    for level in range(5, -1, -1):
        n = 2**level

        def parent(q, _, n=n):
            n_ref[n + q] = term(2 * (n + q)) + term(2 * (n + q) + 1)
            return 0

        lax.fori_loop(0, n, parent, 0, unroll=min(4, n))
    top_ref[...] = n_ref[1]
    pay_ref[...] = jnp.concatenate([term(1), transfer(0)], axis=1)


def climb(basis, transfers):
    m = jax.ShapeDtypeStruct((64, 64), F32)
    return pl.pallas_call(
        climb_kernel,
        out_shape=(
            jax.ShapeDtypeStruct((32, 64, 128), F32),
            m,
            jax.ShapeDtypeStruct((64, 128), F32),
        ),
        scratch_shapes=[
            pltpu.VMEM((128, 32, 128), F32),
            pltpu.VMEM((128, 64, 64), F32),
        ],
        compiler_params=pltpu.CompilerParams(vmem_limit_bytes=20 * 2**20),
        name="climb",
    )(basis, transfers)


def branch_kernel(
    at_ref, p0_ref, p1_ref, p2_ref, p3_ref, top_ref, gf_ref, low_ref, t_ref, e_ref, n_ref, q_ref, a_ref
):
    z = at_ref[0]
    y = at_ref[1]
    pick = at_ref[2]
    for u, ref in enumerate((p0_ref, p1_ref, p2_ref, p3_ref)):
        for s in range(4):
            n = ((z + 4 - u) % 4) * 4 + (y + 4 - s) % 4
            x = ref[s]
            t_ref[n] = x[:, 0:64]
            e_ref[n] = x[:, 64:128]
    n_ref[0] = top_ref[...]

    def term(h):
        g = n_ref[h]
        e = e_ref[h]
        gh, gl = split(g)
        eh, el = split(e)
        prod = mm(
            jnp.concatenate([gh, gl, gh], axis=1), jnp.concatenate([eh, eh, el], axis=0)
        )
        th, tl = split(e.T)
        ph, pl_ = split(prod)
        return mm(
            jnp.concatenate([th, tl, th], axis=1), jnp.concatenate([ph, ph, pl_], axis=0)
        )

    for m in range(8):
        n_ref[8 + m] = t_ref[2 * m] + t_ref[2 * m + 1]
    for level in (2, 1, 0):
        for q in range(2**level):
            p = 2**level + q
            n_ref[p] = term(2 * p) + term(2 * p + 1)

    zero = jnp.zeros((64, 64), F32)
    q_ref[...] = jnp.zeros((64, 8, 128), F32)
    q_ref[:, 0, :] = jnp.concatenate([n_ref[pick], zero], axis=1)
    q_ref[:, 1, :] = jnp.concatenate([n_ref[1], zero], axis=1)

    def load(k, _):
        x = jnp.concatenate([q_ref[k], jnp.zeros((120, 128), F32)], axis=0)
        a_ref[k] = x.T[0:64]
        return 0

    lax.fori_loop(0, 64, load, 0, unroll=4)
    chol_lanes(a_ref)

    def store(k, _):
        x = jnp.concatenate([a_ref[k], jnp.zeros((64, 128), F32)], axis=0)
        q_ref[k] = x.T[0:8]
        return 0

    lax.fori_loop(0, 64, store, 0, unroll=4)
    gf_ref[0] = q_ref[:, 0, :][:, 0:64]
    low_ref[...] = q_ref[:, 1, :][:, 0:64].T


def branch(at, parts, top):
    m = jax.ShapeDtypeStruct((64, 64), F32)
    vmem = pl.BlockSpec(memory_space=pltpu.VMEM)
    return pl.pallas_call(
        branch_kernel,
        out_shape=(jax.ShapeDtypeStruct((1, 64, 64), F32), m),
        in_specs=[pl.BlockSpec(memory_space=pltpu.SMEM)] + [vmem] * 5,
        out_specs=(vmem, vmem),
        scratch_shapes=[
            pltpu.VMEM((16, 64, 64), F32),
            pltpu.VMEM((16, 64, 64), F32),
            pltpu.VMEM((16, 64, 64), F32),
            pltpu.VMEM((64, 8, 128), F32),
            pltpu.VMEM((64, 64, 128), F32),
        ],
        compiler_params=pltpu.CompilerParams(vmem_limit_bytes=12 * 2**20),
        name="branch",
    )(at, *parts, top)


def far_kernel(cols_ref, f_ref, own_ref, *refs):
    others = refs[:7]
    o_ref, l_ref = refs[7:]
    own = own_ref[...]
    lh, ll = split(own.T)
    left = jnp.concatenate([lh, ll, lh], axis=1)
    for s, ref in enumerate((own_ref,) + tuple(others)):
        h, l = split(ref[...])
        l_ref[s] = jnp.concatenate([h, h, l], axis=0)
    for f in range(16):
        ch, cl = split(f_ref[:, f, :])
        half = mm(left, jnp.concatenate([ch, ch, cl], axis=0))
        hh, hl = split(half)
        o_ref[:, f, :] = mm(jnp.concatenate([hh, hl, hh], axis=1), l_ref[cols_ref[f]])


def far(cols, coupling, lowers):
    vmem = pl.BlockSpec(memory_space=pltpu.VMEM)
    return pl.pallas_call(
        far_kernel,
        out_shape=jax.ShapeDtypeStruct(coupling.shape, F32),
        in_specs=[pl.BlockSpec(memory_space=pltpu.SMEM)] + [vmem] * 9,
        out_specs=vmem,
        scratch_shapes=[pltpu.VMEM((8, 192, 64), BF16)],
        compiler_params=pltpu.CompilerParams(vmem_limit_bytes=8 * 2**20),
        name="far",
    )(cols, coupling, *lowers)


def shifted(value, axis, count, by):
    return lax.ppermute(value, axis, [(i, by(i)) for i in range(count)])


def steps(
    basis_t, nested_transfer_matrices, leaf_coupling, leaf_columns, far_coupling, far_columns
):
    both = ("wide", "narrow")
    branches = lax.axis_size("wide")
    group = lax.axis_size("narrow")
    wide_at = lax.axis_index("wide")
    at = lax.axis_index("narrow")
    gram, top, pay = climb(basis_t, nested_transfer_matrices)
    near = [pay] + [
        shifted(pay, "narrow", group, lambda i, s=s: (i // 4) * 4 + (i + s) % 4)
        for s in range(1, 4)
    ]
    near = jnp.stack(near)
    leaf_t, lower = leaf_chol(gram)
    ends = branches * group - 1
    before = lax.ppermute(lower, both, [(i, i + 1) for i in range(ends)])
    after = lax.ppermute(lower, both, [(i + 1, i) for i in range(ends)])
    parts = [near] + [
        shifted(near, "narrow", group, lambda i, s=s: (i + 4 * s) % 16) for s in range(1, 4)
    ]
    half = half_leaf(leaf_coupling, leaf_t)
    ones = 1 + sum(
        (at % 2**k == 2**k - 1).astype(jnp.int32) for k in range(1, 5)
    )
    pick = jnp.where(ones <= 4, (16 + at) >> ones, 0)
    place = jnp.stack([at // 4, at % 4, pick]).astype(jnp.int32)
    group_factors, low = branch(place, parts, top)
    lows = [low] + [
        shifted(low, "wide", branches, lambda i, s=s: (i + s) % branches)
        for s in range(1, branches)
    ]
    first = lax.axis_index(both) * 64 - 64
    leaf_coupled = full_leaf(leaf_columns - first, half, before, lower, after)
    far_in = jnp.transpose(far_coupling, (0, 2, 1))
    far_out = far((wide_at - far_columns) % branches, far_in, lows)
    return leaf_coupled, jnp.transpose(far_out, (0, 2, 1)), group_factors


def solution(mesh):
    spread = P(None, None, ("wide", "narrow"))
    in_specs = (
        P(("wide", "narrow"), None, None),
        spread,
        spread,
        P(("wide", "narrow")),
        spread,
        P(("wide", "narrow")),
    )
    return jax.shard_map(
        steps,
        mesh=mesh,
        in_specs=in_specs,
        out_specs=(spread, spread, P(("wide", "narrow"), None, None)),
        check_vma=False,
    )
```

```python
import functools

import jax
import jax.numpy as jnp
from jax import lax
from jax.experimental import pallas as pl
from jax.experimental.pallas import tpu as pltpu
from jax.sharding import PartitionSpec as P

F32 = jnp.float32
BF16 = jnp.bfloat16
ANY = pl.BlockSpec(memory_space=pl.ANY)
VMEM = pl.BlockSpec(memory_space=pltpu.VMEM)
SMEM = pl.BlockSpec(memory_space=pltpu.SMEM)


def params(mib):
    return pltpu.CompilerParams(vmem_limit_bytes=mib * 2**20)


def cost(us):
    return pl.CostEstimate(flops=int(us * 1.15e9), bytes_accessed=4096, transcendentals=0)


def split(x):
    hi = x.astype(BF16)
    lo = (x - hi.astype(F32)).astype(BF16)
    return hi, lo


def mm(a, b):
    return lax.dot_general(a, b, (((1,), (0,)), ((), ())), preferred_element_type=F32)


def mm_nt(a, b):
    return lax.dot_general(a, b, (((1,), (1,)), ((), ())), preferred_element_type=F32)


def mm_tn(a, b):
    return lax.dot_general(a, b, (((0,), (0,)), ((), ())), preferred_element_type=F32)


def lanes(*parts):
    return jnp.concatenate(parts, axis=1)


def rows(*parts):
    return jnp.concatenate(parts, axis=0)


def first_half(shape=(64, 128)):
    return lax.broadcasted_iota(jnp.int32, shape, 1) % 128 < 64


def left_of(m):
    h, l = split(m)
    v = jnp.where(first_half(), h, l)
    return lanes(v, v)


def right_of(m):
    return lanes(*split(m))


def twice(m):
    return rows(m, m)


def climb_kernel(b_hbm, t_hbm, g_ref, top_ref, pay_ref, b_ref, t_ref, e_ref, v_ref, sem):
    t_copies = [
        pltpu.make_async_copy(
            t_hbm.at[pl.ds(16 * n, 16)], t_ref.at[pl.ds(16 * n, 16)], sem.at[n]
        )
        for n in range(4)
    ]
    b_copies = [
        pltpu.make_async_copy(
            b_hbm.at[pl.ds(32 * n, 32)], b_ref.at[pl.ds(32 * n, 32)], sem.at[4 + n]
        )
        for n in range(2)
    ]
    for copy in t_copies + b_copies:
        copy.start()
    first = first_half()

    def turn(k, _):
        x = t_ref[k]
        e_ref[k] = rows(x, x).T
        return 0

    for n in range(4):
        t_copies[n].wait()
        lax.fori_loop(16 * n, 16 * n + 16, turn, 0, unroll=8)

    row = lax.broadcasted_iota(jnp.int32, (64, 128), 0)
    col = lax.broadcasted_iota(jnp.int32, (64, 128), 1)
    eye = (row == col).astype(F32)
    v_ref[1, :, 0:128] = lanes(eye[:, 0:64], eye[:, 0:64]).astype(BF16)
    v_ref[1, :, 128:256] = jnp.zeros((64, 128), BF16)

    def down(p, _):
        v = jnp.where(first, v_ref[p, :, 0:128], v_ref[p, :, 128:256])
        r0 = right_of(e_ref[:, 2 * p, :])
        r1 = right_of(e_ref[:, 2 * p + 1, :])
        z = mm_nt(lanes(v, v), rows(r0, r0, r1, r1))
        for c in range(2):
            v_ref[2 * p + c] = right_of(z[:, 128 * c : 128 * c + 128])
        return 0

    for level in range(6):
        n = 2**level
        lax.fori_loop(n, 2 * n, down, 0, unroll=min(8, n))
    for copy in b_copies:
        copy.wait()

    def leaf(q, acc):
        grams, prods, vs = [], [], []
        for c in range(2):
            t = q + 32 * c
            b = b_ref[t]
            g = mm_nt(b, twice(b))
            grams.append(g)
            v = v_ref[64 + t]
            vs.append(v)
            vv = jnp.where(first, v[:, 0:128], v[:, 128:256])
            prods.append(mm_nt(lanes(vv, vv), twice(right_of(g))))
        g_ref[q] = jnp.where(first, grams[0], grams[1])
        ph, pl_ = split(jnp.where(first, prods[0], prods[1]))
        vh = jnp.where(first, vs[0][:, 0:128], vs[1][:, 0:128])
        vl = jnp.where(first, vs[0][:, 128:256], vs[1][:, 128:256])
        right = lanes(vh, vh, vl)
        return acc + mm_nt(lanes(ph, pl_, ph), twice(right))

    top = lax.fori_loop(0, 32, leaf, jnp.zeros((64, 128), F32), unroll=8)
    top_ref[...] = top
    e = e_ref[:, 1, :]
    v = mm_nt(lanes(eye, eye).astype(BF16)[:, 0:128], twice(split(e)[0])) + mm_nt(
        eye.astype(BF16), twice(split(e)[1])
    )
    prod = mm_nt(left_of(v), twice(right_of(top)))
    vh, vl = split(v)
    term = mm_nt(left_of(prod), twice(lanes(vh, vl)))
    pay_ref[...] = jnp.where(first, term, e_ref[:, 0, :])


def climb(basis, transfers):
    return pl.pallas_call(
        climb_kernel,
        out_shape=(
            jax.ShapeDtypeStruct((32, 64, 128), F32),
            jax.ShapeDtypeStruct((64, 128), F32),
            jax.ShapeDtypeStruct((64, 128), F32),
        ),
        in_specs=[pl.BlockSpec(memory_space=pltpu.HBM)] * 2,
        out_specs=(VMEM,) * 3,
        scratch_shapes=[
            pltpu.VMEM((64, 64, 256), BF16),
            pltpu.VMEM((64, 64, 128), F32),
            pltpu.VMEM((64, 128, 128), F32),
            pltpu.VMEM((128, 64, 256), BF16),
            pltpu.SemaphoreType.DMA((6,)),
        ],
        compiler_params=params(20),
        cost_estimate=cost(10),
        name="climb",
    )(basis, transfers)


def chol_lanes(a_ref, count=64, panel=8):
    sub = lax.broadcasted_iota(jnp.int32, (8, 128), 0)
    for p in range(count // panel):
        base = p * panel
        if p > 0:
            for it in range(p, count // 8):

                def body(k, accs):
                    lv = a_ref[k, it * 8 : it * 8 + 8, :]
                    return tuple(
                        accs[j] - lv * a_ref[k, pl.ds(base + j, 8, stride=0), :]
                        for j in range(panel)
                    )

                accs = tuple(
                    a_ref[base + j, it * 8 : it * 8 + 8, :] for j in range(panel)
                )
                accs = lax.fori_loop(0, base, body, accs, unroll=8)
                for j in range(panel):
                    a_ref[base + j, it * 8 : it * 8 + 8, :] = accs[j]
        d = [a_ref[base + j, base : base + 8, :] for j in range(8)]
        invs = []
        for j in range(8):
            piv = jnp.broadcast_to(d[j][j : j + 1, :], (8, 128))
            inv = lax.rsqrt(piv)
            invs.append(inv)
            d[j] = jnp.where(sub >= j, d[j] * inv, 0.0)
            for m in range(j + 1, 8):
                d[m] = d[m] - d[j] * jnp.broadcast_to(d[j][m : m + 1, :], (8, 128))
            a_ref[base + j, base : base + 8, :] = d[j]
            if base > 0:
                a_ref[base + j, 0:base, :] = jnp.zeros((base, 128), F32)
        bc = {}
        for j in range(8):
            for m in range(j + 1, 8):
                bc[j, m] = jnp.broadcast_to(d[j][m : m + 1, :], (8, 128))
        for it in range(p + 1, count // 8):
            v = [a_ref[base + j, it * 8 : it * 8 + 8, :] for j in range(8)]
            for j in range(8):
                v[j] = v[j] * invs[j]
                for m in range(j + 1, 8):
                    v[m] = v[m] - v[j] * bc[j, m]
                a_ref[base + j, it * 8 : it * 8 + 8, :] = v[j]


def leaf_chol_kernel(g_ref, low_ref, a_ref):
    def load(k, _):
        x = g_ref[:, k, :]
        y = pltpu.roll(x, 64, 1)
        a_ref[k] = rows(x, y, x, y).T[0:64]
        return 0

    lax.fori_loop(0, 64, load, 0, unroll=8)
    chol_lanes(a_ref)

    def store(i, _):
        x = a_ref[:, i, :]
        low_ref[i] = rows(x, pltpu.roll(x, 96, 1)).T[0:32]
        return 0

    lax.fori_loop(0, 64, store, 0, unroll=8)


def leaf_chol(gram):
    return pl.pallas_call(
        leaf_chol_kernel,
        out_shape=jax.ShapeDtypeStruct((64, 32, 128), F32),
        in_specs=[VMEM],
        out_specs=VMEM,
        scratch_shapes=[pltpu.VMEM((64, 64, 128), F32)],
        compiler_params=params(8),
        cost_estimate=cost(6),
        name="leaf_chol",
    )(gram)


def half_kernel(c0_ref, c1_ref, low_ref, y_ref, s_ref, part):
    step = pl.program_id(0)

    def turn(k, _):
        s_ref[step * 16 + k] = rows(c0_ref[k], c1_ref[k]).T
        return 0

    lax.fori_loop(0, 16, turn, 0, unroll=8)

    @pl.when(step == 3)
    def _():
        first = first_half((64, 1024))

        def leaf(t, _):
            w = lanes(*[s_ref[:, t * 8 + n, :] for n in range(8)])
            wh, wl = split(w)
            lh, ll = split(low_ref[:, 16 * part + t, :])
            z = mm_tn(rows(lh, ll, lh), rows(wh, wh, wl))
            yh, yl = split(jnp.where(first, z[0:64], z[64:128]))
            for n in range(8):
                y_ref[t * 8 + n, :, 0:128] = yh[:, n * 128 : n * 128 + 128]
                y_ref[t * 8 + n, :, 128:256] = yl[:, n * 128 : n * 128 + 128]
            return 0

        lax.fori_loop(0, 16, leaf, 0, unroll=2)


def half_leaf(coupling, low, part):
    return pl.pallas_call(
        functools.partial(half_kernel, part=part),
        out_shape=jax.ShapeDtypeStruct((128, 64, 256), BF16),
        grid=(4,),
        in_specs=[
            pl.BlockSpec((16, 64, 128), lambda s: (s, 0, part)),
            pl.BlockSpec((16, 64, 128), lambda s: (s, 0, part + 2)),
            pl.BlockSpec((64, 32, 128), lambda s: (0, 0, 0)),
        ],
        out_specs=pl.BlockSpec((128, 64, 256), lambda s: (0, 0, 0)),
        scratch_shapes=[pltpu.VMEM((64, 128, 128), F32)],
        compiler_params=params(22),
        cost_estimate=cost(6),
    )(coupling, coupling, low)


def prep_kernel(before_ref, own_ref, after_ref, d_ref):
    first = first_half()
    for group, ref in enumerate((before_ref, own_ref, after_ref)):

        def pair(q, _, ref=ref, group=group):
            x = ref[:, q, :]
            y = pltpu.roll(x, 64, 1)
            d_ref[group * 64 + q] = right_of(jnp.where(first, x, y))
            d_ref[group * 64 + 32 + q] = right_of(jnp.where(first, y, x))
            return 0

        lax.fori_loop(0, 32, pair, 0, unroll=8)


def prep(before, own, after):
    return pl.pallas_call(
        prep_kernel,
        out_shape=jax.ShapeDtypeStruct((192, 64, 256), BF16),
        in_specs=[VMEM] * 3,
        out_specs=VMEM,
        compiler_params=params(16),
        cost_estimate=cost(3),
        name="prep",
    )(before, own, after)


def full_kernel(cols_ref, y_ref, d_ref, *refs, part, mode):
    out_ref, s_ref, o_ref, sem = refs[-4:]
    lane = lax.broadcasted_iota(jnp.int32, (64, 256), 1)
    keep = ((lane % 128) < 64).astype(BF16)
    drop = ((lane % 128) >= 64).astype(BF16)
    zero = jnp.zeros((128, 128), BF16)

    def pair(p, _):
        sa = cols_ref[part * 128 + p]
        sb = cols_ref[part * 128 + 256 + p]
        r = rows(d_ref[sa] * keep, d_ref[sb] * drop)
        y = y_ref[p]
        if mode == 0:
            z = mm(y, rows(r, lanes(r[:, 0:128], zero)))
            s_ref[p] = z[:, 0:128] + z[:, 128:256]
        else:
            z = mm(rows(y[:, 0:128], y[:, 128:256]), r)
            s_ref[p] = z[0:64, 0:128] + z[0:64, 128:256] + z[64:128, 0:128]
        return 0

    lax.fori_loop(0, 128, pair, 0, unroll=8)

    def send(n):
        return [
            pltpu.make_async_copy(
                o_ref.at[c, pl.ds(16 * n, 16)],
                out_ref.at[pl.ds(16 * n, 16), :, pl.ds((part + 2 * c) * 128, 128)],
                sem.at[n, c],
            )
            for c in range(2)
        ]

    def turn(i, _):
        x = s_ref[:, i, :].T
        o_ref[0, i] = x[0:64]
        o_ref[1, i] = x[64:128]
        return 0

    for n in range(4):
        lax.fori_loop(16 * n, 16 * n + 16, turn, 0, unroll=8)
        for copy in send(n):
            copy.start()
    for n in range(4):
        for copy in send(n):
            copy.wait()


def full_leaf(cols, y, d, part, into=None, mode=1):
    extra = [] if into is None else [into]
    return pl.pallas_call(
        functools.partial(full_kernel, part=part, mode=mode),
        out_shape=jax.ShapeDtypeStruct((64, 64, 512), F32),
        in_specs=[SMEM, VMEM, VMEM] + [pl.BlockSpec(memory_space=pltpu.HBM)] * len(extra),
        out_specs=pl.BlockSpec(memory_space=pltpu.HBM),
        scratch_shapes=[
            pltpu.VMEM((128, 64, 128), F32),
            pltpu.VMEM((2, 64, 64, 128), F32),
            pltpu.SemaphoreType.DMA((4, 2)),
        ],
        input_output_aliases={} if into is None else {3: 0},
        compiler_params=params(22),
        cost_estimate=cost(8),
    )(cols, y, d, *extra)


def branch_kernel(at_ref, p0, p1, p2, p3, p4, p5, top_ref, gf_ref, low_ref, t_ref, e_ref, n_ref, a_ref):
    at = at_ref[0]
    pick = at_ref[1]
    first = first_half()

    def place(n, x):
        y = pltpu.roll(x, 64, 1)
        t_ref[n] = jnp.where(first, x, y)
        e_ref[n] = jnp.where(first, y, x)

    place(at, p0[...])
    place(at ^ 1, p1[...])
    for i in range(2):
        place(at ^ (2 + i), p2[i])
    for s, ref in enumerate((p3, p4, p5)):
        for i in range(4):
            place((at ^ i) - 4 * (s + 1) & 15, ref[i])
    n_ref[0] = top_ref[...]
    row = lax.broadcasted_iota(jnp.int32, (64, 64), 0)
    col = lax.broadcasted_iota(jnp.int32, (64, 64), 1)
    eye = (row == col).astype(BF16)
    eye = lanes(eye, eye)

    def term(p):
        v = mm_nt(eye, twice(jnp.where(first, *split(e_ref[p]))))
        prod = mm_nt(left_of(v), twice(right_of(n_ref[p])))
        return mm_nt(left_of(prod), twice(right_of(v)))

    for m in range(8):
        n_ref[8 + m] = t_ref[2 * m] + t_ref[2 * m + 1]
    for level in (2, 1, 0):
        for p in range(2**level, 2 ** (level + 1)):
            n_ref[p] = term(2 * p) + term(2 * p + 1)

    both = jnp.where(first, n_ref[pick], n_ref[1])
    lane = lax.broadcasted_iota(jnp.int32, (64, 128), 1)

    def load(k, _):
        a_ref[k] = jnp.take_along_axis(both, (lane & 64) + k, axis=1)
        return 0

    lax.fori_loop(0, 64, load, 0, unroll=8)
    chol_lanes(a_ref)

    def store(k, out):
        return jnp.where((lane & 63) == k, a_ref[k], out)

    out = lax.fori_loop(0, 64, store, jnp.zeros((64, 128), F32), unroll=8)
    gf_ref[0] = out.T[0:64]
    low_ref[...] = jnp.where(first, pltpu.roll(out, 64, 1), out)


def branch(at, parts, top):
    return pl.pallas_call(
        branch_kernel,
        out_shape=(
            jax.ShapeDtypeStruct((1, 64, 64), F32),
            jax.ShapeDtypeStruct((64, 128), F32),
        ),
        in_specs=[SMEM] + [VMEM] * 7,
        out_specs=(VMEM, VMEM),
        scratch_shapes=[
            pltpu.VMEM((16, 64, 128), F32),
            pltpu.VMEM((16, 64, 128), F32),
            pltpu.VMEM((16, 64, 128), F32),
            pltpu.VMEM((64, 64, 128), F32),
        ],
        compiler_params=params(8),
        cost_estimate=cost(5),
        name="branch",
    )(at, *parts, top)


def far_kernel(cols_ref, f_ref, l0, l1, l2, l3, o_ref, l_ref):
    for s, part in enumerate((l0[...], l1[...], l2[0], l2[1], l3[0], l3[1], l3[2], l3[3])):
        h, l = split(part[:, 0:64])
        l_ref[s] = rows(h, h, l)
    lh, ll = split(l0[...].T[0:64])
    left = lanes(lh, ll, lh)
    for f in range(16):
        ch, cl = split(f_ref[:, f, :])
        hh, hl = split(mm(left, rows(ch, ch, cl)))
        o_ref[:, f, :] = mm(lanes(hh, hl, hh), l_ref[cols_ref[f]])


def far(cols, coupling, lowers):
    return pl.pallas_call(
        far_kernel,
        out_shape=jax.ShapeDtypeStruct(coupling.shape, F32),
        in_specs=[SMEM] + [VMEM] * 5,
        out_specs=VMEM,
        scratch_shapes=[pltpu.VMEM((8, 192, 64), BF16)],
        compiler_params=params(6),
        cost_estimate=cost(3),
        name="far",
    )(cols, coupling, *lowers)


def shifted(value, axis, to):
    return lax.ppermute(value, axis, [(i, to(i)) for i in range(lax.axis_size(axis))])


def steps(
    basis_t, nested_transfer_matrices, leaf_coupling, leaf_columns, far_coupling, far_columns
):
    basis_t, nested_transfer_matrices, leaf_coupling = (
        pltpu.with_memory_space_constraint(x, pltpu.HBM)
        for x in (basis_t, nested_transfer_matrices, leaf_coupling)
    )
    both = ("wide", "narrow")
    wide_at = lax.axis_index("wide")
    at = lax.axis_index("narrow")
    gram, top, pay = climb(basis_t, nested_transfer_matrices)
    pay_a = shifted(pay, "narrow", lambda i: i ^ 1)
    low = leaf_chol(gram)
    pair = jnp.stack([pay, pay_a])
    pay_b = shifted(pair, "narrow", lambda i: i ^ 2)
    ends = lax.axis_size(both) - 1
    before = lax.ppermute(low, both, [(i, i + 1) for i in range(ends)])
    after = lax.ppermute(low, both, [(i + 1, i) for i in range(ends)])
    half_a = half_leaf(leaf_coupling, low, 0)
    quad = jnp.concatenate([pair, pay_b])
    pay_c = [shifted(quad, "narrow", lambda i, s=s: (i + 4 * s) % 16) for s in (1, 2, 3)]
    half_b = half_leaf(leaf_coupling, low, 1)
    ones = 1 + sum((at % 2**k == 2**k - 1).astype(jnp.int32) for k in range(1, 5))
    pick = jnp.where(ones <= 4, (16 + at) >> ones, 0)
    place = jnp.stack([at, pick]).astype(jnp.int32)
    group_factors, own = branch(place, [pay, pay_a, pay_b, *pay_c], top)
    own_a = shifted(own, "wide", lambda i: i ^ 1)
    factors = prep(before, low, after)
    two = jnp.stack([own, own_a])
    own_b = shifted(two, "wide", lambda i: i ^ 2)
    cols = leaf_columns - (lax.axis_index(both) * 64 - 64)
    out = full_leaf(cols, half_a, factors, 0)
    four = jnp.concatenate([two, own_b])
    own_c = shifted(four, "wide", lambda i: i ^ 4)
    leaf_coupled = full_leaf(cols, half_b, factors, 1, out)
    far_out = far(
        wide_at ^ far_columns,
        jnp.transpose(far_coupling, (0, 2, 1)),
        [own, own_a, own_b, own_c],
    )
    return leaf_coupled, jnp.transpose(far_out, (0, 2, 1)), group_factors


def solution(mesh):
    spread = P(None, None, ("wide", "narrow"))
    split_first = P(("wide", "narrow"), None, None)
    ids = P(("wide", "narrow"))
    return jax.shard_map(
        steps,
        mesh=mesh,
        in_specs=(split_first, spread, spread, ids, spread, ids),
        out_specs=(spread, spread, split_first),
        check_vma=False,
    )
```

```python
import functools

import jax
import jax.numpy as jnp
from jax import lax
from jax.experimental import pallas as pl
from jax.experimental.pallas import tpu as pltpu
from jax.sharding import PartitionSpec as P

F32 = jnp.float32
BF16 = jnp.bfloat16
ANY = pl.BlockSpec(memory_space=pl.ANY)
VMEM = pl.BlockSpec(memory_space=pltpu.VMEM)
SMEM = pl.BlockSpec(memory_space=pltpu.SMEM)


def params(mib):
    return pltpu.CompilerParams(vmem_limit_bytes=mib * 2**20)


def cost(us):
    return pl.CostEstimate(flops=int(us * 1.15e9), bytes_accessed=4096, transcendentals=0)


def split(x):
    hi = x.astype(BF16)
    lo = (x - hi.astype(F32)).astype(BF16)
    return hi, lo


def mm(a, b):
    return lax.dot_general(a, b, (((1,), (0,)), ((), ())), preferred_element_type=F32)


def mm_nt(a, b):
    return lax.dot_general(a, b, (((1,), (1,)), ((), ())), preferred_element_type=F32)


def mm_tn(a, b):
    return lax.dot_general(a, b, (((0,), (0,)), ((), ())), preferred_element_type=F32)


def lanes(*parts):
    return jnp.concatenate(parts, axis=1)


def rows(*parts):
    return jnp.concatenate(parts, axis=0)


def first_half(shape=(64, 128)):
    return lax.broadcasted_iota(jnp.int32, shape, 1) % 128 < 64


def mixed(m):
    h = m.astype(BF16).astype(F32)
    return jnp.where(first_half(m.shape), h, m - h).astype(BF16)


def left_of(m):
    v = mixed(m)
    return lanes(v, v)


def right_of(m):
    return lanes(*split(m))


def twice(m):
    return rows(m, m)


LEAVES = 16
HALF = 4
PAIRS = 32


def climb_kernel(
    b_hbm, t_hbm, g_ref, top_ref, pay_ref, b_ref, t_ref, u_ref, e_ref, w_ref, sem
):
    t_copies = [
        pltpu.make_async_copy(
            t_hbm.at[pl.ds(16 * n, 16)], t_ref.at[pl.ds(16 * n, 16)], sem.at[n]
        )
        for n in range(4)
    ]
    b_copies = [
        pltpu.make_async_copy(
            b_hbm.at[pl.ds(32 * n, 32)], b_ref.at[pl.ds(32 * n, 32)], sem.at[4 + n]
        )
        for n in range(2)
    ]
    for copy in t_copies + b_copies:
        copy.start()
    first = first_half()

    def turn(s, _):
        for r in range(8):
            x = t_ref[s * 8 + r]
            u_ref[r] = rows(x, x).T
        for g in range(16):
            x = u_ref[:, 8 * g : 8 * g + 8, :]
            e_ref[8 * g : 8 * g + 8, pl.ds(pl.multiple_of(s * 8, 8), 8), :] = jnp.swapaxes(x, 0, 1)
        return 0

    for n in range(4):
        t_copies[n].wait()
        lax.fori_loop(2 * n, 2 * n + 2, turn, 0)

    row = lax.broadcasted_iota(jnp.int32, (64, 128), 0)
    col = lax.broadcasted_iota(jnp.int32, (64, 128), 1)
    w_ref[1, 0:64] = (row == col % 64).astype(BF16)
    w_ref[1, 64:128] = jnp.zeros((64, 128), BF16)

    def right_rows(h):
        w = w_ref[h]
        return rows(w[0:64], w[0:64], w[64:128], w[64:128])

    def down(clusters):
        zs = [
            mm(rows(left_of(e_ref[2 * p]), left_of(e_ref[2 * p + 1])), right_rows(p))
            for p in clusters
        ]
        for p, z in zip(clusters, zs):
            for c in range(2):
                w_ref[2 * p + c] = rows(*split(z[64 * c : 64 * c + 64]))

    def downs(s, _):
        down([s * 8 + j for j in range(8)])
        return 0

    for level in range(3):
        down(range(2**level, 2 ** (level + 1)))
    for level in range(3, 6):
        n = 2**level
        lax.fori_loop(n // 8, n // 4, downs, 0)
    for copy in b_copies:
        copy.wait()

    def leaves(s, acc):
        count = LEAVES // 2
        qs = [s * count + j for j in range(count)]
        ts = qs + [q + 32 for q in qs]
        bs = [b_ref[t] for t in ts]
        grams = [mm_nt(b, twice(b)) for b in bs]
        for j, q in enumerate(qs):
            g_ref[q] = jnp.where(first, grams[j], grams[count + j])
        prods = [mm(left_of(g), right_rows(64 + t)) for g, t in zip(grams, ts)]
        for p, t in zip(prods, ts):
            ph, pl_ = split(p)
            w = w_ref[64 + t][:, 0:64]
            acc = acc + mm_tn(rows(w, w), rows(ph, ph, pl_, pl_))
        return acc

    top = lax.fori_loop(0, 64 // LEAVES, leaves, jnp.zeros((64, 128), F32))
    top_ref[...] = top
    h, l = split(e_ref[1])
    prod = mm(left_of(top), rows(h, h, l, l))
    ph, pl_ = split(prod)
    up = rows(h, l).T[0:64]
    term = mm(lanes(up, up), rows(ph, ph, pl_, pl_))
    pay_ref[...] = jnp.where(first, term, e_ref[0])


def climb(basis, transfers):
    return pl.pallas_call(
        climb_kernel,
        out_shape=(
            jax.ShapeDtypeStruct((32, 64, 128), F32),
            jax.ShapeDtypeStruct((64, 128), F32),
            jax.ShapeDtypeStruct((64, 128), F32),
        ),
        in_specs=[pl.BlockSpec(memory_space=pltpu.HBM)] * 2,
        out_specs=(VMEM,) * 3,
        scratch_shapes=[
            pltpu.VMEM((64, 64, 256), BF16),
            pltpu.VMEM((64, 64, 128), F32),
            pltpu.VMEM((8, 128, 128), F32),
            pltpu.VMEM((128, 64, 128), F32),
            pltpu.VMEM((128, 128, 128), BF16),
            pltpu.SemaphoreType.DMA((6,)),
        ],
        compiler_params=params(20),
        cost_estimate=cost(10),
        name="climb",
    )(basis, transfers)


def chol_lanes(a_ref, count=64, panel=8):
    sub = lax.broadcasted_iota(jnp.int32, (8, 128), 0)
    for p in range(count // panel):
        base = p * panel
        if p > 0:
            for it in range(p, count // 8):

                def body(k, accs):
                    lv = a_ref[k, it * 8 : it * 8 + 8, :]
                    return tuple(
                        accs[j] - lv * a_ref[k, pl.ds(base + j, 8, stride=0), :]
                        for j in range(panel)
                    )

                accs = tuple(
                    a_ref[base + j, it * 8 : it * 8 + 8, :] for j in range(panel)
                )
                accs = lax.fori_loop(0, base, body, accs, unroll=8)
                for j in range(panel):
                    a_ref[base + j, it * 8 : it * 8 + 8, :] = accs[j]
        d = [a_ref[base + j, base : base + 8, :] for j in range(8)]
        invs = []
        for j in range(8):
            piv = jnp.broadcast_to(d[j][j : j + 1, :], (8, 128))
            inv = lax.rsqrt(piv)
            invs.append(inv)
            d[j] = jnp.where(sub >= j, d[j] * inv, 0.0)
            for m in range(j + 1, 8):
                d[m] = d[m] - d[j] * jnp.broadcast_to(d[j][m : m + 1, :], (8, 128))
            a_ref[base + j, base : base + 8, :] = d[j]
            if base > 0:
                a_ref[base + j, 0:base, :] = jnp.zeros((base, 128), F32)
        bc = {}
        for j in range(8):
            for m in range(j + 1, 8):
                bc[j, m] = jnp.broadcast_to(d[j][m : m + 1, :], (8, 128))
        for it in range(p + 1, count // 8):
            v = [a_ref[base + j, it * 8 : it * 8 + 8, :] for j in range(8)]
            for j in range(8):
                v[j] = v[j] * invs[j]
                for m in range(j + 1, 8):
                    v[m] = v[m] - v[j] * bc[j, m]
                a_ref[base + j, it * 8 : it * 8 + 8, :] = v[j]


def leaf_chol_kernel(g_ref, low_ref, a_ref, u_ref):
    def load(s, _):
        at = pl.ds(pl.multiple_of(s * 8, 8), 8)
        for g in range(4):
            u_ref[:, 8 * g : 8 * g + 8, :] = jnp.swapaxes(g_ref[8 * g : 8 * g + 8, at, :], 0, 1)
        for r in range(8):
            x = u_ref[r, 0:32, :]
            y = pltpu.roll(x, 64, 1)
            a_ref[s * 8 + r] = rows(x, y, x, y).T[0:64]
        return 0

    lax.fori_loop(0, 8, load, 0)
    chol_lanes(a_ref)

    def store(s, _):
        at = pl.ds(pl.multiple_of(s * 8, 8), 8)
        for g in range(8):
            u_ref[:, 8 * g : 8 * g + 8, :] = jnp.swapaxes(a_ref[8 * g : 8 * g + 8, at, :], 0, 1)
        for r in range(8):
            x = u_ref[r]
            u_ref[r, 0:32, :] = rows(x, pltpu.roll(x, 96, 1)).T[0:32]
        for g in range(4):
            low_ref[8 * g : 8 * g + 8, at, :] = jnp.swapaxes(u_ref[:, 8 * g : 8 * g + 8, :], 0, 1)
        return 0

    lax.fori_loop(0, 8, store, 0)


def leaf_chol(gram):
    return pl.pallas_call(
        leaf_chol_kernel,
        out_shape=jax.ShapeDtypeStruct((32, 64, 128), F32),
        in_specs=[VMEM],
        out_specs=VMEM,
        scratch_shapes=[pltpu.VMEM((64, 64, 128), F32), pltpu.VMEM((8, 64, 128), F32)],
        compiler_params=params(8),
        cost_estimate=cost(6),
        name="leaf_chol",
    )(gram)


def half_kernel(c0_ref, c1_ref, low_ref, y_ref, s_ref, u_ref, part):
    step = pl.program_id(0)

    def turn(s, _):
        for r in range(8):
            u_ref[r] = rows(c0_ref[s * 8 + r], c1_ref[s * 8 + r]).T
        at = pl.ds(pl.multiple_of(step * 16 + s * 8, 8), 8)
        for g in range(16):
            s_ref[8 * g : 8 * g + 8, at, :] = jnp.swapaxes(u_ref[:, 8 * g : 8 * g + 8, :], 0, 1)
        return 0

    lax.fori_loop(0, 2, turn, 0)

    @pl.when(step == 3)
    def _():
        first = first_half((64, 256))

        def leaf(s, _):
            ts = [s * HALF + j for j in range(HALF)]
            lefts = []
            for t in ts:
                lh, ll = split(low_ref[16 * part + t])
                lefts.append(rows(lh, ll, lh).T)
            at = [(j, n) for j in range(HALF) for n in range(0, 8, 2)]
            zs = []
            for j, n in at:
                wh, wl = split(lanes(s_ref[ts[j] * 8 + n], s_ref[ts[j] * 8 + n + 1]))
                zs.append(mm(lefts[j], rows(wh, wh, wl)))
            for (j, n), z in zip(at, zs):
                yh, yl = split(jnp.where(first, z[0:64], z[64:128]))
                for m in range(2):
                    b = ts[j] * 8 + n + m
                    y_ref[b, :, 0:128] = yh[:, m * 128 : m * 128 + 128]
                    y_ref[b, :, 128:256] = yl[:, m * 128 : m * 128 + 128]
            return 0

        lax.fori_loop(0, 16 // HALF, leaf, 0)


def half_leaf(coupling, low, part):
    return pl.pallas_call(
        functools.partial(half_kernel, part=part),
        out_shape=jax.ShapeDtypeStruct((128, 64, 256), BF16),
        grid=(4,),
        in_specs=[
            pl.BlockSpec((16, 64, 128), lambda s: (s, 0, part)),
            pl.BlockSpec((16, 64, 128), lambda s: (s, 0, part + 2)),
            pl.BlockSpec((32, 64, 128), lambda s: (0, 0, 0)),
        ],
        out_specs=pl.BlockSpec((128, 64, 256), lambda s: (0, 0, 0)),
        scratch_shapes=[pltpu.VMEM((128, 64, 128), F32), pltpu.VMEM((8, 128, 128), F32)],
        compiler_params=params(22),
        cost_estimate=cost(6),
    )(coupling, coupling, low)


def prep_kernel(before_ref, own_ref, after_ref, d_ref):
    first = first_half()
    for group, ref in enumerate((before_ref, own_ref, after_ref)):

        def pair(q, _, ref=ref, group=group):
            x = ref[q]
            y = pltpu.roll(x, 64, 1)
            d_ref[group * 64 + q] = right_of(jnp.where(first, x, y))
            d_ref[group * 64 + 32 + q] = right_of(jnp.where(first, y, x))
            return 0

        lax.fori_loop(0, 32, pair, 0, unroll=8)


def prep(before, own, after):
    return pl.pallas_call(
        prep_kernel,
        out_shape=jax.ShapeDtypeStruct((192, 64, 256), BF16),
        in_specs=[VMEM] * 3,
        out_specs=VMEM,
        compiler_params=params(16),
        cost_estimate=cost(3),
        name="prep",
    )(before, own, after)


def full_kernel(cols_ref, y_ref, d_ref, *refs, part):
    out_ref, s_ref, u_ref, o_ref, sem = refs[-5:]
    lane = lax.broadcasted_iota(jnp.int32, (64, 256), 1)
    keep = ((lane % 128) < 64).astype(BF16)
    drop = ((lane % 128) >= 64).astype(BF16)

    def pair(s, _):
        ps = [s * PAIRS + j for j in range(PAIRS)]
        zs = []
        for p in ps:
            sa = cols_ref[part * 128 + p]
            sb = cols_ref[part * 128 + 256 + p]
            r = rows(d_ref[sa] * keep, d_ref[sb] * drop)
            y = y_ref[p]
            zs.append(mm(rows(y[:, 0:128], y[:, 128:256]), r))
        for p, z in zip(ps, zs):
            s_ref[p] = z[0:64, 0:128] + z[0:64, 128:256] + z[64:128, 0:128]
        return 0

    lax.fori_loop(0, 128 // PAIRS, pair, 0)

    def send(n):
        return [
            pltpu.make_async_copy(
                o_ref.at[c, pl.ds(16 * n, 16)],
                out_ref.at[pl.ds(16 * n, 16), :, pl.ds((part + 2 * c) * 128, 128)],
                sem.at[n, c],
            )
            for c in range(2)
        ]

    def turn(s, _):
        at = pl.ds(pl.multiple_of(s * 8, 8), 8)
        for g in range(16):
            u_ref[:, 8 * g : 8 * g + 8, :] = jnp.swapaxes(s_ref[8 * g : 8 * g + 8, at, :], 0, 1)
        for r in range(8):
            x = u_ref[r].T
            o_ref[0, s * 8 + r] = x[0:64]
            o_ref[1, s * 8 + r] = x[64:128]
        return 0

    for n in range(4):
        lax.fori_loop(2 * n, 2 * n + 2, turn, 0)
        for copy in send(n):
            copy.start()
    for n in range(4):
        for copy in send(n):
            copy.wait()


def full_leaf(cols, y, d, part, into=None):
    extra = [] if into is None else [into]
    return pl.pallas_call(
        functools.partial(full_kernel, part=part),
        out_shape=jax.ShapeDtypeStruct((64, 64, 512), F32),
        in_specs=[SMEM, VMEM, VMEM] + [pl.BlockSpec(memory_space=pltpu.HBM)] * len(extra),
        out_specs=pl.BlockSpec(memory_space=pltpu.HBM),
        scratch_shapes=[
            pltpu.VMEM((128, 64, 128), F32),
            pltpu.VMEM((8, 128, 128), F32),
            pltpu.VMEM((2, 64, 64, 128), F32),
            pltpu.SemaphoreType.DMA((4, 2)),
        ],
        input_output_aliases={} if into is None else {3: 0},
        compiler_params=params(22),
        cost_estimate=cost(8),
    )(cols, y, d, *extra)


def branch_kernel(at_ref, p0, p1, p2, p3, p4, p5, top_ref, gf_ref, low_ref, t_ref, e_ref, n_ref, a_ref):
    at = at_ref[0]
    pick = at_ref[1]
    first = first_half()

    def place(n, x):
        y = pltpu.roll(x, 64, 1)
        t_ref[n] = jnp.where(first, x, y)
        e_ref[n] = jnp.where(first, y, x)

    place(at, p0[...])
    place(at ^ 1, p1[...])
    for i in range(2):
        place(at ^ (2 + i), p2[i])
    for s, ref in enumerate((p3, p4, p5)):
        for i in range(4):
            place((at ^ i) - 4 * (s + 1) & 15, ref[i])
    n_ref[0] = top_ref[...]
    for m in range(8):
        n_ref[8 + m] = t_ref[2 * m] + t_ref[2 * m + 1]
    ups = {}
    for p in range(2, 16):
        h, l = split(e_ref[p])
        ups[p] = rows(h, l).T[0:64]
    for level in (2, 1, 0):
        parents = range(2**level, 2 ** (level + 1))
        children = [c for p in parents for c in (2 * p, 2 * p + 1)]
        prods = []
        for c in children:
            h, l = split(e_ref[c])
            prods.append(mm(left_of(n_ref[c]), rows(h, h, l, l)))
        terms = []
        for c, prod in zip(children, prods):
            h, l = split(prod)
            terms.append(mm(lanes(ups[c], ups[c]), rows(h, h, l, l)))
        for n, p in enumerate(parents):
            n_ref[p] = terms[2 * n] + terms[2 * n + 1]

    both = jnp.where(first, n_ref[pick], n_ref[1])
    lane = lax.broadcasted_iota(jnp.int32, (64, 128), 1)

    def load(k, _):
        a_ref[k] = jnp.take_along_axis(both, (lane & 64) + k, axis=1)
        return 0

    lax.fori_loop(0, 64, load, 0, unroll=8)
    chol_lanes(a_ref)

    def store(k, out):
        return jnp.where((lane & 63) == k, a_ref[k], out)

    out = lax.fori_loop(0, 64, store, jnp.zeros((64, 128), F32), unroll=8)
    gf_ref[0] = out.T[0:64]
    low_ref[...] = jnp.where(first, pltpu.roll(out, 64, 1), out)


def branch(at, parts, top):
    return pl.pallas_call(
        branch_kernel,
        out_shape=(
            jax.ShapeDtypeStruct((1, 64, 64), F32),
            jax.ShapeDtypeStruct((64, 128), F32),
        ),
        in_specs=[SMEM] + [VMEM] * 7,
        out_specs=(VMEM, VMEM),
        scratch_shapes=[
            pltpu.VMEM((16, 64, 128), F32),
            pltpu.VMEM((16, 64, 128), F32),
            pltpu.VMEM((16, 64, 128), F32),
            pltpu.VMEM((64, 64, 128), F32),
        ],
        compiler_params=params(8),
        cost_estimate=cost(5),
        name="branch",
    )(at, *parts, top)


def far_kernel(cols_ref, f_ref, l0, l1, l2, l3, o_ref, l_ref, c_ref):
    for s, part in enumerate((l0[...], l1[...], l2[0], l2[1], l3[0], l3[1], l3[2], l3[3])):
        h, l = split(part[:, 0:64])
        l_ref[s] = rows(h, h, l)
    lh, ll = split(l0[...].T[0:64])
    left = lanes(lh, ll, lh)
    halves = []
    for g in range(2):
        for s in range(8):
            x = f_ref[8 * s : 8 * s + 8, 8 * g : 8 * g + 8, :]
            c_ref[8 * g : 8 * g + 8, 8 * s : 8 * s + 8, :] = jnp.swapaxes(x, 0, 1)
        for f in range(8 * g, 8 * g + 8):
            ch, cl = split(c_ref[f])
            halves.append(mm(left, rows(ch, ch, cl)))
    outs = []
    for f in range(16):
        hh, hl = split(halves[f])
        outs.append(mm(lanes(hh, hl, hh), l_ref[cols_ref[f]]))
    for f in range(16):
        c_ref[f] = outs[f]
    for g in range(2):
        for s in range(8):
            x = c_ref[8 * g : 8 * g + 8, 8 * s : 8 * s + 8, :]
            o_ref[8 * s : 8 * s + 8, 8 * g : 8 * g + 8, :] = jnp.swapaxes(x, 0, 1)


def far(cols, coupling, lowers):
    return pl.pallas_call(
        far_kernel,
        out_shape=jax.ShapeDtypeStruct(coupling.shape, F32),
        in_specs=[SMEM] + [VMEM] * 5,
        out_specs=VMEM,
        scratch_shapes=[pltpu.VMEM((8, 192, 64), BF16), pltpu.VMEM((16, 64, 64), F32)],
        compiler_params=params(6),
        cost_estimate=cost(3),
        name="far",
    )(cols, coupling, *lowers)


def shifted(value, axis, to):
    return lax.ppermute(value, axis, [(i, to(i)) for i in range(lax.axis_size(axis))])


def steps(
    basis_t, nested_transfer_matrices, leaf_coupling, leaf_columns, far_coupling, far_columns
):
    basis_t, nested_transfer_matrices, leaf_coupling = (
        pltpu.with_memory_space_constraint(x, pltpu.HBM)
        for x in (basis_t, nested_transfer_matrices, leaf_coupling)
    )
    both = ("wide", "narrow")
    wide_at = lax.axis_index("wide")
    at = lax.axis_index("narrow")
    gram, top, pay = climb(basis_t, nested_transfer_matrices)
    pay_a = shifted(pay, "narrow", lambda i: i ^ 1)
    low = leaf_chol(gram)
    pair = jnp.stack([pay, pay_a])
    pay_b = shifted(pair, "narrow", lambda i: i ^ 2)
    ends = lax.axis_size(both) - 1
    before = lax.ppermute(low, both, [(i, i + 1) for i in range(ends)])
    after = lax.ppermute(low, both, [(i + 1, i) for i in range(ends)])
    half_a = half_leaf(leaf_coupling, low, 0)
    quad = jnp.concatenate([pair, pay_b])
    pay_c = [shifted(quad, "narrow", lambda i, s=s: (i + 4 * s) % 16) for s in (1, 2, 3)]
    half_b = half_leaf(leaf_coupling, low, 1)
    ones = 1 + sum((at % 2**k == 2**k - 1).astype(jnp.int32) for k in range(1, 5))
    pick = jnp.where(ones <= 4, (16 + at) >> ones, 0)
    place = jnp.stack([at, pick]).astype(jnp.int32)
    group_factors, own = branch(place, [pay, pay_a, pay_b, *pay_c], top)
    own_a = shifted(own, "wide", lambda i: i ^ 1)
    factors = prep(before, low, after)
    two = jnp.stack([own, own_a])
    own_b = shifted(two, "wide", lambda i: i ^ 2)
    cols = leaf_columns - (lax.axis_index(both) * 64 - 64)
    out = full_leaf(cols, half_a, factors, 0)
    four = jnp.concatenate([two, own_b])
    own_c = shifted(four, "wide", lambda i: i ^ 4)
    leaf_coupled = full_leaf(cols, half_b, factors, 1, out)
    far_out = far(
        wide_at ^ far_columns,
        jnp.transpose(far_coupling, (0, 2, 1)),
        [own, own_a, own_b, own_c],
    )
    return leaf_coupled, jnp.transpose(far_out, (0, 2, 1)), group_factors


def solution(mesh):
    spread = P(None, None, ("wide", "narrow"))
    split_first = P(("wide", "narrow"), None, None)
    ids = P(("wide", "narrow"))
    return jax.shard_map(
        steps,
        mesh=mesh,
        in_specs=(split_first, spread, spread, ids, spread, ids),
        out_specs=(spread, spread, split_first),
        check_vma=False,
    )
```

```python
import functools

import jax
import jax.numpy as jnp
from jax import lax
from jax.experimental import pallas as pl
from jax.experimental.pallas import tpu as pltpu
from jax.sharding import PartitionSpec as P

F32 = jnp.float32
BF16 = jnp.bfloat16
ANY = pl.BlockSpec(memory_space=pl.ANY)
VMEM = pl.BlockSpec(memory_space=pltpu.VMEM)
SMEM = pl.BlockSpec(memory_space=pltpu.SMEM)


def params(mib):
    return pltpu.CompilerParams(vmem_limit_bytes=mib * 2**20)


def cost(us):
    return pl.CostEstimate(flops=int(us * 1.15e9), bytes_accessed=4096, transcendentals=0)


def split(x):
    hi = x.astype(BF16)
    lo = (x - hi.astype(F32)).astype(BF16)
    return hi, lo


def mm(a, b):
    return lax.dot_general(a, b, (((1,), (0,)), ((), ())), preferred_element_type=F32)


def mm_nt(a, b):
    return lax.dot_general(a, b, (((1,), (1,)), ((), ())), preferred_element_type=F32)


def mm_tn(a, b):
    return lax.dot_general(a, b, (((0,), (0,)), ((), ())), preferred_element_type=F32)


def lanes(*parts):
    return jnp.concatenate(parts, axis=1)


def rows(*parts):
    return jnp.concatenate(parts, axis=0)


def first_half(shape=(64, 128)):
    return lax.broadcasted_iota(jnp.int32, shape, 1) % 128 < 64


def mixed(m):
    h = m.astype(BF16).astype(F32)
    return jnp.where(first_half(m.shape), h, m - h).astype(BF16)


def left_of(m):
    v = mixed(m)
    return lanes(v, v)


def right_of(m):
    return lanes(*split(m))


def twice(m):
    return rows(m, m)


LEAVES = 16
HALF = 4
PAIRS = 32


def climb_kernel(
    b_hbm, t_hbm, g_ref, top_ref, pay_ref, b_ref, t_ref, u_ref, e_ref, w_ref, sem
):
    t_copies = [
        pltpu.make_async_copy(
            t_hbm.at[pl.ds(16 * n, 16)], t_ref.at[pl.ds(16 * n, 16)], sem.at[n]
        )
        for n in range(4)
    ]
    b_copies = [
        pltpu.make_async_copy(
            b_hbm.at[pl.ds(32 * n, 32)], b_ref.at[pl.ds(32 * n, 32)], sem.at[4 + n]
        )
        for n in range(2)
    ]
    for copy in t_copies + b_copies:
        copy.start()
    first = first_half()

    def turn(s, _):
        for r in range(8):
            x = t_ref[s * 8 + r]
            u_ref[r] = rows(x, x).T
        for g in range(16):
            x = u_ref[:, 8 * g : 8 * g + 8, :]
            e_ref[8 * g : 8 * g + 8, pl.ds(pl.multiple_of(s * 8, 8), 8), :] = jnp.swapaxes(x, 0, 1)
        return 0

    for n in range(4):
        t_copies[n].wait()
        lax.fori_loop(2 * n, 2 * n + 2, turn, 0)

    row = lax.broadcasted_iota(jnp.int32, (64, 128), 0)
    col = lax.broadcasted_iota(jnp.int32, (64, 128), 1)
    w_ref[1, 0:64] = (row == col % 64).astype(BF16)
    w_ref[1, 64:128] = jnp.zeros((64, 128), BF16)

    def right_rows(h):
        w = w_ref[h]
        return rows(w[0:64], w[0:64], w[64:128], w[64:128])

    def down(clusters):
        zs = [
            mm(rows(left_of(e_ref[2 * p]), left_of(e_ref[2 * p + 1])), right_rows(p))
            for p in clusters
        ]
        for p, z in zip(clusters, zs):
            for c in range(2):
                w_ref[2 * p + c] = rows(*split(z[64 * c : 64 * c + 64]))

    def downs(s, _):
        down([s * 8 + j for j in range(8)])
        return 0

    for level in range(3):
        down(range(2**level, 2 ** (level + 1)))
    for level in range(3, 6):
        n = 2**level
        lax.fori_loop(n // 8, n // 4, downs, 0)
    for copy in b_copies:
        copy.wait()

    def leaves(s, acc):
        count = LEAVES // 2
        qs = [s * count + j for j in range(count)]
        ts = qs + [q + 32 for q in qs]
        bs = [b_ref[t] for t in ts]
        grams = [mm_nt(b, twice(b)) for b in bs]
        for j, q in enumerate(qs):
            g_ref[q] = jnp.where(first, grams[j], grams[count + j])
        prods = [mm(left_of(g), right_rows(64 + t)) for g, t in zip(grams, ts)]
        for p, t in zip(prods, ts):
            ph, pl_ = split(p)
            w = w_ref[64 + t][:, 0:64]
            acc = acc + mm_tn(rows(w, w), rows(ph, ph, pl_, pl_))
        return acc

    top = lax.fori_loop(0, 64 // LEAVES, leaves, jnp.zeros((64, 128), F32))
    top_ref[...] = top
    h, l = split(e_ref[1])
    prod = mm(left_of(top), rows(h, h, l, l))
    ph, pl_ = split(prod)
    up = rows(h, l).T[0:64]
    term = mm(lanes(up, up), rows(ph, ph, pl_, pl_))
    pay_ref[...] = jnp.where(first, term, e_ref[0])


def climb(basis, transfers):
    return pl.pallas_call(
        climb_kernel,
        out_shape=(
            jax.ShapeDtypeStruct((32, 64, 128), F32),
            jax.ShapeDtypeStruct((64, 128), F32),
            jax.ShapeDtypeStruct((64, 128), F32),
        ),
        in_specs=[pl.BlockSpec(memory_space=pltpu.HBM)] * 2,
        out_specs=(VMEM,) * 3,
        scratch_shapes=[
            pltpu.VMEM((64, 64, 256), BF16),
            pltpu.VMEM((64, 64, 128), F32),
            pltpu.VMEM((8, 128, 128), F32),
            pltpu.VMEM((128, 64, 128), F32),
            pltpu.VMEM((128, 128, 128), BF16),
            pltpu.SemaphoreType.DMA((6,)),
        ],
        compiler_params=params(20),
        cost_estimate=cost(10),
        name="climb",
    )(basis, transfers)


def chol_lanes(a_ref, panels=range(8), count=64, panel=8):
    sub = lax.broadcasted_iota(jnp.int32, (8, 128), 0)
    for p in panels:
        base = p * panel
        if p > 0:
            for it in range(p, count // 8):

                def body(k, accs):
                    lv = a_ref[k, it * 8 : it * 8 + 8, :]
                    return tuple(
                        accs[j] - lv * a_ref[k, pl.ds(base + j, 8, stride=0), :]
                        for j in range(panel)
                    )

                accs = tuple(
                    a_ref[base + j, it * 8 : it * 8 + 8, :] for j in range(panel)
                )
                accs = lax.fori_loop(0, base, body, accs, unroll=8)
                for j in range(panel):
                    a_ref[base + j, it * 8 : it * 8 + 8, :] = accs[j]
        d = [a_ref[base + j, base : base + 8, :] for j in range(8)]
        invs = []
        for j in range(8):
            piv = jnp.broadcast_to(d[j][j : j + 1, :], (8, 128))
            inv = lax.rsqrt(piv)
            invs.append(inv)
            d[j] = jnp.where(sub >= j, d[j] * inv, 0.0)
            for m in range(j + 1, 8):
                d[m] = d[m] - d[j] * jnp.broadcast_to(d[j][m : m + 1, :], (8, 128))
            a_ref[base + j, base : base + 8, :] = d[j]
            if base > 0:
                a_ref[base + j, 0:base, :] = jnp.zeros((base, 128), F32)
        bc = {}
        for j in range(8):
            for m in range(j + 1, 8):
                bc[j, m] = jnp.broadcast_to(d[j][m : m + 1, :], (8, 128))
        for it in range(p + 1, count // 8):
            v = [a_ref[base + j, it * 8 : it * 8 + 8, :] for j in range(8)]
            for j in range(8):
                v[j] = v[j] * invs[j]
                for m in range(j + 1, 8):
                    v[m] = v[m] - v[j] * bc[j, m]
                a_ref[base + j, it * 8 : it * 8 + 8, :] = v[j]


EARLY = 3


def chol_head_kernel(g_ref, a_ref, u_ref):
    def load(s, _):
        at = pl.ds(pl.multiple_of(s * 8, 8), 8)
        for g in range(4):
            u_ref[:, 8 * g : 8 * g + 8, :] = jnp.swapaxes(g_ref[8 * g : 8 * g + 8, at, :], 0, 1)
        for r in range(8):
            x = u_ref[r, 0:32, :]
            y = pltpu.roll(x, 64, 1)
            a_ref[s * 8 + r] = rows(x, y, x, y).T[0:64]
        return 0

    lax.fori_loop(0, 8, load, 0)
    chol_lanes(a_ref, range(EARLY))


def chol_head(gram):
    return pl.pallas_call(
        chol_head_kernel,
        out_shape=jax.ShapeDtypeStruct((64, 64, 128), F32),
        in_specs=[VMEM],
        out_specs=VMEM,
        scratch_shapes=[pltpu.VMEM((8, 64, 128), F32)],
        compiler_params=params(8),
        cost_estimate=cost(4),
        name="chol_head",
    )(gram)


def chol_tail_kernel(i_ref, low_ref, a_ref, u_ref):
    a_ref[...] = i_ref[...]
    chol_lanes(a_ref, range(EARLY, 8))

    def store(s, _):
        at = pl.ds(pl.multiple_of(s * 8, 8), 8)
        for g in range(8):
            u_ref[:, 8 * g : 8 * g + 8, :] = jnp.swapaxes(a_ref[8 * g : 8 * g + 8, at, :], 0, 1)
        for r in range(8):
            x = u_ref[r]
            u_ref[r, 0:32, :] = rows(x, pltpu.roll(x, 96, 1)).T[0:32]
        for g in range(4):
            low_ref[8 * g : 8 * g + 8, at, :] = jnp.swapaxes(u_ref[:, 8 * g : 8 * g + 8, :], 0, 1)
        return 0

    lax.fori_loop(0, 8, store, 0)


def chol_tail(part):
    return pl.pallas_call(
        chol_tail_kernel,
        out_shape=jax.ShapeDtypeStruct((32, 64, 128), F32),
        in_specs=[VMEM],
        out_specs=VMEM,
        scratch_shapes=[pltpu.VMEM((64, 64, 128), F32), pltpu.VMEM((8, 64, 128), F32)],
        compiler_params=params(8),
        cost_estimate=cost(4),
        name="chol_tail",
    )(part)


def half_kernel(c0_ref, c1_ref, low_ref, y_ref, s_ref, u_ref, part):
    step = pl.program_id(0)

    def turn(s, _):
        for r in range(8):
            u_ref[r] = rows(c0_ref[s * 8 + r], c1_ref[s * 8 + r]).T
        at = pl.ds(pl.multiple_of(step * 16 + s * 8, 8), 8)
        for g in range(16):
            s_ref[8 * g : 8 * g + 8, at, :] = jnp.swapaxes(u_ref[:, 8 * g : 8 * g + 8, :], 0, 1)
        return 0

    lax.fori_loop(0, 2, turn, 0)

    @pl.when(step == 3)
    def _():
        first = first_half((64, 256))

        def leaf(s, _):
            ts = [s * HALF + j for j in range(HALF)]
            lefts = []
            for t in ts:
                lh, ll = split(low_ref[16 * part + t])
                lefts.append(rows(lh, ll, lh).T)
            at = [(j, n) for j in range(HALF) for n in range(0, 8, 2)]
            zs = []
            for j, n in at:
                wh, wl = split(lanes(s_ref[ts[j] * 8 + n], s_ref[ts[j] * 8 + n + 1]))
                zs.append(mm(lefts[j], rows(wh, wh, wl)))
            for (j, n), z in zip(at, zs):
                yh, yl = split(jnp.where(first, z[0:64], z[64:128]))
                for m in range(2):
                    b = ts[j] * 8 + n + m
                    y_ref[b, :, 0:128] = yh[:, m * 128 : m * 128 + 128]
                    y_ref[b, :, 128:256] = yl[:, m * 128 : m * 128 + 128]
            return 0

        lax.fori_loop(0, 16 // HALF, leaf, 0)


def half_leaf(coupling, low, part):
    return pl.pallas_call(
        functools.partial(half_kernel, part=part),
        out_shape=jax.ShapeDtypeStruct((128, 64, 256), BF16),
        grid=(4,),
        in_specs=[
            pl.BlockSpec((16, 64, 128), lambda s: (s, 0, part)),
            pl.BlockSpec((16, 64, 128), lambda s: (s, 0, part + 2)),
            pl.BlockSpec((32, 64, 128), lambda s: (0, 0, 0)),
        ],
        out_specs=pl.BlockSpec((128, 64, 256), lambda s: (0, 0, 0)),
        scratch_shapes=[pltpu.VMEM((128, 64, 128), F32), pltpu.VMEM((8, 128, 128), F32)],
        compiler_params=params(22),
        cost_estimate=cost(6),
    )(coupling, coupling, low)


def prep_kernel(odd_ref, near_ref, own_ref, far_ref, d_ref):
    first = first_half()
    odd = odd_ref[0]
    for base, ref in ((64, own_ref), (128 - 128 * odd, near_ref), (128 * odd, far_ref)):

        def pair(q, _, ref=ref, base=base):
            x = ref[q]
            y = pltpu.roll(x, 64, 1)
            d_ref[base + q] = right_of(jnp.where(first, x, y))
            d_ref[base + 32 + q] = right_of(jnp.where(first, y, x))
            return 0

        lax.fori_loop(0, 32, pair, 0, unroll=8)


def prep(odd, near, own, far):
    return pl.pallas_call(
        prep_kernel,
        out_shape=jax.ShapeDtypeStruct((192, 64, 256), BF16),
        in_specs=[SMEM] + [VMEM] * 3,
        out_specs=VMEM,
        compiler_params=params(16),
        cost_estimate=cost(3),
        name="prep",
    )(odd, near, own, far)


def full_kernel(cols_ref, y_ref, d_ref, *refs, part):
    out_ref, s_ref, u_ref, o_ref, sem = refs[-5:]
    lane = lax.broadcasted_iota(jnp.int32, (64, 256), 1)
    keep = ((lane % 128) < 64).astype(BF16)
    drop = ((lane % 128) >= 64).astype(BF16)

    def pair(s, _):
        ps = [s * PAIRS + j for j in range(PAIRS)]
        zs = []
        for p in ps:
            sa = cols_ref[part * 128 + p]
            sb = cols_ref[part * 128 + 256 + p]
            r = rows(d_ref[sa] * keep, d_ref[sb] * drop)
            y = y_ref[p]
            zs.append(mm(rows(y[:, 0:128], y[:, 128:256]), r))
        for p, z in zip(ps, zs):
            s_ref[p] = z[0:64, 0:128] + z[0:64, 128:256] + z[64:128, 0:128]
        return 0

    lax.fori_loop(0, 128 // PAIRS, pair, 0)

    def send(n):
        return [
            pltpu.make_async_copy(
                o_ref.at[c, pl.ds(16 * n, 16)],
                out_ref.at[pl.ds(16 * n, 16), :, pl.ds((part + 2 * c) * 128, 128)],
                sem.at[n, c],
            )
            for c in range(2)
        ]

    def turn(s, _):
        at = pl.ds(pl.multiple_of(s * 8, 8), 8)
        for g in range(16):
            u_ref[:, 8 * g : 8 * g + 8, :] = jnp.swapaxes(s_ref[8 * g : 8 * g + 8, at, :], 0, 1)
        for r in range(8):
            x = u_ref[r].T
            o_ref[0, s * 8 + r] = x[0:64]
            o_ref[1, s * 8 + r] = x[64:128]
        return 0

    for n in range(4):
        lax.fori_loop(2 * n, 2 * n + 2, turn, 0)
        for copy in send(n):
            copy.start()
    for n in range(4):
        for copy in send(n):
            copy.wait()


def full_leaf(cols, y, d, part, into=None):
    extra = [] if into is None else [into]
    return pl.pallas_call(
        functools.partial(full_kernel, part=part),
        out_shape=jax.ShapeDtypeStruct((64, 64, 512), F32),
        in_specs=[SMEM, VMEM, VMEM] + [pl.BlockSpec(memory_space=pltpu.HBM)] * len(extra),
        out_specs=pl.BlockSpec(memory_space=pltpu.HBM),
        scratch_shapes=[
            pltpu.VMEM((128, 64, 128), F32),
            pltpu.VMEM((8, 128, 128), F32),
            pltpu.VMEM((2, 64, 64, 128), F32),
            pltpu.SemaphoreType.DMA((4, 2)),
        ],
        input_output_aliases={} if into is None else {3: 0},
        compiler_params=params(22),
        cost_estimate=cost(8),
    )(cols, y, d, *extra)


def branch_kernel(at_ref, p0, p1, p2, p3, p4, p5, top_ref, gf_ref, low_ref, t_ref, e_ref, n_ref, a_ref):
    at = at_ref[0]
    pick = at_ref[1]
    first = first_half()

    def place(n, x):
        y = pltpu.roll(x, 64, 1)
        t_ref[n] = jnp.where(first, x, y)
        e_ref[n] = jnp.where(first, y, x)

    place(at, p0[...])
    place(at ^ 1, p1[...])
    for i in range(2):
        place(at ^ (2 + i), p2[i])
    for s, ref in enumerate((p3, p4, p5)):
        for i in range(4):
            place((at ^ i) - 4 * (s + 1) & 15, ref[i])
    n_ref[0] = top_ref[...]
    for m in range(8):
        n_ref[8 + m] = t_ref[2 * m] + t_ref[2 * m + 1]
    ups = {}
    for p in range(2, 16):
        h, l = split(e_ref[p])
        ups[p] = rows(h, l).T[0:64]
    for level in (2, 1, 0):
        parents = range(2**level, 2 ** (level + 1))
        children = [c for p in parents for c in (2 * p, 2 * p + 1)]
        prods = []
        for c in children:
            h, l = split(e_ref[c])
            prods.append(mm(left_of(n_ref[c]), rows(h, h, l, l)))
        terms = []
        for c, prod in zip(children, prods):
            h, l = split(prod)
            terms.append(mm(lanes(ups[c], ups[c]), rows(h, h, l, l)))
        for n, p in enumerate(parents):
            n_ref[p] = terms[2 * n] + terms[2 * n + 1]

    both = jnp.where(first, n_ref[pick], n_ref[1])
    lane = lax.broadcasted_iota(jnp.int32, (64, 128), 1)

    def load(k, _):
        a_ref[k] = jnp.take_along_axis(both, (lane & 64) + k, axis=1)
        return 0

    lax.fori_loop(0, 64, load, 0, unroll=8)
    chol_lanes(a_ref)

    def store(k, out):
        return jnp.where((lane & 63) == k, a_ref[k], out)

    out = lax.fori_loop(0, 64, store, jnp.zeros((64, 128), F32), unroll=8)
    gf_ref[0] = out.T[0:64]
    low_ref[...] = jnp.where(first, pltpu.roll(out, 64, 1), out)


def branch(at, parts, top):
    return pl.pallas_call(
        branch_kernel,
        out_shape=(
            jax.ShapeDtypeStruct((1, 64, 64), F32),
            jax.ShapeDtypeStruct((64, 128), F32),
        ),
        in_specs=[SMEM] + [VMEM] * 7,
        out_specs=(VMEM, VMEM),
        scratch_shapes=[
            pltpu.VMEM((16, 64, 128), F32),
            pltpu.VMEM((16, 64, 128), F32),
            pltpu.VMEM((16, 64, 128), F32),
            pltpu.VMEM((64, 64, 128), F32),
        ],
        compiler_params=params(8),
        cost_estimate=cost(5),
        name="branch",
    )(at, *parts, top)


def far_kernel(cols_ref, f_ref, l0, l1, l2, l3, o_ref, l_ref, c_ref):
    for s, part in enumerate((l0[...], l1[...], l2[0], l2[1], l3[0], l3[1], l3[2], l3[3])):
        h, l = split(part[:, 0:64])
        l_ref[s] = rows(h, h, l)
    lh, ll = split(l0[...].T[0:64])
    left = lanes(lh, ll, lh)
    halves = []
    for g in range(2):
        for s in range(8):
            x = f_ref[8 * s : 8 * s + 8, 8 * g : 8 * g + 8, :]
            c_ref[8 * g : 8 * g + 8, 8 * s : 8 * s + 8, :] = jnp.swapaxes(x, 0, 1)
        for f in range(8 * g, 8 * g + 8):
            ch, cl = split(c_ref[f])
            halves.append(mm(left, rows(ch, ch, cl)))
    outs = []
    for f in range(16):
        hh, hl = split(halves[f])
        outs.append(mm(lanes(hh, hl, hh), l_ref[cols_ref[f]]))
    for f in range(16):
        c_ref[f] = outs[f]
    for g in range(2):
        for s in range(8):
            x = c_ref[8 * g : 8 * g + 8, 8 * s : 8 * s + 8, :]
            o_ref[8 * s : 8 * s + 8, 8 * g : 8 * g + 8, :] = jnp.swapaxes(x, 0, 1)


def far(cols, coupling, lowers):
    return pl.pallas_call(
        far_kernel,
        out_shape=jax.ShapeDtypeStruct(coupling.shape, F32),
        in_specs=[SMEM] + [VMEM] * 5,
        out_specs=VMEM,
        scratch_shapes=[pltpu.VMEM((8, 192, 64), BF16), pltpu.VMEM((16, 64, 64), F32)],
        compiler_params=params(6),
        cost_estimate=cost(3),
        name="far",
    )(cols, coupling, *lowers)


def shifted(value, axis, to):
    return lax.ppermute(value, axis, [(i, to(i)) for i in range(lax.axis_size(axis))])


def steps(
    basis_t, nested_transfer_matrices, leaf_coupling, leaf_columns, far_coupling, far_columns
):
    basis_t, nested_transfer_matrices, leaf_coupling = (
        pltpu.with_memory_space_constraint(x, pltpu.HBM)
        for x in (basis_t, nested_transfer_matrices, leaf_coupling)
    )
    both = ("wide", "narrow")
    wide_at = lax.axis_index("wide")
    at = lax.axis_index("narrow")
    gram, top, pay = climb(basis_t, nested_transfer_matrices)
    pay_a = shifted(pay, "narrow", lambda i: i ^ 1)
    head = chol_head(gram)
    pair = jnp.stack([pay, pay_a])
    pay_b = shifted(pair, "narrow", lambda i: i ^ 2)
    low = chol_tail(head)
    quad = jnp.concatenate([pair, pay_b])
    pay_c = [shifted(quad, "narrow", lambda i, s=s: (i + 4 * s) % 16) for s in (1, 2, 3)]
    count = lax.axis_size(both)
    low_near = lax.ppermute(low, both, [(i, i ^ 1) for i in range(count)])
    later = [(i, i + 1) for i in range(1, count - 1, 2)]
    low_far = lax.ppermute(low, both, later + [(j, i) for i, j in later])
    half_a = half_leaf(leaf_coupling, low, 0)
    half_b = half_leaf(leaf_coupling, low, 1)
    ones = 1 + sum((at % 2**k == 2**k - 1).astype(jnp.int32) for k in range(1, 5))
    pick = jnp.where(ones <= 4, (16 + at) >> ones, 0)
    place = jnp.stack([at, pick]).astype(jnp.int32)
    group_factors, own = branch(place, [pay, pay_a, pay_b, *pay_c], top)
    own_a = shifted(own, "wide", lambda i: i ^ 1)
    factors = prep(at.reshape(1) % 2, low_near, low, low_far)
    two = jnp.stack([own, own_a])
    own_b = shifted(two, "wide", lambda i: i ^ 2)
    cols = leaf_columns - (lax.axis_index(both) * 64 - 64)
    out = full_leaf(cols, half_a, factors, 0)
    four = jnp.concatenate([two, own_b])
    own_c = shifted(four, "wide", lambda i: i ^ 4)
    leaf_coupled = full_leaf(cols, half_b, factors, 1, out)
    far_out = far(
        wide_at ^ far_columns,
        jnp.transpose(far_coupling, (0, 2, 1)),
        [own, own_a, own_b, own_c],
    )
    return leaf_coupled, jnp.transpose(far_out, (0, 2, 1)), group_factors


def solution(mesh):
    spread = P(None, None, ("wide", "narrow"))
    split_first = P(("wide", "narrow"), None, None)
    ids = P(("wide", "narrow"))
    return jax.shard_map(
        steps,
        mesh=mesh,
        in_specs=(split_first, spread, spread, ids, spread, ids),
        out_specs=(spread, spread, split_first),
        check_vma=False,
    )
```

```python
import functools

import jax
import jax.numpy as jnp
from jax import lax
from jax.experimental import pallas as pl
from jax.experimental.pallas import tpu as pltpu
from jax.sharding import PartitionSpec as P

F32 = jnp.float32
BF16 = jnp.bfloat16
ANY = pl.BlockSpec(memory_space=pl.ANY)
VMEM = pl.BlockSpec(memory_space=pltpu.VMEM)
SMEM = pl.BlockSpec(memory_space=pltpu.SMEM)


def params(mib):
    return pltpu.CompilerParams(vmem_limit_bytes=mib * 2**20)


def cost(us):
    return pl.CostEstimate(flops=int(us * 1.15e9), bytes_accessed=4096, transcendentals=0)


def split(x):
    hi = x.astype(BF16)
    lo = (x - hi.astype(F32)).astype(BF16)
    return hi, lo


def mm(a, b):
    return lax.dot_general(a, b, (((1,), (0,)), ((), ())), preferred_element_type=F32)


def mm_nt(a, b):
    return lax.dot_general(a, b, (((1,), (1,)), ((), ())), preferred_element_type=F32)


def mm_tn(a, b):
    return lax.dot_general(a, b, (((0,), (0,)), ((), ())), preferred_element_type=F32)


def lanes(*parts):
    return jnp.concatenate(parts, axis=1)


def rows(*parts):
    return jnp.concatenate(parts, axis=0)


def first_half(shape=(64, 128)):
    return lax.broadcasted_iota(jnp.int32, shape, 1) % 128 < 64


def mixed(m):
    h = m.astype(BF16).astype(F32)
    return jnp.where(first_half(m.shape), h, m - h).astype(BF16)


def left_of(m):
    v = mixed(m)
    return lanes(v, v)


def right_of(m):
    return lanes(*split(m))


def twice(m):
    return rows(m, m)


LEAVES = 16
HALF = 4
PAIRS = 32


def climb_kernel(
    b_hbm, t_hbm, g_ref, top_ref, pay_ref, b_ref, t_ref, u_ref, e_ref, w_ref, sem
):
    t_copies = [
        pltpu.make_async_copy(
            t_hbm.at[pl.ds(16 * n, 16)], t_ref.at[pl.ds(16 * n, 16)], sem.at[n]
        )
        for n in range(4)
    ]
    b_copies = [
        pltpu.make_async_copy(
            b_hbm.at[pl.ds(32 * n, 32)], b_ref.at[pl.ds(32 * n, 32)], sem.at[4 + n]
        )
        for n in range(2)
    ]
    for copy in t_copies + b_copies:
        copy.start()
    first = first_half()

    def turn(s, _):
        for r in range(8):
            x = t_ref[s * 8 + r]
            u_ref[r] = rows(x, x).T
        for g in range(16):
            x = u_ref[:, 8 * g : 8 * g + 8, :]
            e_ref[8 * g : 8 * g + 8, pl.ds(pl.multiple_of(s * 8, 8), 8), :] = jnp.swapaxes(x, 0, 1)
        return 0

    for n in range(4):
        t_copies[n].wait()
        lax.fori_loop(2 * n, 2 * n + 2, turn, 0)

    row = lax.broadcasted_iota(jnp.int32, (64, 128), 0)
    col = lax.broadcasted_iota(jnp.int32, (64, 128), 1)
    w_ref[1, 0:64] = (row == col % 64).astype(BF16)
    w_ref[1, 64:128] = jnp.zeros((64, 128), BF16)

    def right_rows(h):
        w = w_ref[h]
        return rows(w[0:64], w[0:64], w[64:128], w[64:128])

    def down(clusters):
        zs = [
            mm(rows(left_of(e_ref[2 * p]), left_of(e_ref[2 * p + 1])), right_rows(p))
            for p in clusters
        ]
        for p, z in zip(clusters, zs):
            for c in range(2):
                w_ref[2 * p + c] = rows(*split(z[64 * c : 64 * c + 64]))

    def downs(s, _):
        down([s * 8 + j for j in range(8)])
        return 0

    for level in range(3):
        down(range(2**level, 2 ** (level + 1)))
    for level in range(3, 6):
        n = 2**level
        lax.fori_loop(n // 8, n // 4, downs, 0)
    for copy in b_copies:
        copy.wait()

    def leaves(s, acc):
        count = LEAVES // 2
        qs = [s * count + j for j in range(count)]
        ts = qs + [q + 32 for q in qs]
        bs = [b_ref[t] for t in ts]
        grams = [mm_nt(b, twice(b)) for b in bs]
        for j, q in enumerate(qs):
            g_ref[q] = jnp.where(first, grams[j], grams[count + j])
        prods = [mm(left_of(g), right_rows(64 + t)) for g, t in zip(grams, ts)]
        for p, t in zip(prods, ts):
            ph, pl_ = split(p)
            w = w_ref[64 + t][:, 0:64]
            acc = acc + mm_tn(rows(w, w), rows(ph, ph, pl_, pl_))
        return acc

    top = lax.fori_loop(0, 64 // LEAVES, leaves, jnp.zeros((64, 128), F32))
    top_ref[...] = top
    h, l = split(e_ref[1])
    prod = mm(left_of(top), rows(h, h, l, l))
    ph, pl_ = split(prod)
    up = rows(h, l).T[0:64]
    term = mm(lanes(up, up), rows(ph, ph, pl_, pl_))
    pay_ref[...] = jnp.where(first, term, e_ref[0])


def climb(basis, transfers):
    return pl.pallas_call(
        climb_kernel,
        out_shape=(
            jax.ShapeDtypeStruct((32, 64, 128), F32),
            jax.ShapeDtypeStruct((64, 128), F32),
            jax.ShapeDtypeStruct((64, 128), F32),
        ),
        in_specs=[pl.BlockSpec(memory_space=pltpu.HBM)] * 2,
        out_specs=(VMEM,) * 3,
        scratch_shapes=[
            pltpu.VMEM((64, 64, 256), BF16),
            pltpu.VMEM((64, 64, 128), F32),
            pltpu.VMEM((8, 128, 128), F32),
            pltpu.VMEM((128, 64, 128), F32),
            pltpu.VMEM((128, 128, 128), BF16),
            pltpu.SemaphoreType.DMA((6,)),
        ],
        compiler_params=params(20),
        cost_estimate=cost(10),
        name="climb",
    )(basis, transfers)


def chol_lanes(a_ref, panels=range(8), count=64, panel=8):
    sub = lax.broadcasted_iota(jnp.int32, (8, 128), 0)
    for p in panels:
        base = p * panel
        if p > 0:
            for it in range(p, count // 8):

                def body(k, accs):
                    lv = a_ref[k, it * 8 : it * 8 + 8, :]
                    return tuple(
                        accs[j] - lv * a_ref[k, pl.ds(base + j, 8, stride=0), :]
                        for j in range(panel)
                    )

                accs = tuple(
                    a_ref[base + j, it * 8 : it * 8 + 8, :] for j in range(panel)
                )
                accs = lax.fori_loop(0, base, body, accs, unroll=8)
                for j in range(panel):
                    a_ref[base + j, it * 8 : it * 8 + 8, :] = accs[j]
        d = [a_ref[base + j, base : base + 8, :] for j in range(8)]
        invs = []
        for j in range(8):
            piv = jnp.broadcast_to(d[j][j : j + 1, :], (8, 128))
            inv = lax.rsqrt(piv)
            invs.append(inv)
            d[j] = jnp.where(sub >= j, d[j] * inv, 0.0)
            for m in range(j + 1, 8):
                d[m] = d[m] - d[j] * jnp.broadcast_to(d[j][m : m + 1, :], (8, 128))
            a_ref[base + j, base : base + 8, :] = d[j]
            if base > 0:
                a_ref[base + j, 0:base, :] = jnp.zeros((base, 128), F32)
        bc = {}
        for j in range(8):
            for m in range(j + 1, 8):
                bc[j, m] = jnp.broadcast_to(d[j][m : m + 1, :], (8, 128))
        for it in range(p + 1, count // 8):
            v = [a_ref[base + j, it * 8 : it * 8 + 8, :] for j in range(8)]
            for j in range(8):
                v[j] = v[j] * invs[j]
                for m in range(j + 1, 8):
                    v[m] = v[m] - v[j] * bc[j, m]
                a_ref[base + j, it * 8 : it * 8 + 8, :] = v[j]


EARLY = 3


def chol_head_kernel(g_ref, a_ref, u_ref):
    def load(s, _):
        at = pl.ds(pl.multiple_of(s * 8, 8), 8)
        for g in range(4):
            u_ref[:, 8 * g : 8 * g + 8, :] = jnp.swapaxes(g_ref[8 * g : 8 * g + 8, at, :], 0, 1)
        for r in range(8):
            x = u_ref[r, 0:32, :]
            y = pltpu.roll(x, 64, 1)
            a_ref[s * 8 + r] = rows(x, y, x, y).T[0:64]
        return 0

    lax.fori_loop(0, 8, load, 0)
    chol_lanes(a_ref, range(EARLY))


def chol_head(gram):
    return pl.pallas_call(
        chol_head_kernel,
        out_shape=jax.ShapeDtypeStruct((64, 64, 128), F32),
        in_specs=[VMEM],
        out_specs=VMEM,
        scratch_shapes=[pltpu.VMEM((8, 64, 128), F32)],
        compiler_params=params(8),
        cost_estimate=cost(4),
        name="chol_head",
    )(gram)


def chol_tail_kernel(i_ref, low_ref, pack_ref, a_ref, u_ref, v_ref):
    a_ref[...] = i_ref[...]
    chol_lanes(a_ref, range(EARLY, 8))
    below = lax.broadcasted_iota(jnp.int32, (32, 128), 0)

    def paired(x):
        return rows(x, pltpu.roll(x, 96, 1)).T[0:32]

    def gather(s):
        at = pl.ds(pl.multiple_of(s * 8, 8), 8)
        for g in range(8):
            u_ref[:, 8 * g : 8 * g + 8, :] = jnp.swapaxes(a_ref[8 * g : 8 * g + 8, at, :], 0, 1)

    def spread(ref, to, s):
        at = pl.ds(pl.multiple_of(s * 8, 8), 8)
        for g in range(4):
            to[8 * g : 8 * g + 8, at, :] = jnp.swapaxes(ref[:, 8 * g : 8 * g + 8, :], 0, 1)

    def upper(s, _):
        gather(s)
        for r in range(8):
            v_ref[r] = paired(u_ref[r])
        spread(v_ref, low_ref, s)
        return 0

    def lower(s, _):
        gather(s + 4)
        for r in range(8):
            v_ref[r] = paired(u_ref[r])
        spread(v_ref, low_ref, s + 4)
        for r in range(8):
            a = s * 8 + r
            free = jnp.where(below <= a, u_ref[r, 32:64, :], a_ref[a, 0:32, :])
            v_ref[r] = paired(rows(u_ref[r, 0:32, :], free))
        spread(v_ref, pack_ref, s)
        return 0

    lax.fori_loop(0, 4, upper, 0)
    lax.fori_loop(0, 4, lower, 0)
    diagonal = rows(*[a_ref[b, b : b + 1, :] for b in range(32)])
    pack_ref[32] = paired(rows(jnp.zeros((32, 128), F32), diagonal))


def chol_tail(part):
    return pl.pallas_call(
        chol_tail_kernel,
        out_shape=(
            jax.ShapeDtypeStruct((32, 64, 128), F32),
            jax.ShapeDtypeStruct((33, 32, 128), F32),
        ),
        in_specs=[VMEM],
        out_specs=(VMEM, VMEM),
        scratch_shapes=[
            pltpu.VMEM((64, 64, 128), F32),
            pltpu.VMEM((8, 64, 128), F32),
            pltpu.VMEM((8, 32, 128), F32),
        ],
        compiler_params=params(10),
        cost_estimate=cost(5),
        name="chol_tail",
    )(part)


def half_kernel(c0_ref, c1_ref, low_ref, y_ref, s_ref, u_ref, part):
    step = pl.program_id(0)

    def turn(s, _):
        for r in range(8):
            u_ref[r] = rows(c0_ref[s * 8 + r], c1_ref[s * 8 + r]).T
        at = pl.ds(pl.multiple_of(step * 16 + s * 8, 8), 8)
        for g in range(16):
            s_ref[8 * g : 8 * g + 8, at, :] = jnp.swapaxes(u_ref[:, 8 * g : 8 * g + 8, :], 0, 1)
        return 0

    lax.fori_loop(0, 2, turn, 0)

    @pl.when(step == 3)
    def _():
        first = first_half((64, 256))

        def leaf(s, _):
            ts = [s * HALF + j for j in range(HALF)]
            lefts = []
            for t in ts:
                lh, ll = split(low_ref[16 * part + t])
                lefts.append(rows(lh, ll, lh).T)
            at = [(j, n) for j in range(HALF) for n in range(0, 8, 2)]
            zs = []
            for j, n in at:
                wh, wl = split(lanes(s_ref[ts[j] * 8 + n], s_ref[ts[j] * 8 + n + 1]))
                zs.append(mm(lefts[j], rows(wh, wh, wl)))
            for (j, n), z in zip(at, zs):
                yh, yl = split(jnp.where(first, z[0:64], z[64:128]))
                for m in range(2):
                    b = ts[j] * 8 + n + m
                    y_ref[b, :, 0:128] = yh[:, m * 128 : m * 128 + 128]
                    y_ref[b, :, 128:256] = yl[:, m * 128 : m * 128 + 128]
            return 0

        lax.fori_loop(0, 16 // HALF, leaf, 0)


def half_leaf(coupling, low, part):
    return pl.pallas_call(
        functools.partial(half_kernel, part=part),
        out_shape=jax.ShapeDtypeStruct((128, 64, 256), BF16),
        grid=(4,),
        in_specs=[
            pl.BlockSpec((16, 64, 128), lambda s: (s, 0, part)),
            pl.BlockSpec((16, 64, 128), lambda s: (s, 0, part + 2)),
            pl.BlockSpec((32, 64, 128), lambda s: (0, 0, 0)),
        ],
        out_specs=pl.BlockSpec((128, 64, 256), lambda s: (0, 0, 0)),
        scratch_shapes=[pltpu.VMEM((128, 64, 128), F32), pltpu.VMEM((8, 128, 128), F32)],
        compiler_params=params(22),
        cost_estimate=cost(6),
    )(coupling, coupling, low)


def prep_kernel(odd_ref, near_ref, own_ref, far_ref, d_ref):
    first = first_half()
    odd = odd_ref[0]

    def plain(q, _):
        x = own_ref[q]
        y = pltpu.roll(x, 64, 1)
        d_ref[64 + q] = right_of(jnp.where(first, x, y))
        d_ref[96 + q] = right_of(jnp.where(first, y, x))
        return 0

    lax.fori_loop(0, 32, plain, 0, unroll=8)
    half = first[0:32]
    row = lax.broadcasted_iota(jnp.int32, (32, 128), 0)
    col = lax.broadcasted_iota(jnp.int32, (32, 128), 1) % 64 - 32
    for base, ref in ((128 - 128 * odd, near_ref), (128 * odd, far_ref)):

        def packed(s, _, ref=ref, base=base):
            qs = [s * 4 + j for j in range(4)]
            ups = []
            for q in qs:
                diagonal = ref[32, pl.ds(q, 32, stride=0), :]
                rest = jnp.where(col == row, diagonal, 0.0)
                ups.append(jnp.where(col > row, ref[q], rest))
            turned = rows(*ups).T
            shifts = [
                [turned[64 * c + 32 : 64 * c + 64]]
                + [
                    pltpu.roll(turned[64 * c + 32 : 64 * c + 64], 32 * n, 1)
                    for n in range(1, 4)
                ]
                for c in range(2)
            ]
            for j, q in enumerate(qs):
                x = jnp.where(col <= row, ref[q], 0.0)
                y = pltpu.roll(x, 64, 1)
                for c in range(2):
                    at = shifts[c]
                    top = jnp.where(half, at[(4 - j) % 4], at[(6 - j) % 4])
                    top = jnp.where(col < 0, top, 0.0)
                    low = jnp.where(half, x, y) if c == 0 else jnp.where(half, y, x)
                    d_ref[base + 32 * c + q] = right_of(rows(top, low))
            return 0

        lax.fori_loop(0, 8, packed, 0, unroll=2)


def prep(odd, near, own, far):
    return pl.pallas_call(
        prep_kernel,
        out_shape=jax.ShapeDtypeStruct((192, 64, 256), BF16),
        in_specs=[SMEM] + [VMEM] * 3,
        out_specs=VMEM,
        compiler_params=params(16),
        cost_estimate=cost(3),
        name="prep",
    )(odd, near, own, far)


def full_kernel(cols_ref, y_ref, d_ref, *refs, part):
    out_ref, s_ref, u_ref, o_ref, sem = refs[-5:]
    lane = lax.broadcasted_iota(jnp.int32, (64, 256), 1)
    keep = ((lane % 128) < 64).astype(BF16)
    drop = ((lane % 128) >= 64).astype(BF16)

    def pair(s, _):
        ps = [s * PAIRS + j for j in range(PAIRS)]
        zs = []
        for p in ps:
            sa = cols_ref[part * 128 + p]
            sb = cols_ref[part * 128 + 256 + p]
            r = rows(d_ref[sa] * keep, d_ref[sb] * drop)
            y = y_ref[p]
            zs.append(mm(rows(y[:, 0:128], y[:, 128:256]), r))
        for p, z in zip(ps, zs):
            s_ref[p] = z[0:64, 0:128] + z[0:64, 128:256] + z[64:128, 0:128]
        return 0

    lax.fori_loop(0, 128 // PAIRS, pair, 0)

    def send(n):
        return [
            pltpu.make_async_copy(
                o_ref.at[c, pl.ds(16 * n, 16)],
                out_ref.at[pl.ds(16 * n, 16), :, pl.ds((part + 2 * c) * 128, 128)],
                sem.at[n, c],
            )
            for c in range(2)
        ]

    def turn(s, _):
        at = pl.ds(pl.multiple_of(s * 8, 8), 8)
        for g in range(16):
            u_ref[:, 8 * g : 8 * g + 8, :] = jnp.swapaxes(s_ref[8 * g : 8 * g + 8, at, :], 0, 1)
        for r in range(8):
            x = u_ref[r].T
            o_ref[0, s * 8 + r] = x[0:64]
            o_ref[1, s * 8 + r] = x[64:128]
        return 0

    for n in range(4):
        lax.fori_loop(2 * n, 2 * n + 2, turn, 0)
        for copy in send(n):
            copy.start()
    for n in range(4):
        for copy in send(n):
            copy.wait()


def full_leaf(cols, y, d, part, into=None):
    extra = [] if into is None else [into]
    return pl.pallas_call(
        functools.partial(full_kernel, part=part),
        out_shape=jax.ShapeDtypeStruct((64, 64, 512), F32),
        in_specs=[SMEM, VMEM, VMEM] + [pl.BlockSpec(memory_space=pltpu.HBM)] * len(extra),
        out_specs=pl.BlockSpec(memory_space=pltpu.HBM),
        scratch_shapes=[
            pltpu.VMEM((128, 64, 128), F32),
            pltpu.VMEM((8, 128, 128), F32),
            pltpu.VMEM((2, 64, 64, 128), F32),
            pltpu.SemaphoreType.DMA((4, 2)),
        ],
        input_output_aliases={} if into is None else {3: 0},
        compiler_params=params(22),
        cost_estimate=cost(8),
    )(cols, y, d, *extra)


def branch_kernel(at_ref, p0, p1, p2, p3, p4, p5, top_ref, gf_ref, low_ref, t_ref, e_ref, n_ref, a_ref):
    at = at_ref[0]
    pick = at_ref[1]
    first = first_half()

    def place(n, x):
        y = pltpu.roll(x, 64, 1)
        t_ref[n] = jnp.where(first, x, y)
        e_ref[n] = jnp.where(first, y, x)

    place(at, p0[...])
    place(at ^ 1, p1[...])
    for i in range(2):
        place(at ^ (2 + i), p2[i])
    for s, ref in enumerate((p3, p4, p5)):
        for i in range(4):
            place((at ^ i) - 4 * (s + 1) & 15, ref[i])
    n_ref[0] = top_ref[...]
    for m in range(8):
        n_ref[8 + m] = t_ref[2 * m] + t_ref[2 * m + 1]
    ups = {}
    for p in range(2, 16):
        h, l = split(e_ref[p])
        ups[p] = rows(h, l).T[0:64]
    for level in (2, 1, 0):
        parents = range(2**level, 2 ** (level + 1))
        children = [c for p in parents for c in (2 * p, 2 * p + 1)]
        prods = []
        for c in children:
            h, l = split(e_ref[c])
            prods.append(mm(left_of(n_ref[c]), rows(h, h, l, l)))
        terms = []
        for c, prod in zip(children, prods):
            h, l = split(prod)
            terms.append(mm(lanes(ups[c], ups[c]), rows(h, h, l, l)))
        for n, p in enumerate(parents):
            n_ref[p] = terms[2 * n] + terms[2 * n + 1]

    both = jnp.where(first, n_ref[pick], n_ref[1])
    lane = lax.broadcasted_iota(jnp.int32, (64, 128), 1)

    def load(k, _):
        a_ref[k] = jnp.take_along_axis(both, (lane & 64) + k, axis=1)
        return 0

    lax.fori_loop(0, 64, load, 0, unroll=8)
    chol_lanes(a_ref)

    def store(k, out):
        return jnp.where((lane & 63) == k, a_ref[k], out)

    out = lax.fori_loop(0, 64, store, jnp.zeros((64, 128), F32), unroll=8)
    gf_ref[0] = out.T[0:64]
    low_ref[...] = jnp.where(first, pltpu.roll(out, 64, 1), out)


def branch(at, parts, top):
    return pl.pallas_call(
        branch_kernel,
        out_shape=(
            jax.ShapeDtypeStruct((1, 64, 64), F32),
            jax.ShapeDtypeStruct((64, 128), F32),
        ),
        in_specs=[SMEM] + [VMEM] * 7,
        out_specs=(VMEM, VMEM),
        scratch_shapes=[
            pltpu.VMEM((16, 64, 128), F32),
            pltpu.VMEM((16, 64, 128), F32),
            pltpu.VMEM((16, 64, 128), F32),
            pltpu.VMEM((64, 64, 128), F32),
        ],
        compiler_params=params(8),
        cost_estimate=cost(5),
        name="branch",
    )(at, *parts, top)


def far_kernel(cols_ref, f_ref, l0, l1, l2, l3, o_ref, l_ref, c_ref):
    for s, part in enumerate((l0[...], l1[...], l2[0], l2[1], l3[0], l3[1], l3[2], l3[3])):
        h, l = split(part[:, 0:64])
        l_ref[s] = rows(h, h, l)
    lh, ll = split(l0[...].T[0:64])
    left = lanes(lh, ll, lh)
    halves = []
    for g in range(2):
        for s in range(8):
            x = f_ref[8 * s : 8 * s + 8, 8 * g : 8 * g + 8, :]
            c_ref[8 * g : 8 * g + 8, 8 * s : 8 * s + 8, :] = jnp.swapaxes(x, 0, 1)
        for f in range(8 * g, 8 * g + 8):
            ch, cl = split(c_ref[f])
            halves.append(mm(left, rows(ch, ch, cl)))
    outs = []
    for f in range(16):
        hh, hl = split(halves[f])
        outs.append(mm(lanes(hh, hl, hh), l_ref[cols_ref[f]]))
    for f in range(16):
        c_ref[f] = outs[f]
    for g in range(2):
        for s in range(8):
            x = c_ref[8 * g : 8 * g + 8, 8 * s : 8 * s + 8, :]
            o_ref[8 * s : 8 * s + 8, 8 * g : 8 * g + 8, :] = jnp.swapaxes(x, 0, 1)


def far(cols, coupling, lowers):
    return pl.pallas_call(
        far_kernel,
        out_shape=jax.ShapeDtypeStruct(coupling.shape, F32),
        in_specs=[SMEM] + [VMEM] * 5,
        out_specs=VMEM,
        scratch_shapes=[pltpu.VMEM((8, 192, 64), BF16), pltpu.VMEM((16, 64, 64), F32)],
        compiler_params=params(6),
        cost_estimate=cost(3),
        name="far",
    )(cols, coupling, *lowers)


def shifted(value, axis, to):
    return lax.ppermute(value, axis, [(i, to(i)) for i in range(lax.axis_size(axis))])


def steps(
    basis_t, nested_transfer_matrices, leaf_coupling, leaf_columns, far_coupling, far_columns
):
    basis_t, nested_transfer_matrices, leaf_coupling = (
        pltpu.with_memory_space_constraint(x, pltpu.HBM)
        for x in (basis_t, nested_transfer_matrices, leaf_coupling)
    )
    both = ("wide", "narrow")
    wide_at = lax.axis_index("wide")
    at = lax.axis_index("narrow")
    gram, top, pay = climb(basis_t, nested_transfer_matrices)
    pay_a = shifted(pay, "narrow", lambda i: i ^ 1)
    head = chol_head(gram)
    pair = jnp.stack([pay, pay_a])
    pay_b = shifted(pair, "narrow", lambda i: i ^ 2)
    low, pack = chol_tail(head)
    quad = jnp.concatenate([pair, pay_b])
    pay_c = [shifted(quad, "narrow", lambda i, s=s: (i + 4 * s) % 16) for s in (1, 2, 3)]
    count = lax.axis_size(both)
    low_near = lax.ppermute(pack, both, [(i, i ^ 1) for i in range(count)])
    later = [(i, i + 1) for i in range(1, count - 1, 2)]
    low_far = lax.ppermute(pack, both, later + [(j, i) for i, j in later])
    half_a = half_leaf(leaf_coupling, low, 0)
    half_b = half_leaf(leaf_coupling, low, 1)
    ones = 1 + sum((at % 2**k == 2**k - 1).astype(jnp.int32) for k in range(1, 5))
    pick = jnp.where(ones <= 4, (16 + at) >> ones, 0)
    place = jnp.stack([at, pick]).astype(jnp.int32)
    group_factors, own = branch(place, [pay, pay_a, pay_b, *pay_c], top)
    own_a = shifted(own, "wide", lambda i: i ^ 1)
    factors = prep(at.reshape(1) % 2, low_near, low, low_far)
    two = jnp.stack([own, own_a])
    own_b = shifted(two, "wide", lambda i: i ^ 2)
    cols = leaf_columns - (lax.axis_index(both) * 64 - 64)
    out = full_leaf(cols, half_a, factors, 0)
    four = jnp.concatenate([two, own_b])
    own_c = shifted(four, "wide", lambda i: i ^ 4)
    leaf_coupled = full_leaf(cols, half_b, factors, 1, out)
    far_out = far(
        wide_at ^ far_columns,
        jnp.transpose(far_coupling, (0, 2, 1)),
        [own, own_a, own_b, own_c],
    )
    return leaf_coupled, jnp.transpose(far_out, (0, 2, 1)), group_factors


def solution(mesh):
    spread = P(None, None, ("wide", "narrow"))
    split_first = P(("wide", "narrow"), None, None)
    ids = P(("wide", "narrow"))
    return jax.shard_map(
        steps,
        mesh=mesh,
        in_specs=(split_first, spread, spread, ids, spread, ids),
        out_specs=(spread, spread, split_first),
        check_vma=False,
    )
```

```python
import functools

import jax
import jax.numpy as jnp
from jax import lax
from jax.experimental import pallas as pl
from jax.experimental.pallas import tpu as pltpu
from jax.sharding import PartitionSpec as P

F32 = jnp.float32
BF16 = jnp.bfloat16
ANY = pl.BlockSpec(memory_space=pl.ANY)
VMEM = pl.BlockSpec(memory_space=pltpu.VMEM)
SMEM = pl.BlockSpec(memory_space=pltpu.SMEM)


def params(mib):
    return pltpu.CompilerParams(vmem_limit_bytes=mib * 2**20)


def cost(us):
    return pl.CostEstimate(flops=int(us * 1.15e9), bytes_accessed=4096, transcendentals=0)


def split(x):
    hi = x.astype(BF16)
    lo = (x - hi.astype(F32)).astype(BF16)
    return hi, lo


def mm(a, b):
    return lax.dot_general(a, b, (((1,), (0,)), ((), ())), preferred_element_type=F32)


def mm_nt(a, b):
    return lax.dot_general(a, b, (((1,), (1,)), ((), ())), preferred_element_type=F32)


def mm_tn(a, b):
    return lax.dot_general(a, b, (((0,), (0,)), ((), ())), preferred_element_type=F32)


def lanes(*parts):
    return jnp.concatenate(parts, axis=1)


def rows(*parts):
    return jnp.concatenate(parts, axis=0)


def first_half(shape=(64, 128)):
    return lax.broadcasted_iota(jnp.int32, shape, 1) % 128 < 64


def mixed(m):
    h = m.astype(BF16).astype(F32)
    return jnp.where(first_half(m.shape), h, m - h).astype(BF16)


def left_of(m):
    v = mixed(m)
    return lanes(v, v)


def right_of(m):
    return lanes(*split(m))


def twice(m):
    return rows(m, m)


LEAVES = 16
HALF = 4
PAIRS = 32


def climb_kernel(
    b_hbm, t_hbm, g_ref, top_ref, pay_ref, b_ref, t_ref, u_ref, e_ref, w_ref, sem
):
    t_copies = [
        pltpu.make_async_copy(
            t_hbm.at[pl.ds(16 * n, 16)], t_ref.at[pl.ds(16 * n, 16)], sem.at[n]
        )
        for n in range(4)
    ]
    b_copies = [
        pltpu.make_async_copy(
            b_hbm.at[pl.ds(32 * n, 32)], b_ref.at[pl.ds(32 * n, 32)], sem.at[4 + n]
        )
        for n in range(2)
    ]
    for copy in t_copies + b_copies:
        copy.start()
    first = first_half()

    def turn(s, _):
        for r in range(8):
            x = t_ref[s * 8 + r]
            u_ref[r] = rows(x, x).T
        for g in range(16):
            x = u_ref[:, 8 * g : 8 * g + 8, :]
            e_ref[8 * g : 8 * g + 8, pl.ds(pl.multiple_of(s * 8, 8), 8), :] = jnp.swapaxes(x, 0, 1)
        return 0

    for n in range(4):
        t_copies[n].wait()
        lax.fori_loop(2 * n, 2 * n + 2, turn, 0)

    row = lax.broadcasted_iota(jnp.int32, (64, 128), 0)
    col = lax.broadcasted_iota(jnp.int32, (64, 128), 1)
    w_ref[1, 0:64] = (row == col % 64).astype(BF16)
    w_ref[1, 64:128] = jnp.zeros((64, 128), BF16)

    def right_rows(h):
        w = w_ref[h]
        return rows(w[0:64], w[0:64], w[64:128], w[64:128])

    def down(clusters):
        zs = [
            mm(rows(left_of(e_ref[2 * p]), left_of(e_ref[2 * p + 1])), right_rows(p))
            for p in clusters
        ]
        for p, z in zip(clusters, zs):
            for c in range(2):
                w_ref[2 * p + c] = rows(*split(z[64 * c : 64 * c + 64]))

    def downs(s, _):
        down([s * 8 + j for j in range(8)])
        return 0

    for level in range(3):
        down(range(2**level, 2 ** (level + 1)))
    for level in range(3, 6):
        n = 2**level
        lax.fori_loop(n // 8, n // 4, downs, 0)
    for copy in b_copies:
        copy.wait()

    def leaves(s, acc):
        count = LEAVES // 2
        qs = [s * count + j for j in range(count)]
        ts = qs + [q + 32 for q in qs]
        bs = [b_ref[t] for t in ts]
        grams = [mm_nt(b, twice(b)) for b in bs]
        for j, q in enumerate(qs):
            g_ref[q] = jnp.where(first, grams[j], grams[count + j])
        prods = [mm(left_of(g), right_rows(64 + t)) for g, t in zip(grams, ts)]
        for p, t in zip(prods, ts):
            ph, pl_ = split(p)
            w = w_ref[64 + t][:, 0:64]
            acc = acc + mm_tn(rows(w, w), rows(ph, ph, pl_, pl_))
        return acc

    top = lax.fori_loop(0, 64 // LEAVES, leaves, jnp.zeros((64, 128), F32))
    top_ref[...] = top
    h, l = split(e_ref[1])
    prod = mm(left_of(top), rows(h, h, l, l))
    ph, pl_ = split(prod)
    up = rows(h, l).T[0:64]
    term = mm(lanes(up, up), rows(ph, ph, pl_, pl_))
    pay_ref[...] = jnp.where(first, term, e_ref[0])


def climb(basis, transfers):
    return pl.pallas_call(
        climb_kernel,
        out_shape=(
            jax.ShapeDtypeStruct((32, 64, 128), F32),
            jax.ShapeDtypeStruct((64, 128), F32),
            jax.ShapeDtypeStruct((64, 128), F32),
        ),
        in_specs=[pl.BlockSpec(memory_space=pltpu.HBM)] * 2,
        out_specs=(VMEM,) * 3,
        scratch_shapes=[
            pltpu.VMEM((64, 64, 256), BF16),
            pltpu.VMEM((64, 64, 128), F32),
            pltpu.VMEM((8, 128, 128), F32),
            pltpu.VMEM((128, 64, 128), F32),
            pltpu.VMEM((128, 128, 128), BF16),
            pltpu.SemaphoreType.DMA((6,)),
        ],
        compiler_params=params(20),
        cost_estimate=cost(10),
        name="climb",
    )(basis, transfers)


def chol_lanes(a_ref, panels=range(8), count=64, panel=8):
    sub = lax.broadcasted_iota(jnp.int32, (8, 128), 0)
    for p in panels:
        base = p * panel
        if p > 0:
            for it in range(p, count // 8):

                def body(k, accs):
                    lv = a_ref[k, it * 8 : it * 8 + 8, :]
                    return tuple(
                        accs[j] - lv * a_ref[k, pl.ds(base + j, 8, stride=0), :]
                        for j in range(panel)
                    )

                accs = tuple(
                    a_ref[base + j, it * 8 : it * 8 + 8, :] for j in range(panel)
                )
                accs = lax.fori_loop(0, base, body, accs, unroll=8)
                for j in range(panel):
                    a_ref[base + j, it * 8 : it * 8 + 8, :] = accs[j]
        d = [a_ref[base + j, base : base + 8, :] for j in range(8)]
        invs = []
        for j in range(8):
            piv = jnp.broadcast_to(d[j][j : j + 1, :], (8, 128))
            inv = lax.rsqrt(piv)
            invs.append(inv)
            d[j] = jnp.where(sub >= j, d[j] * inv, 0.0)
            for m in range(j + 1, 8):
                d[m] = d[m] - d[j] * jnp.broadcast_to(d[j][m : m + 1, :], (8, 128))
            a_ref[base + j, base : base + 8, :] = d[j]
            if base > 0:
                a_ref[base + j, 0:base, :] = jnp.zeros((base, 128), F32)
        bc = {}
        for j in range(8):
            for m in range(j + 1, 8):
                bc[j, m] = jnp.broadcast_to(d[j][m : m + 1, :], (8, 128))
        for it in range(p + 1, count // 8):
            v = [a_ref[base + j, it * 8 : it * 8 + 8, :] for j in range(8)]
            for j in range(8):
                v[j] = v[j] * invs[j]
                for m in range(j + 1, 8):
                    v[m] = v[m] - v[j] * bc[j, m]
                a_ref[base + j, it * 8 : it * 8 + 8, :] = v[j]


EARLY = 3


def chol_head_kernel(g_ref, a_ref, u_ref):
    def load(s, _):
        at = pl.ds(pl.multiple_of(s * 8, 8), 8)
        for g in range(4):
            u_ref[:, 8 * g : 8 * g + 8, :] = jnp.swapaxes(g_ref[8 * g : 8 * g + 8, at, :], 0, 1)
        for r in range(8):
            x = u_ref[r, 0:32, :]
            y = pltpu.roll(x, 64, 1)
            a_ref[s * 8 + r] = rows(x, y, x, y).T[0:64]
        return 0

    lax.fori_loop(0, 8, load, 0)
    chol_lanes(a_ref, range(EARLY))


def chol_head(gram):
    return pl.pallas_call(
        chol_head_kernel,
        out_shape=jax.ShapeDtypeStruct((64, 64, 128), F32),
        in_specs=[VMEM],
        out_specs=VMEM,
        scratch_shapes=[pltpu.VMEM((8, 64, 128), F32)],
        compiler_params=params(8),
        cost_estimate=cost(4),
        name="chol_head",
    )(gram)


def chol_tail_kernel(i_ref, low_ref, pack_ref, a_ref, u_ref, v_ref):
    a_ref[...] = i_ref[...]
    chol_lanes(a_ref, range(EARLY, 8))
    below = lax.broadcasted_iota(jnp.int32, (32, 128), 0)

    def paired(x):
        return rows(x, pltpu.roll(x, 96, 1)).T[0:32]

    def gather(s):
        at = pl.ds(pl.multiple_of(s * 8, 8), 8)
        for g in range(8):
            u_ref[:, 8 * g : 8 * g + 8, :] = jnp.swapaxes(a_ref[8 * g : 8 * g + 8, at, :], 0, 1)

    def spread(ref, to, s):
        at = pl.ds(pl.multiple_of(s * 8, 8), 8)
        for g in range(4):
            to[8 * g : 8 * g + 8, at, :] = jnp.swapaxes(ref[:, 8 * g : 8 * g + 8, :], 0, 1)

    def upper(s, _):
        gather(s)
        for r in range(8):
            v_ref[r] = paired(u_ref[r])
        spread(v_ref, low_ref, s)
        return 0

    def lower(s, _):
        gather(s + 4)
        for r in range(8):
            v_ref[r] = paired(u_ref[r])
        spread(v_ref, low_ref, s + 4)
        for r in range(8):
            a = s * 8 + r
            free = jnp.where(below <= a, u_ref[r, 32:64, :], a_ref[a, 0:32, :])
            v_ref[r] = paired(rows(u_ref[r, 0:32, :], free))
        spread(v_ref, pack_ref, s)
        return 0

    lax.fori_loop(0, 4, upper, 0)
    lax.fori_loop(0, 4, lower, 0)
    diagonal = rows(*[a_ref[b, b : b + 1, :] for b in range(32)])
    pack_ref[32] = paired(rows(jnp.zeros((32, 128), F32), diagonal))


def chol_tail(part):
    return pl.pallas_call(
        chol_tail_kernel,
        out_shape=(
            jax.ShapeDtypeStruct((32, 64, 128), F32),
            jax.ShapeDtypeStruct((33, 32, 128), F32),
        ),
        in_specs=[VMEM],
        out_specs=(VMEM, VMEM),
        scratch_shapes=[
            pltpu.VMEM((64, 64, 128), F32),
            pltpu.VMEM((8, 64, 128), F32),
            pltpu.VMEM((8, 32, 128), F32),
        ],
        compiler_params=params(10),
        cost_estimate=cost(5),
        name="chol_tail",
    )(part)


def half_kernel(c0_ref, c1_ref, low_ref, y_ref, s_ref, u_ref, part):
    step = pl.program_id(0)

    def turn(s, _):
        for r in range(8):
            u_ref[r] = rows(c0_ref[s * 8 + r], c1_ref[s * 8 + r]).T
        at = pl.ds(pl.multiple_of(step * 16 + s * 8, 8), 8)
        for g in range(16):
            s_ref[8 * g : 8 * g + 8, at, :] = jnp.swapaxes(u_ref[:, 8 * g : 8 * g + 8, :], 0, 1)
        return 0

    lax.fori_loop(0, 2, turn, 0)

    @pl.when(step == 3)
    def _():
        first = first_half((64, 256))

        def leaf(s, _):
            ts = [s * HALF + j for j in range(HALF)]
            lefts = []
            for t in ts:
                lh, ll = split(low_ref[16 * part + t])
                lefts.append(rows(lh, ll, lh).T)
            at = [(j, n) for j in range(HALF) for n in range(0, 8, 2)]
            zs = []
            for j, n in at:
                wh, wl = split(lanes(s_ref[ts[j] * 8 + n], s_ref[ts[j] * 8 + n + 1]))
                zs.append(mm(lefts[j], rows(wh, wh, wl)))
            for (j, n), z in zip(at, zs):
                yh, yl = split(jnp.where(first, z[0:64], z[64:128]))
                for m in range(2):
                    b = ts[j] * 8 + n + m
                    y_ref[b, :, 0:128] = yh[:, m * 128 : m * 128 + 128]
                    y_ref[b, :, 128:256] = yl[:, m * 128 : m * 128 + 128]
            return 0

        lax.fori_loop(0, 16 // HALF, leaf, 0)


def half_leaf(coupling, low, part):
    return pl.pallas_call(
        functools.partial(half_kernel, part=part),
        out_shape=jax.ShapeDtypeStruct((128, 64, 256), BF16),
        grid=(4,),
        in_specs=[
            pl.BlockSpec((16, 64, 128), lambda s: (s, 0, part)),
            pl.BlockSpec((16, 64, 128), lambda s: (s, 0, part + 2)),
            pl.BlockSpec((32, 64, 128), lambda s: (0, 0, 0)),
        ],
        out_specs=pl.BlockSpec((128, 64, 256), lambda s: (0, 0, 0)),
        scratch_shapes=[pltpu.VMEM((128, 64, 128), F32), pltpu.VMEM((8, 128, 128), F32)],
        compiler_params=params(22),
        cost_estimate=cost(6),
    )(coupling, coupling, low)


def prep_kernel(odd_ref, near_ref, own_ref, far_ref, d_ref):
    first = first_half()
    odd = odd_ref[0]

    def plain(q, _):
        x = own_ref[q]
        y = pltpu.roll(x, 64, 1)
        d_ref[64 + q] = right_of(jnp.where(first, x, y))
        d_ref[96 + q] = right_of(jnp.where(first, y, x))
        return 0

    lax.fori_loop(0, 32, plain, 0, unroll=8)
    half = first[0:32]
    row = lax.broadcasted_iota(jnp.int32, (32, 128), 0)
    col = lax.broadcasted_iota(jnp.int32, (32, 128), 1) % 64 - 32
    for base, ref in ((128 - 128 * odd, near_ref), (128 * odd, far_ref)):

        def packed(s, _, ref=ref, base=base):
            qs = [s * 4 + j for j in range(4)]
            ups = []
            for q in qs:
                diagonal = ref[32, pl.ds(q, 32, stride=0), :]
                rest = jnp.where(col == row, diagonal, 0.0)
                ups.append(jnp.where(col > row, ref[q], rest))
            turned = rows(*ups).T
            shifts = [
                [turned[64 * c + 32 : 64 * c + 64]]
                + [
                    pltpu.roll(turned[64 * c + 32 : 64 * c + 64], 32 * n, 1)
                    for n in range(1, 4)
                ]
                for c in range(2)
            ]
            for j, q in enumerate(qs):
                x = jnp.where(col <= row, ref[q], 0.0)
                y = pltpu.roll(x, 64, 1)
                for c in range(2):
                    at = shifts[c]
                    top = jnp.where(half, at[(4 - j) % 4], at[(6 - j) % 4])
                    top = jnp.where(col < 0, top, 0.0)
                    low = jnp.where(half, x, y) if c == 0 else jnp.where(half, y, x)
                    d_ref[base + 32 * c + q] = right_of(rows(top, low))
            return 0

        lax.fori_loop(0, 8, packed, 0, unroll=2)


def prep(odd, near, own, far):
    return pl.pallas_call(
        prep_kernel,
        out_shape=jax.ShapeDtypeStruct((192, 64, 256), BF16),
        in_specs=[SMEM] + [VMEM] * 3,
        out_specs=VMEM,
        compiler_params=params(16),
        cost_estimate=cost(3),
        name="prep",
    )(odd, near, own, far)


def full_kernel(cols_ref, y_ref, d_ref, *refs, part):
    out_ref, s_ref, u_ref, o_ref, sem = refs[-5:]
    lane = lax.broadcasted_iota(jnp.int32, (64, 256), 1)
    keep = ((lane % 128) < 64).astype(BF16)
    drop = ((lane % 128) >= 64).astype(BF16)

    def pair(s, _):
        ps = [s * PAIRS + j for j in range(PAIRS)]
        zs = []
        for p in ps:
            sa = cols_ref[part * 128 + p]
            sb = cols_ref[part * 128 + 256 + p]
            r = rows(d_ref[sa] * keep, d_ref[sb] * drop)
            y = y_ref[p]
            zs.append(mm(rows(y[:, 0:128], y[:, 128:256]), r))
        for p, z in zip(ps, zs):
            s_ref[p] = z[0:64, 0:128] + z[0:64, 128:256] + z[64:128, 0:128]
        return 0

    lax.fori_loop(0, 128 // PAIRS, pair, 0)

    def send(n):
        return [
            pltpu.make_async_copy(
                o_ref.at[c, pl.ds(16 * n, 16)],
                out_ref.at[pl.ds(16 * n, 16), :, pl.ds((part + 2 * c) * 128, 128)],
                sem.at[n, c],
            )
            for c in range(2)
        ]

    def turn(s, _):
        at = pl.ds(pl.multiple_of(s * 8, 8), 8)
        for g in range(16):
            u_ref[:, 8 * g : 8 * g + 8, :] = jnp.swapaxes(s_ref[8 * g : 8 * g + 8, at, :], 0, 1)
        for r in range(8):
            x = u_ref[r].T
            o_ref[0, s * 8 + r] = x[0:64]
            o_ref[1, s * 8 + r] = x[64:128]
        return 0

    for n in range(4):
        lax.fori_loop(2 * n, 2 * n + 2, turn, 0)
        for copy in send(n):
            copy.start()
    for n in range(4):
        for copy in send(n):
            copy.wait()


def full_leaf(cols, y, d, part, into=None):
    extra = [] if into is None else [into]
    return pl.pallas_call(
        functools.partial(full_kernel, part=part),
        out_shape=jax.ShapeDtypeStruct((64, 64, 512), F32),
        in_specs=[SMEM, VMEM, VMEM] + [pl.BlockSpec(memory_space=pltpu.HBM)] * len(extra),
        out_specs=pl.BlockSpec(memory_space=pltpu.HBM),
        scratch_shapes=[
            pltpu.VMEM((128, 64, 128), F32),
            pltpu.VMEM((8, 128, 128), F32),
            pltpu.VMEM((2, 64, 64, 128), F32),
            pltpu.SemaphoreType.DMA((4, 2)),
        ],
        input_output_aliases={} if into is None else {3: 0},
        compiler_params=params(22),
        cost_estimate=cost(8),
    )(cols, y, d, *extra)


def branch_kernel(at_ref, p0, p1, p2, p3, p4, top_ref, gf_ref, low_ref, t_ref, e_ref, n_ref, a_ref):
    at = at_ref[0]
    pick = at_ref[1]
    first = first_half()

    def place(n, x):
        y = pltpu.roll(x, 64, 1)
        t_ref[n] = jnp.where(first, x, y)
        e_ref[n] = jnp.where(first, y, x)

    place(at, p0[...])
    place(at ^ 1, p1[...])
    near = (0, 1, 3, 2)
    for i in range(2):
        place(at ^ near[2 + i], p2[i])
    for i in range(4):
        place(at ^ 4 ^ near[i], p3[i])
    for i in range(8):
        place(at ^ (12, 8)[i // 4] ^ near[i % 4], p4[i])
    n_ref[0] = top_ref[...]
    for m in range(8):
        n_ref[8 + m] = t_ref[2 * m] + t_ref[2 * m + 1]
    ups = {}
    for p in range(2, 16):
        h, l = split(e_ref[p])
        ups[p] = rows(h, l).T[0:64]
    for level in (2, 1, 0):
        parents = range(2**level, 2 ** (level + 1))
        children = [c for p in parents for c in (2 * p, 2 * p + 1)]
        prods = []
        for c in children:
            h, l = split(e_ref[c])
            prods.append(mm(left_of(n_ref[c]), rows(h, h, l, l)))
        terms = []
        for c, prod in zip(children, prods):
            h, l = split(prod)
            terms.append(mm(lanes(ups[c], ups[c]), rows(h, h, l, l)))
        for n, p in enumerate(parents):
            n_ref[p] = terms[2 * n] + terms[2 * n + 1]

    both = jnp.where(first, n_ref[pick], n_ref[1])
    lane = lax.broadcasted_iota(jnp.int32, (64, 128), 1)

    def load(k, _):
        a_ref[k] = jnp.take_along_axis(both, (lane & 64) + k, axis=1)
        return 0

    lax.fori_loop(0, 64, load, 0, unroll=8)
    chol_lanes(a_ref)

    def store(k, out):
        return jnp.where((lane & 63) == k, a_ref[k], out)

    out = lax.fori_loop(0, 64, store, jnp.zeros((64, 128), F32), unroll=8)
    gf_ref[0] = out.T[0:64]
    low_ref[...] = jnp.where(first, pltpu.roll(out, 64, 1), out)


def branch(at, parts, top):
    return pl.pallas_call(
        branch_kernel,
        out_shape=(
            jax.ShapeDtypeStruct((1, 64, 64), F32),
            jax.ShapeDtypeStruct((64, 128), F32),
        ),
        in_specs=[SMEM] + [VMEM] * 6,
        out_specs=(VMEM, VMEM),
        scratch_shapes=[
            pltpu.VMEM((16, 64, 128), F32),
            pltpu.VMEM((16, 64, 128), F32),
            pltpu.VMEM((16, 64, 128), F32),
            pltpu.VMEM((64, 64, 128), F32),
        ],
        compiler_params=params(8),
        cost_estimate=cost(5),
        name="branch",
    )(at, *parts, top)


def far_kernel(cols_ref, f_ref, l0, l1, l2, l3, o_ref, l_ref, c_ref):
    for s, part in enumerate((l0[...], l1[...], l2[0], l2[1], l3[2], l3[3], l3[0], l3[1])):
        h, l = split(part[:, 0:64])
        l_ref[s] = rows(h, h, l)
    lh, ll = split(l0[...].T[0:64])
    left = lanes(lh, ll, lh)
    halves = []
    for g in range(2):
        for s in range(8):
            x = f_ref[8 * s : 8 * s + 8, 8 * g : 8 * g + 8, :]
            c_ref[8 * g : 8 * g + 8, 8 * s : 8 * s + 8, :] = jnp.swapaxes(x, 0, 1)
        for f in range(8 * g, 8 * g + 8):
            ch, cl = split(c_ref[f])
            halves.append(mm(left, rows(ch, ch, cl)))
    outs = []
    for f in range(16):
        hh, hl = split(halves[f])
        outs.append(mm(lanes(hh, hl, hh), l_ref[cols_ref[f]]))
    for f in range(16):
        c_ref[f] = outs[f]
    for g in range(2):
        for s in range(8):
            x = c_ref[8 * g : 8 * g + 8, 8 * s : 8 * s + 8, :]
            o_ref[8 * s : 8 * s + 8, 8 * g : 8 * g + 8, :] = jnp.swapaxes(x, 0, 1)


def far(cols, coupling, lowers):
    return pl.pallas_call(
        far_kernel,
        out_shape=jax.ShapeDtypeStruct(coupling.shape, F32),
        in_specs=[SMEM] + [VMEM] * 5,
        out_specs=VMEM,
        scratch_shapes=[pltpu.VMEM((8, 192, 64), BF16), pltpu.VMEM((16, 64, 64), F32)],
        compiler_params=params(6),
        cost_estimate=cost(3),
        name="far",
    )(cols, coupling, *lowers)


def shifted(value, axis, to):
    return lax.ppermute(value, axis, [(i, to(i)) for i in range(lax.axis_size(axis))])


def steps(
    basis_t, nested_transfer_matrices, leaf_coupling, leaf_columns, far_coupling, far_columns
):
    basis_t, nested_transfer_matrices, leaf_coupling = (
        pltpu.with_memory_space_constraint(x, pltpu.HBM)
        for x in (basis_t, nested_transfer_matrices, leaf_coupling)
    )
    both = ("wide", "narrow")
    wide_at = lax.axis_index("wide")
    at = lax.axis_index("narrow")
    gram, top, pay = climb(basis_t, nested_transfer_matrices)
    pay_a = shifted(pay, "narrow", lambda i: i ^ 1)
    head = chol_head(gram)
    pair = jnp.stack([pay, pay_a])
    pay_b = shifted(pair, "narrow", lambda i: i ^ 3)
    low, pack = chol_tail(head)
    quad = jnp.concatenate([pair, pay_b])
    pay_c = shifted(quad, "narrow", lambda i: i ^ 4)
    count = lax.axis_size(both)
    low_near = lax.ppermute(pack, both, [(i, i ^ 1) for i in range(count)])
    later = [(i, i + 1) for i in range(1, count - 1, 2)]
    low_far = lax.ppermute(pack, both, later + [(j, i) for i, j in later])
    half_a = half_leaf(leaf_coupling, low, 0)
    octet = jnp.concatenate([quad, pay_c])
    pay_d = shifted(octet, "narrow", lambda i: i ^ 12)
    half_b = half_leaf(leaf_coupling, low, 1)
    ones = 1 + sum((at % 2**k == 2**k - 1).astype(jnp.int32) for k in range(1, 5))
    pick = jnp.where(ones <= 4, (16 + at) >> ones, 0)
    place = jnp.stack([at, pick]).astype(jnp.int32)
    group_factors, own = branch(place, [pay, pay_a, pay_b, pay_c, pay_d], top)
    own_a = shifted(own, "wide", lambda i: i ^ 1)
    factors = prep(at.reshape(1) % 2, low_near, low, low_far)
    two = jnp.stack([own, own_a])
    own_b = shifted(two, "wide", lambda i: i ^ 2)
    cols = leaf_columns - (lax.axis_index(both) * 64 - 64)
    out = full_leaf(cols, half_a, factors, 0)
    four = jnp.concatenate([two, own_b])
    own_c = shifted(four, "wide", lambda i: i ^ 6)
    leaf_coupled = full_leaf(cols, half_b, factors, 1, out)
    far_out = far(
        wide_at ^ far_columns,
        jnp.transpose(far_coupling, (0, 2, 1)),
        [own, own_a, own_b, own_c],
    )
    return leaf_coupled, jnp.transpose(far_out, (0, 2, 1)), group_factors


def solution(mesh):
    spread = P(None, None, ("wide", "narrow"))
    split_first = P(("wide", "narrow"), None, None)
    ids = P(("wide", "narrow"))
    return jax.shard_map(
        steps,
        mesh=mesh,
        in_specs=(split_first, spread, spread, ids, spread, ids),
        out_specs=(spread, spread, split_first),
        check_vma=False,
    )
```

```python
import functools

import jax
import jax.numpy as jnp
from jax import lax
from jax.experimental import pallas as pl
from jax.experimental.pallas import tpu as pltpu
from jax.sharding import PartitionSpec as P

F32 = jnp.float32
BF16 = jnp.bfloat16
ANY = pl.BlockSpec(memory_space=pl.ANY)
VMEM = pl.BlockSpec(memory_space=pltpu.VMEM)
SMEM = pl.BlockSpec(memory_space=pltpu.SMEM)


def params(mib):
    return pltpu.CompilerParams(vmem_limit_bytes=mib * 2**20)


def cost(us):
    return pl.CostEstimate(flops=int(us * 1.15e9), bytes_accessed=4096, transcendentals=0)


def split(x):
    hi = x.astype(BF16)
    lo = (x - hi.astype(F32)).astype(BF16)
    return hi, lo


def mm(a, b):
    return lax.dot_general(a, b, (((1,), (0,)), ((), ())), preferred_element_type=F32)


def mm_nt(a, b):
    return lax.dot_general(a, b, (((1,), (1,)), ((), ())), preferred_element_type=F32)


def mm_tn(a, b):
    return lax.dot_general(a, b, (((0,), (0,)), ((), ())), preferred_element_type=F32)


def lanes(*parts):
    return jnp.concatenate(parts, axis=1)


def rows(*parts):
    return jnp.concatenate(parts, axis=0)


def first_half(shape=(64, 128)):
    return lax.broadcasted_iota(jnp.int32, shape, 1) % 128 < 64


def mixed(m):
    h = m.astype(BF16).astype(F32)
    return jnp.where(first_half(m.shape), h, m - h).astype(BF16)


def left_of(m):
    v = mixed(m)
    return lanes(v, v)


def right_of(m):
    return lanes(*split(m))


def twice(m):
    return rows(m, m)


LEAVES = 32
HALF = 8
PAIRS = 64


def climb_kernel(
    b_hbm, t_hbm, g_ref, top_ref, pay_ref, b_ref, t_ref, u_ref, e_ref, w_ref, sem
):
    t_copies = [
        pltpu.make_async_copy(
            t_hbm.at[pl.ds(16 * n, 16)], t_ref.at[pl.ds(16 * n, 16)], sem.at[n]
        )
        for n in range(4)
    ]
    b_copies = [
        pltpu.make_async_copy(
            b_hbm.at[pl.ds(32 * n, 32)], b_ref.at[pl.ds(32 * n, 32)], sem.at[4 + n]
        )
        for n in range(2)
    ]
    for copy in t_copies + b_copies:
        copy.start()
    first = first_half()

    def turn(s, _):
        for r in range(8):
            x = t_ref[s * 8 + r]
            u_ref[r] = rows(x, x).T
        for g in range(16):
            x = u_ref[:, 8 * g : 8 * g + 8, :]
            e_ref[8 * g : 8 * g + 8, pl.ds(pl.multiple_of(s * 8, 8), 8), :] = jnp.swapaxes(x, 0, 1)
        return 0

    for n in range(4):
        t_copies[n].wait()
        lax.fori_loop(2 * n, 2 * n + 2, turn, 0)

    row = lax.broadcasted_iota(jnp.int32, (64, 128), 0)
    col = lax.broadcasted_iota(jnp.int32, (64, 128), 1)
    w_ref[1, 0:64] = (row == col % 64).astype(BF16)
    w_ref[1, 64:128] = jnp.zeros((64, 128), BF16)

    def right_rows(h):
        w = w_ref[h]
        return rows(w[0:64], w[0:64], w[64:128], w[64:128])

    def down(clusters):
        zs = [
            mm(rows(left_of(e_ref[2 * p]), left_of(e_ref[2 * p + 1])), right_rows(p))
            for p in clusters
        ]
        for p, z in zip(clusters, zs):
            for c in range(2):
                w_ref[2 * p + c] = rows(*split(z[64 * c : 64 * c + 64]))

    def downs(s, _):
        down([s * 8 + j for j in range(8)])
        return 0

    for level in range(3):
        down(range(2**level, 2 ** (level + 1)))
    for level in range(3, 6):
        n = 2**level
        lax.fori_loop(n // 8, n // 4, downs, 0)
    for copy in b_copies:
        copy.wait()

    def leaves(s, acc):
        count = LEAVES // 2
        qs = [s * count + j for j in range(count)]
        ts = qs + [q + 32 for q in qs]
        bs = [b_ref[t] for t in ts]
        grams = [mm_nt(b, twice(b)) for b in bs]
        for j, q in enumerate(qs):
            g_ref[q] = jnp.where(first, grams[j], grams[count + j])
        prods = [mm(left_of(g), right_rows(64 + t)) for g, t in zip(grams, ts)]
        for p, t in zip(prods, ts):
            ph, pl_ = split(p)
            w = w_ref[64 + t][:, 0:64]
            acc = acc + mm_tn(rows(w, w), rows(ph, ph, pl_, pl_))
        return acc

    top = lax.fori_loop(0, 64 // LEAVES, leaves, jnp.zeros((64, 128), F32))
    top_ref[...] = top
    h, l = split(e_ref[1])
    prod = mm(left_of(top), rows(h, h, l, l))
    ph, pl_ = split(prod)
    up = rows(h, l).T[0:64]
    term = mm(lanes(up, up), rows(ph, ph, pl_, pl_))
    pay_ref[...] = jnp.where(first, term, e_ref[0])


def climb(basis, transfers):
    return pl.pallas_call(
        climb_kernel,
        out_shape=(
            jax.ShapeDtypeStruct((32, 64, 128), F32),
            jax.ShapeDtypeStruct((64, 128), F32),
            jax.ShapeDtypeStruct((64, 128), F32),
        ),
        in_specs=[pl.BlockSpec(memory_space=pltpu.HBM)] * 2,
        out_specs=(VMEM,) * 3,
        scratch_shapes=[
            pltpu.VMEM((64, 64, 256), BF16),
            pltpu.VMEM((64, 64, 128), F32),
            pltpu.VMEM((8, 128, 128), F32),
            pltpu.VMEM((128, 64, 128), F32),
            pltpu.VMEM((128, 128, 128), BF16),
            pltpu.SemaphoreType.DMA((6,)),
        ],
        compiler_params=params(20),
        cost_estimate=cost(10),
        name="climb",
    )(basis, transfers)


def chol_lanes(a_ref, panels=range(8), count=64, panel=8):
    sub = lax.broadcasted_iota(jnp.int32, (8, 128), 0)
    for p in panels:
        base = p * panel
        if p > 0:
            for it in range(p, count // 8):

                def body(k, accs):
                    lv = a_ref[k, it * 8 : it * 8 + 8, :]
                    return tuple(
                        accs[j] - lv * a_ref[k, pl.ds(base + j, 8, stride=0), :]
                        for j in range(panel)
                    )

                accs = tuple(
                    a_ref[base + j, it * 8 : it * 8 + 8, :] for j in range(panel)
                )
                accs = lax.fori_loop(0, base, body, accs, unroll=8)
                for j in range(panel):
                    a_ref[base + j, it * 8 : it * 8 + 8, :] = accs[j]
        d = [a_ref[base + j, base : base + 8, :] for j in range(8)]
        invs = []
        for j in range(8):
            piv = jnp.broadcast_to(d[j][j : j + 1, :], (8, 128))
            inv = lax.rsqrt(piv)
            invs.append(inv)
            d[j] = jnp.where(sub >= j, d[j] * inv, 0.0)
            for m in range(j + 1, 8):
                d[m] = d[m] - d[j] * jnp.broadcast_to(d[j][m : m + 1, :], (8, 128))
            a_ref[base + j, base : base + 8, :] = d[j]
            if base > 0:
                a_ref[base + j, 0:base, :] = jnp.zeros((base, 128), F32)
        bc = {}
        for j in range(8):
            for m in range(j + 1, 8):
                bc[j, m] = jnp.broadcast_to(d[j][m : m + 1, :], (8, 128))
        for it in range(p + 1, count // 8):
            v = [a_ref[base + j, it * 8 : it * 8 + 8, :] for j in range(8)]
            for j in range(8):
                v[j] = v[j] * invs[j]
                for m in range(j + 1, 8):
                    v[m] = v[m] - v[j] * bc[j, m]
                a_ref[base + j, it * 8 : it * 8 + 8, :] = v[j]


EARLY = 3


def chol_head_kernel(g_ref, a_ref, u_ref):
    def load(s, _):
        at = pl.ds(pl.multiple_of(s * 8, 8), 8)
        for g in range(4):
            u_ref[:, 8 * g : 8 * g + 8, :] = jnp.swapaxes(g_ref[8 * g : 8 * g + 8, at, :], 0, 1)
        for r in range(8):
            x = u_ref[r, 0:32, :]
            y = pltpu.roll(x, 64, 1)
            a_ref[s * 8 + r] = rows(x, y, x, y).T[0:64]
        return 0

    lax.fori_loop(0, 8, load, 0)
    chol_lanes(a_ref, range(EARLY))


def chol_head(gram):
    return pl.pallas_call(
        chol_head_kernel,
        out_shape=jax.ShapeDtypeStruct((64, 64, 128), F32),
        in_specs=[VMEM],
        out_specs=VMEM,
        scratch_shapes=[pltpu.VMEM((8, 64, 128), F32)],
        compiler_params=params(8),
        cost_estimate=cost(4),
        name="chol_head",
    )(gram)


def chol_tail_kernel(i_ref, low_ref, pack_ref, a_ref, u_ref, v_ref):
    a_ref[...] = i_ref[...]
    chol_lanes(a_ref, range(EARLY, 8))
    below = lax.broadcasted_iota(jnp.int32, (32, 128), 0)

    def paired(x):
        return rows(x, pltpu.roll(x, 96, 1)).T[0:32]

    def gather(s):
        at = pl.ds(pl.multiple_of(s * 8, 8), 8)
        for g in range(8):
            u_ref[:, 8 * g : 8 * g + 8, :] = jnp.swapaxes(a_ref[8 * g : 8 * g + 8, at, :], 0, 1)

    def spread(ref, to, s):
        at = pl.ds(pl.multiple_of(s * 8, 8), 8)
        for g in range(4):
            to[8 * g : 8 * g + 8, at, :] = jnp.swapaxes(ref[:, 8 * g : 8 * g + 8, :], 0, 1)

    def upper(s, _):
        gather(s)
        for r in range(8):
            v_ref[r] = paired(u_ref[r])
        spread(v_ref, low_ref, s)
        return 0

    def lower(s, _):
        gather(s + 4)
        for r in range(8):
            v_ref[r] = paired(u_ref[r])
        spread(v_ref, low_ref, s + 4)
        for r in range(8):
            a = s * 8 + r
            free = jnp.where(below <= a, u_ref[r, 32:64, :], a_ref[a, 0:32, :])
            v_ref[r] = paired(rows(u_ref[r, 0:32, :], free))
        spread(v_ref, pack_ref, s)
        return 0

    lax.fori_loop(0, 4, upper, 0)
    lax.fori_loop(0, 4, lower, 0)
    diagonal = rows(*[a_ref[b, b : b + 1, :] for b in range(32)])
    pack_ref[32] = paired(rows(jnp.zeros((32, 128), F32), diagonal))


def chol_tail(part):
    return pl.pallas_call(
        chol_tail_kernel,
        out_shape=(
            jax.ShapeDtypeStruct((32, 64, 128), F32),
            jax.ShapeDtypeStruct((33, 32, 128), F32),
        ),
        in_specs=[VMEM],
        out_specs=(VMEM, VMEM),
        scratch_shapes=[
            pltpu.VMEM((64, 64, 128), F32),
            pltpu.VMEM((8, 64, 128), F32),
            pltpu.VMEM((8, 32, 128), F32),
        ],
        compiler_params=params(10),
        cost_estimate=cost(5),
        name="chol_tail",
    )(part)


def half_kernel(c0_ref, c1_ref, low_ref, y_ref, s_ref, u_ref, part):
    step = pl.program_id(0)

    def turn(s, _):
        for r in range(8):
            u_ref[r] = rows(c0_ref[s * 8 + r], c1_ref[s * 8 + r]).T
        at = pl.ds(pl.multiple_of(step * 16 + s * 8, 8), 8)
        for g in range(16):
            s_ref[8 * g : 8 * g + 8, at, :] = jnp.swapaxes(u_ref[:, 8 * g : 8 * g + 8, :], 0, 1)
        return 0

    lax.fori_loop(0, 2, turn, 0)

    @pl.when(step == 3)
    def _():
        first = first_half((64, 256))

        def leaf(s, _):
            ts = [s * HALF + j for j in range(HALF)]
            lefts = []
            for t in ts:
                lh, ll = split(low_ref[16 * part + t])
                lefts.append(rows(lh, ll, lh).T)
            at = [(j, n) for j in range(HALF) for n in range(0, 8, 2)]
            zs = []
            for j, n in at:
                wh, wl = split(lanes(s_ref[ts[j] * 8 + n], s_ref[ts[j] * 8 + n + 1]))
                zs.append(mm(lefts[j], rows(wh, wh, wl)))
            for (j, n), z in zip(at, zs):
                yh, yl = split(jnp.where(first, z[0:64], z[64:128]))
                for m in range(2):
                    b = ts[j] * 8 + n + m
                    y_ref[b, :, 0:128] = yh[:, m * 128 : m * 128 + 128]
                    y_ref[b, :, 128:256] = yl[:, m * 128 : m * 128 + 128]
            return 0

        lax.fori_loop(0, 16 // HALF, leaf, 0)


def half_leaf(coupling, low, part):
    return pl.pallas_call(
        functools.partial(half_kernel, part=part),
        out_shape=jax.ShapeDtypeStruct((128, 64, 256), BF16),
        grid=(4,),
        in_specs=[
            pl.BlockSpec((16, 64, 128), lambda s: (s, 0, part)),
            pl.BlockSpec((16, 64, 128), lambda s: (s, 0, part + 2)),
            pl.BlockSpec((32, 64, 128), lambda s: (0, 0, 0)),
        ],
        out_specs=pl.BlockSpec((128, 64, 256), lambda s: (0, 0, 0)),
        scratch_shapes=[pltpu.VMEM((128, 64, 128), F32), pltpu.VMEM((8, 128, 128), F32)],
        compiler_params=params(22),
        cost_estimate=cost(6),
    )(coupling, coupling, low)


def prep_kernel(odd_ref, near_ref, own_ref, far_ref, d_ref):
    first = first_half()
    odd = odd_ref[0]

    def plain(q, _):
        x = own_ref[q]
        y = pltpu.roll(x, 64, 1)
        d_ref[64 + q] = right_of(jnp.where(first, x, y))
        d_ref[96 + q] = right_of(jnp.where(first, y, x))
        return 0

    lax.fori_loop(0, 32, plain, 0, unroll=8)
    half = first[0:32]
    row = lax.broadcasted_iota(jnp.int32, (32, 128), 0)
    col = lax.broadcasted_iota(jnp.int32, (32, 128), 1) % 64 - 32
    for base, ref in ((128 - 128 * odd, near_ref), (128 * odd, far_ref)):

        def packed(s, _, ref=ref, base=base):
            qs = [s * 4 + j for j in range(4)]
            ups = []
            for q in qs:
                diagonal = ref[32, pl.ds(q, 32, stride=0), :]
                rest = jnp.where(col == row, diagonal, 0.0)
                ups.append(jnp.where(col > row, ref[q], rest))
            turned = rows(*ups).T
            shifts = [
                [turned[64 * c + 32 : 64 * c + 64]]
                + [
                    pltpu.roll(turned[64 * c + 32 : 64 * c + 64], 32 * n, 1)
                    for n in range(1, 4)
                ]
                for c in range(2)
            ]
            for j, q in enumerate(qs):
                x = jnp.where(col <= row, ref[q], 0.0)
                y = pltpu.roll(x, 64, 1)
                for c in range(2):
                    at = shifts[c]
                    top = jnp.where(half, at[(4 - j) % 4], at[(6 - j) % 4])
                    top = jnp.where(col < 0, top, 0.0)
                    low = jnp.where(half, x, y) if c == 0 else jnp.where(half, y, x)
                    d_ref[base + 32 * c + q] = right_of(rows(top, low))
            return 0

        lax.fori_loop(0, 8, packed, 0, unroll=2)


def prep(odd, near, own, far):
    return pl.pallas_call(
        prep_kernel,
        out_shape=jax.ShapeDtypeStruct((192, 64, 256), BF16),
        in_specs=[SMEM] + [VMEM] * 3,
        out_specs=VMEM,
        compiler_params=params(16),
        cost_estimate=cost(3),
        name="prep",
    )(odd, near, own, far)


def full_kernel(cols_ref, y_ref, d_ref, *refs, part):
    out_ref, s_ref, u_ref, o_ref, sem = refs[-5:]
    lane = lax.broadcasted_iota(jnp.int32, (64, 256), 1)
    keep = ((lane % 128) < 64).astype(BF16)
    drop = ((lane % 128) >= 64).astype(BF16)

    def pair(s, _):
        ps = [s * PAIRS + j for j in range(PAIRS)]
        zs = []
        for p in ps:
            sa = cols_ref[part * 128 + p]
            sb = cols_ref[part * 128 + 256 + p]
            r = rows(d_ref[sa] * keep, d_ref[sb] * drop)
            y = y_ref[p]
            zs.append(mm(rows(y[:, 0:128], y[:, 128:256]), r))
        for p, z in zip(ps, zs):
            s_ref[p] = z[0:64, 0:128] + z[0:64, 128:256] + z[64:128, 0:128]
        return 0

    lax.fori_loop(0, 128 // PAIRS, pair, 0)

    def send(n):
        return [
            pltpu.make_async_copy(
                o_ref.at[c, pl.ds(16 * n, 16)],
                out_ref.at[pl.ds(16 * n, 16), :, pl.ds((part + 2 * c) * 128, 128)],
                sem.at[n, c],
            )
            for c in range(2)
        ]

    def turn(s, _):
        at = pl.ds(pl.multiple_of(s * 8, 8), 8)
        for g in range(16):
            u_ref[:, 8 * g : 8 * g + 8, :] = jnp.swapaxes(s_ref[8 * g : 8 * g + 8, at, :], 0, 1)
        for r in range(8):
            x = u_ref[r].T
            o_ref[0, s * 8 + r] = x[0:64]
            o_ref[1, s * 8 + r] = x[64:128]
        return 0

    for n in range(4):
        lax.fori_loop(2 * n, 2 * n + 2, turn, 0)
        for copy in send(n):
            copy.start()
    for n in range(4):
        for copy in send(n):
            copy.wait()


def full_leaf(cols, y, d, part, into=None):
    extra = [] if into is None else [into]
    return pl.pallas_call(
        functools.partial(full_kernel, part=part),
        out_shape=jax.ShapeDtypeStruct((64, 64, 512), F32),
        in_specs=[SMEM, VMEM, VMEM] + [pl.BlockSpec(memory_space=pltpu.HBM)] * len(extra),
        out_specs=pl.BlockSpec(memory_space=pltpu.HBM),
        scratch_shapes=[
            pltpu.VMEM((128, 64, 128), F32),
            pltpu.VMEM((8, 128, 128), F32),
            pltpu.VMEM((2, 64, 64, 128), F32),
            pltpu.SemaphoreType.DMA((4, 2)),
        ],
        input_output_aliases={} if into is None else {3: 0},
        compiler_params=params(22),
        cost_estimate=cost(8),
    )(cols, y, d, *extra)


def branch_kernel(at_ref, p0, p1, p2, p3, p4, top_ref, gf_ref, low_ref, t_ref, e_ref, n_ref, a_ref):
    at = at_ref[0]
    pick = at_ref[1]
    first = first_half()

    def place(n, x):
        y = pltpu.roll(x, 64, 1)
        t_ref[n] = jnp.where(first, x, y)
        e_ref[n] = jnp.where(first, y, x)

    place(at, p0[...])
    place(at ^ 1, p1[...])
    near = (0, 1, 3, 2)
    for i in range(2):
        place(at ^ near[2 + i], p2[i])
    for i in range(4):
        place(at ^ 4 ^ near[i], p3[i])
    for i in range(8):
        place(at ^ (12, 8)[i // 4] ^ near[i % 4], p4[i])
    n_ref[0] = top_ref[...]
    for m in range(8):
        n_ref[8 + m] = t_ref[2 * m] + t_ref[2 * m + 1]
    ups = {}
    for p in range(2, 16):
        h, l = split(e_ref[p])
        ups[p] = rows(h, l).T[0:64]
    for level in (2, 1, 0):
        parents = range(2**level, 2 ** (level + 1))
        children = [c for p in parents for c in (2 * p, 2 * p + 1)]
        prods = []
        for c in children:
            h, l = split(e_ref[c])
            prods.append(mm(left_of(n_ref[c]), rows(h, h, l, l)))
        terms = []
        for c, prod in zip(children, prods):
            h, l = split(prod)
            terms.append(mm(lanes(ups[c], ups[c]), rows(h, h, l, l)))
        for n, p in enumerate(parents):
            n_ref[p] = terms[2 * n] + terms[2 * n + 1]

    both = jnp.where(first, n_ref[pick], n_ref[1])
    lane = lax.broadcasted_iota(jnp.int32, (64, 128), 1)

    def load(k, _):
        a_ref[k] = jnp.take_along_axis(both, (lane & 64) + k, axis=1)
        return 0

    lax.fori_loop(0, 64, load, 0, unroll=8)
    chol_lanes(a_ref)

    def store(k, out):
        return jnp.where((lane & 63) == k, a_ref[k], out)

    out = lax.fori_loop(0, 64, store, jnp.zeros((64, 128), F32), unroll=8)
    gf_ref[0] = out.T[0:64]
    low_ref[...] = jnp.where(first, pltpu.roll(out, 64, 1), out)


def branch(at, parts, top):
    return pl.pallas_call(
        branch_kernel,
        out_shape=(
            jax.ShapeDtypeStruct((1, 64, 64), F32),
            jax.ShapeDtypeStruct((64, 128), F32),
        ),
        in_specs=[SMEM] + [VMEM] * 6,
        out_specs=(VMEM, VMEM),
        scratch_shapes=[
            pltpu.VMEM((16, 64, 128), F32),
            pltpu.VMEM((16, 64, 128), F32),
            pltpu.VMEM((16, 64, 128), F32),
            pltpu.VMEM((64, 64, 128), F32),
        ],
        compiler_params=params(8),
        cost_estimate=cost(5),
        name="branch",
    )(at, *parts, top)


def far_kernel(cols_ref, f_ref, l0, l1, l2, l3, o_ref, l_ref, c_ref):
    for s, part in enumerate((l0[...], l1[...], l2[0], l2[1], l3[2], l3[3], l3[0], l3[1])):
        h, l = split(part[:, 0:64])
        l_ref[s] = rows(h, h, l)
    lh, ll = split(l0[...].T[0:64])
    left = lanes(lh, ll, lh)
    halves = []
    for g in range(2):
        for s in range(8):
            x = f_ref[8 * s : 8 * s + 8, 8 * g : 8 * g + 8, :]
            c_ref[8 * g : 8 * g + 8, 8 * s : 8 * s + 8, :] = jnp.swapaxes(x, 0, 1)
        for f in range(8 * g, 8 * g + 8):
            ch, cl = split(c_ref[f])
            halves.append(mm(left, rows(ch, ch, cl)))
    outs = []
    for f in range(16):
        hh, hl = split(halves[f])
        outs.append(mm(lanes(hh, hl, hh), l_ref[cols_ref[f]]))
    for f in range(16):
        c_ref[f] = outs[f]
    for g in range(2):
        for s in range(8):
            x = c_ref[8 * g : 8 * g + 8, 8 * s : 8 * s + 8, :]
            o_ref[8 * s : 8 * s + 8, 8 * g : 8 * g + 8, :] = jnp.swapaxes(x, 0, 1)


def far(cols, coupling, lowers):
    return pl.pallas_call(
        far_kernel,
        out_shape=jax.ShapeDtypeStruct(coupling.shape, F32),
        in_specs=[SMEM] + [VMEM] * 5,
        out_specs=VMEM,
        scratch_shapes=[pltpu.VMEM((8, 192, 64), BF16), pltpu.VMEM((16, 64, 64), F32)],
        compiler_params=params(6),
        cost_estimate=cost(3),
        name="far",
    )(cols, coupling, *lowers)


def shifted(value, axis, to):
    return lax.ppermute(value, axis, [(i, to(i)) for i in range(lax.axis_size(axis))])


def steps(
    basis_t, nested_transfer_matrices, leaf_coupling, leaf_columns, far_coupling, far_columns
):
    basis_t, nested_transfer_matrices, leaf_coupling = (
        pltpu.with_memory_space_constraint(x, pltpu.HBM)
        for x in (basis_t, nested_transfer_matrices, leaf_coupling)
    )
    both = ("wide", "narrow")
    wide_at = lax.axis_index("wide")
    at = lax.axis_index("narrow")
    gram, top, pay = climb(basis_t, nested_transfer_matrices)
    pay_a = shifted(pay, "narrow", lambda i: i ^ 1)
    head = chol_head(gram)
    pair = jnp.stack([pay, pay_a])
    pay_b = shifted(pair, "narrow", lambda i: i ^ 3)
    low, pack = chol_tail(head)
    quad = jnp.concatenate([pair, pay_b])
    pay_c = shifted(quad, "narrow", lambda i: i ^ 4)
    count = lax.axis_size(both)
    low_near = lax.ppermute(pack, both, [(i, i ^ 1) for i in range(count)])
    later = [(i, i + 1) for i in range(1, count - 1, 2)]
    low_far = lax.ppermute(pack, both, later + [(j, i) for i, j in later])
    half_a = half_leaf(leaf_coupling, low, 0)
    octet = jnp.concatenate([quad, pay_c])
    pay_d = shifted(octet, "narrow", lambda i: i ^ 12)
    half_b = half_leaf(leaf_coupling, low, 1)
    ones = 1 + sum((at % 2**k == 2**k - 1).astype(jnp.int32) for k in range(1, 5))
    pick = jnp.where(ones <= 4, (16 + at) >> ones, 0)
    place = jnp.stack([at, pick]).astype(jnp.int32)
    group_factors, own = branch(place, [pay, pay_a, pay_b, pay_c, pay_d], top)
    own_a = shifted(own, "wide", lambda i: i ^ 1)
    factors = prep(at.reshape(1) % 2, low_near, low, low_far)
    two = jnp.stack([own, own_a])
    own_b = shifted(two, "wide", lambda i: i ^ 2)
    cols = leaf_columns - (lax.axis_index(both) * 64 - 64)
    out = full_leaf(cols, half_a, factors, 0)
    four = jnp.concatenate([two, own_b])
    own_c = shifted(four, "wide", lambda i: i ^ 6)
    leaf_coupled = full_leaf(cols, half_b, factors, 1, out)
    far_out = far(
        wide_at ^ far_columns,
        jnp.transpose(far_coupling, (0, 2, 1)),
        [own, own_a, own_b, own_c],
    )
    return leaf_coupled, jnp.transpose(far_out, (0, 2, 1)), group_factors


def solution(mesh):
    spread = P(None, None, ("wide", "narrow"))
    split_first = P(("wide", "narrow"), None, None)
    ids = P(("wide", "narrow"))
    return jax.shard_map(
        steps,
        mesh=mesh,
        in_specs=(split_first, spread, spread, ids, spread, ids),
        out_specs=(spread, spread, split_first),
        check_vma=False,
    )
```

```python
import functools

import jax
import jax.numpy as jnp
from jax import lax
from jax.experimental import pallas as pl
from jax.experimental.pallas import tpu as pltpu
from jax.sharding import PartitionSpec as P

F32 = jnp.float32
BF16 = jnp.bfloat16
ANY = pl.BlockSpec(memory_space=pl.ANY)
VMEM = pl.BlockSpec(memory_space=pltpu.VMEM)
SMEM = pl.BlockSpec(memory_space=pltpu.SMEM)


def params(mib):
    return pltpu.CompilerParams(vmem_limit_bytes=mib * 2**20)


def cost(us):
    return pl.CostEstimate(flops=int(us * 1.15e9), bytes_accessed=4096, transcendentals=0)


def split(x):
    hi = x.astype(BF16)
    lo = (x - hi.astype(F32)).astype(BF16)
    return hi, lo


def mm(a, b):
    return lax.dot_general(a, b, (((1,), (0,)), ((), ())), preferred_element_type=F32)


def mm_nt(a, b):
    return lax.dot_general(a, b, (((1,), (1,)), ((), ())), preferred_element_type=F32)


def mm_tn(a, b):
    return lax.dot_general(a, b, (((0,), (0,)), ((), ())), preferred_element_type=F32)


def lanes(*parts):
    return jnp.concatenate(parts, axis=1)


def rows(*parts):
    return jnp.concatenate(parts, axis=0)


def first_half(shape=(64, 128)):
    return lax.broadcasted_iota(jnp.int32, shape, 1) % 128 < 64


def mixed(m):
    h = m.astype(BF16).astype(F32)
    return jnp.where(first_half(m.shape), h, m - h).astype(BF16)


def left_of(m):
    v = mixed(m)
    return lanes(v, v)


def right_of(m):
    return lanes(*split(m))


def twice(m):
    return rows(m, m)


LEAVES = 32
HALF = 8
PAIRS = 64


def climb_kernel(
    b_hbm, t_hbm, g_ref, top_ref, pay_ref, b_ref, t_ref, u_ref, e_ref, w_ref, sem
):
    t_copies = [
        pltpu.make_async_copy(
            t_hbm.at[pl.ds(16 * n, 16)], t_ref.at[pl.ds(16 * n, 16)], sem.at[n]
        )
        for n in range(4)
    ]
    b_copies = [
        pltpu.make_async_copy(
            b_hbm.at[pl.ds(32 * n, 32)], b_ref.at[pl.ds(32 * n, 32)], sem.at[4 + n]
        )
        for n in range(2)
    ]
    for copy in t_copies + b_copies:
        copy.start()
    first = first_half()

    def turn(s, _):
        for r in range(8):
            x = t_ref[s * 8 + r]
            u_ref[r] = rows(x, x).T
        for g in range(16):
            x = u_ref[:, 8 * g : 8 * g + 8, :]
            e_ref[8 * g : 8 * g + 8, pl.ds(pl.multiple_of(s * 8, 8), 8), :] = jnp.swapaxes(x, 0, 1)
        return 0

    for n in range(4):
        t_copies[n].wait()
        lax.fori_loop(2 * n, 2 * n + 2, turn, 0)

    row = lax.broadcasted_iota(jnp.int32, (64, 128), 0)
    col = lax.broadcasted_iota(jnp.int32, (64, 128), 1)
    w_ref[1, 0:64] = (row == col % 64).astype(BF16)
    w_ref[1, 64:128] = jnp.zeros((64, 128), BF16)

    def right_rows(h):
        w = w_ref[h]
        return rows(w[0:64], w[0:64], w[64:128], w[64:128])

    def down(clusters):
        zs = [
            mm(rows(left_of(e_ref[2 * p]), left_of(e_ref[2 * p + 1])), right_rows(p))
            for p in clusters
        ]
        for p, z in zip(clusters, zs):
            for c in range(2):
                w_ref[2 * p + c] = rows(*split(z[64 * c : 64 * c + 64]))

    def downs(s, _):
        down([s * 8 + j for j in range(8)])
        return 0

    for level in range(3):
        down(range(2**level, 2 ** (level + 1)))
    for level in range(3, 6):
        n = 2**level
        lax.fori_loop(n // 8, n // 4, downs, 0)
    for copy in b_copies:
        copy.wait()

    def leaves(s, acc):
        count = LEAVES // 2
        qs = [s * count + j for j in range(count)]
        ts = qs + [q + 32 for q in qs]
        bs = [b_ref[t] for t in ts]
        grams = [mm_nt(b, twice(b)) for b in bs]
        for j, q in enumerate(qs):
            g_ref[q] = jnp.where(first, grams[j], grams[count + j])
        prods = [mm(left_of(g), right_rows(64 + t)) for g, t in zip(grams, ts)]
        for p, t in zip(prods, ts):
            ph, pl_ = split(p)
            w = w_ref[64 + t][:, 0:64]
            acc = acc + mm_tn(rows(w, w), rows(ph, ph, pl_, pl_))
        return acc

    top = lax.fori_loop(0, 64 // LEAVES, leaves, jnp.zeros((64, 128), F32))
    top_ref[...] = top
    h, l = split(e_ref[1])
    prod = mm(left_of(top), rows(h, h, l, l))
    ph, pl_ = split(prod)
    up = rows(h, l).T[0:64]
    term = mm(lanes(up, up), rows(ph, ph, pl_, pl_))
    pay_ref[...] = jnp.where(first, term, e_ref[0])


def climb(basis, transfers):
    return pl.pallas_call(
        climb_kernel,
        out_shape=(
            jax.ShapeDtypeStruct((32, 64, 128), F32),
            jax.ShapeDtypeStruct((64, 128), F32),
            jax.ShapeDtypeStruct((64, 128), F32),
        ),
        in_specs=[pl.BlockSpec(memory_space=pltpu.HBM)] * 2,
        out_specs=(VMEM,) * 3,
        scratch_shapes=[
            pltpu.VMEM((64, 64, 256), BF16),
            pltpu.VMEM((64, 64, 128), F32),
            pltpu.VMEM((8, 128, 128), F32),
            pltpu.VMEM((128, 64, 128), F32),
            pltpu.VMEM((128, 128, 128), BF16),
            pltpu.SemaphoreType.DMA((6,)),
        ],
        compiler_params=params(20),
        cost_estimate=cost(10),
        name="climb",
    )(basis, transfers)


def chol_lanes(a_ref, panels=range(8), count=64, panel=8):
    sub = lax.broadcasted_iota(jnp.int32, (8, 128), 0)
    for p in panels:
        base = p * panel
        if p > 0:
            for it in range(p, count // 8):

                def body(k, accs):
                    lv = a_ref[k, it * 8 : it * 8 + 8, :]
                    return tuple(
                        accs[j] - lv * a_ref[k, pl.ds(base + j, 8, stride=0), :]
                        for j in range(panel)
                    )

                accs = tuple(
                    a_ref[base + j, it * 8 : it * 8 + 8, :] for j in range(panel)
                )
                accs = lax.fori_loop(0, base, body, accs, unroll=8)
                for j in range(panel):
                    a_ref[base + j, it * 8 : it * 8 + 8, :] = accs[j]
        d = [a_ref[base + j, base : base + 8, :] for j in range(8)]
        invs = []
        for j in range(8):
            piv = jnp.broadcast_to(d[j][j : j + 1, :], (8, 128))
            inv = lax.rsqrt(piv)
            invs.append(inv)
            d[j] = jnp.where(sub >= j, d[j] * inv, 0.0)
            for m in range(j + 1, 8):
                d[m] = d[m] - d[j] * jnp.broadcast_to(d[j][m : m + 1, :], (8, 128))
            a_ref[base + j, base : base + 8, :] = d[j]
            if base > 0:
                a_ref[base + j, 0:base, :] = jnp.zeros((base, 128), F32)
        bc = {}
        for j in range(8):
            for m in range(j + 1, 8):
                bc[j, m] = jnp.broadcast_to(d[j][m : m + 1, :], (8, 128))
        for it in range(p + 1, count // 8):
            v = [a_ref[base + j, it * 8 : it * 8 + 8, :] for j in range(8)]
            for j in range(8):
                v[j] = v[j] * invs[j]
                for m in range(j + 1, 8):
                    v[m] = v[m] - v[j] * bc[j, m]
                a_ref[base + j, it * 8 : it * 8 + 8, :] = v[j]


EARLY = 3


def chol_head_kernel(g_ref, a_ref, u_ref):
    def load(s, _):
        at = pl.ds(pl.multiple_of(s * 8, 8), 8)
        for g in range(4):
            u_ref[:, 8 * g : 8 * g + 8, :] = jnp.swapaxes(g_ref[8 * g : 8 * g + 8, at, :], 0, 1)
        for r in range(8):
            x = u_ref[r, 0:32, :]
            y = pltpu.roll(x, 64, 1)
            a_ref[s * 8 + r] = rows(x, y, x, y).T[0:64]
        return 0

    lax.fori_loop(0, 8, load, 0)
    chol_lanes(a_ref, range(EARLY))


def chol_head(gram):
    return pl.pallas_call(
        chol_head_kernel,
        out_shape=jax.ShapeDtypeStruct((64, 64, 128), F32),
        in_specs=[VMEM],
        out_specs=VMEM,
        scratch_shapes=[pltpu.VMEM((8, 64, 128), F32)],
        compiler_params=params(8),
        cost_estimate=cost(4),
        name="chol_head",
    )(gram)


def chol_mid_kernel(i_ref, a_ref):
    a_ref[...] = i_ref[...]
    chol_lanes(a_ref, range(EARLY, 8))


def chol_mid(part):
    return pl.pallas_call(
        chol_mid_kernel,
        out_shape=jax.ShapeDtypeStruct((64, 64, 128), F32),
        in_specs=[VMEM],
        out_specs=VMEM,
        compiler_params=params(8),
        cost_estimate=cost(3),
        name="chol_mid",
    )(part)


def chol_tail_kernel(a_ref, low_ref, pack_ref, u_ref, v_ref):
    below = lax.broadcasted_iota(jnp.int32, (32, 128), 0)

    def paired(x):
        return rows(x, pltpu.roll(x, 96, 1)).T[0:32]

    def gather(s):
        at = pl.ds(pl.multiple_of(s * 8, 8), 8)
        for g in range(8):
            u_ref[:, 8 * g : 8 * g + 8, :] = jnp.swapaxes(a_ref[8 * g : 8 * g + 8, at, :], 0, 1)

    def spread(ref, to, s):
        at = pl.ds(pl.multiple_of(s * 8, 8), 8)
        for g in range(4):
            to[8 * g : 8 * g + 8, at, :] = jnp.swapaxes(ref[:, 8 * g : 8 * g + 8, :], 0, 1)

    def upper(s, _):
        gather(s)
        for r in range(8):
            v_ref[r] = paired(u_ref[r])
        spread(v_ref, low_ref, s)
        return 0

    def lower(s, _):
        gather(s + 4)
        for r in range(8):
            v_ref[r] = paired(u_ref[r])
        spread(v_ref, low_ref, s + 4)
        for r in range(8):
            a = s * 8 + r
            free = jnp.where(below <= a, u_ref[r, 32:64, :], a_ref[a, 0:32, :])
            v_ref[r] = paired(rows(u_ref[r, 0:32, :], free))
        spread(v_ref, pack_ref, s)
        return 0

    lax.fori_loop(0, 4, upper, 0)
    lax.fori_loop(0, 4, lower, 0)
    diagonal = rows(*[a_ref[b, b : b + 1, :] for b in range(32)])
    pack_ref[32] = paired(rows(jnp.zeros((32, 128), F32), diagonal))


def chol_tail(part):
    return pl.pallas_call(
        chol_tail_kernel,
        out_shape=(
            jax.ShapeDtypeStruct((32, 64, 128), F32),
            jax.ShapeDtypeStruct((33, 32, 128), F32),
        ),
        in_specs=[VMEM],
        out_specs=(VMEM, VMEM),
        scratch_shapes=[
            pltpu.VMEM((8, 64, 128), F32),
            pltpu.VMEM((8, 32, 128), F32),
        ],
        compiler_params=params(10),
        cost_estimate=cost(5),
        name="chol_tail",
    )(part)


def half_kernel(c0_ref, c1_ref, low_ref, y_ref, s_ref, u_ref, part):
    step = pl.program_id(0)

    def turn(s, _):
        for r in range(8):
            u_ref[r] = rows(c0_ref[s * 8 + r], c1_ref[s * 8 + r]).T
        at = pl.ds(pl.multiple_of(step * 16 + s * 8, 8), 8)
        for g in range(16):
            s_ref[8 * g : 8 * g + 8, at, :] = jnp.swapaxes(u_ref[:, 8 * g : 8 * g + 8, :], 0, 1)
        return 0

    lax.fori_loop(0, 2, turn, 0)

    @pl.when(step == 3)
    def _():
        first = first_half((64, 256))

        def leaf(s, _):
            ts = [s * HALF + j for j in range(HALF)]
            lefts = []
            for t in ts:
                lh, ll = split(low_ref[16 * part + t])
                lefts.append(rows(lh, ll, lh).T)
            at = [(j, n) for j in range(HALF) for n in range(0, 8, 2)]
            zs = []
            for j, n in at:
                wh, wl = split(lanes(s_ref[ts[j] * 8 + n], s_ref[ts[j] * 8 + n + 1]))
                zs.append(mm(lefts[j], rows(wh, wh, wl)))
            for (j, n), z in zip(at, zs):
                yh, yl = split(jnp.where(first, z[0:64], z[64:128]))
                for m in range(2):
                    b = ts[j] * 8 + n + m
                    y_ref[b, :, 0:128] = yh[:, m * 128 : m * 128 + 128]
                    y_ref[b, :, 128:256] = yl[:, m * 128 : m * 128 + 128]
            return 0

        lax.fori_loop(0, 16 // HALF, leaf, 0)


def half_leaf(coupling, low, part):
    return pl.pallas_call(
        functools.partial(half_kernel, part=part),
        out_shape=jax.ShapeDtypeStruct((128, 64, 256), BF16),
        grid=(4,),
        in_specs=[
            pl.BlockSpec((16, 64, 128), lambda s: (s, 0, part)),
            pl.BlockSpec((16, 64, 128), lambda s: (s, 0, part + 2)),
            pl.BlockSpec((32, 64, 128), lambda s: (0, 0, 0)),
        ],
        out_specs=pl.BlockSpec((128, 64, 256), lambda s: (0, 0, 0)),
        scratch_shapes=[pltpu.VMEM((128, 64, 128), F32), pltpu.VMEM((8, 128, 128), F32)],
        compiler_params=params(22),
        cost_estimate=cost(6),
    )(coupling, coupling, low)


def prep_kernel(odd_ref, near_ref, own_ref, far_ref, d_ref):
    first = first_half()
    odd = odd_ref[0]

    def plain(q, _):
        x = own_ref[q]
        y = pltpu.roll(x, 64, 1)
        d_ref[64 + q] = right_of(jnp.where(first, x, y))
        d_ref[96 + q] = right_of(jnp.where(first, y, x))
        return 0

    lax.fori_loop(0, 32, plain, 0, unroll=8)
    half = first[0:32]
    row = lax.broadcasted_iota(jnp.int32, (32, 128), 0)
    col = lax.broadcasted_iota(jnp.int32, (32, 128), 1) % 64 - 32
    for base, ref in ((128 - 128 * odd, near_ref), (128 * odd, far_ref)):

        def packed(s, _, ref=ref, base=base):
            qs = [s * 4 + j for j in range(4)]
            ups = []
            for q in qs:
                diagonal = ref[32, pl.ds(q, 32, stride=0), :]
                rest = jnp.where(col == row, diagonal, 0.0)
                ups.append(jnp.where(col > row, ref[q], rest))
            turned = rows(*ups).T
            shifts = [
                [turned[64 * c + 32 : 64 * c + 64]]
                + [
                    pltpu.roll(turned[64 * c + 32 : 64 * c + 64], 32 * n, 1)
                    for n in range(1, 4)
                ]
                for c in range(2)
            ]
            for j, q in enumerate(qs):
                x = jnp.where(col <= row, ref[q], 0.0)
                y = pltpu.roll(x, 64, 1)
                for c in range(2):
                    at = shifts[c]
                    top = jnp.where(half, at[(4 - j) % 4], at[(6 - j) % 4])
                    top = jnp.where(col < 0, top, 0.0)
                    low = jnp.where(half, x, y) if c == 0 else jnp.where(half, y, x)
                    d_ref[base + 32 * c + q] = right_of(rows(top, low))
            return 0

        lax.fori_loop(0, 8, packed, 0, unroll=2)


def prep(odd, near, own, far):
    return pl.pallas_call(
        prep_kernel,
        out_shape=jax.ShapeDtypeStruct((192, 64, 256), BF16),
        in_specs=[SMEM] + [VMEM] * 3,
        out_specs=VMEM,
        compiler_params=params(16),
        cost_estimate=cost(3),
        name="prep",
    )(odd, near, own, far)


def full_kernel(cols_ref, y_ref, d_ref, *refs, part):
    out_ref, s_ref, u_ref, o_ref, sem = refs[-5:]
    lane = lax.broadcasted_iota(jnp.int32, (64, 256), 1)
    keep = ((lane % 128) < 64).astype(BF16)
    drop = ((lane % 128) >= 64).astype(BF16)

    def pair(s, _):
        ps = [s * PAIRS + j for j in range(PAIRS)]
        zs = []
        for p in ps:
            sa = cols_ref[part * 128 + p]
            sb = cols_ref[part * 128 + 256 + p]
            r = rows(d_ref[sa] * keep, d_ref[sb] * drop)
            y = y_ref[p]
            zs.append(mm(rows(y[:, 0:128], y[:, 128:256]), r))
        for p, z in zip(ps, zs):
            s_ref[p] = z[0:64, 0:128] + z[0:64, 128:256] + z[64:128, 0:128]
        return 0

    lax.fori_loop(0, 128 // PAIRS, pair, 0)

    def send(n):
        return [
            pltpu.make_async_copy(
                o_ref.at[c, pl.ds(16 * n, 16)],
                out_ref.at[pl.ds(16 * n, 16), :, pl.ds((part + 2 * c) * 128, 128)],
                sem.at[n, c],
            )
            for c in range(2)
        ]

    def turn(s, _):
        at = pl.ds(pl.multiple_of(s * 8, 8), 8)
        for g in range(16):
            u_ref[:, 8 * g : 8 * g + 8, :] = jnp.swapaxes(s_ref[8 * g : 8 * g + 8, at, :], 0, 1)
        for r in range(8):
            x = u_ref[r].T
            o_ref[0, s * 8 + r] = x[0:64]
            o_ref[1, s * 8 + r] = x[64:128]
        return 0

    for n in range(4):
        lax.fori_loop(2 * n, 2 * n + 2, turn, 0)
        for copy in send(n):
            copy.start()
    for n in range(4):
        for copy in send(n):
            copy.wait()


def full_leaf(cols, y, d, part, into=None):
    extra = [] if into is None else [into]
    return pl.pallas_call(
        functools.partial(full_kernel, part=part),
        out_shape=jax.ShapeDtypeStruct((64, 64, 512), F32),
        in_specs=[SMEM, VMEM, VMEM] + [pl.BlockSpec(memory_space=pltpu.HBM)] * len(extra),
        out_specs=pl.BlockSpec(memory_space=pltpu.HBM),
        scratch_shapes=[
            pltpu.VMEM((128, 64, 128), F32),
            pltpu.VMEM((8, 128, 128), F32),
            pltpu.VMEM((2, 64, 64, 128), F32),
            pltpu.SemaphoreType.DMA((4, 2)),
        ],
        input_output_aliases={} if into is None else {3: 0},
        compiler_params=params(22),
        cost_estimate=cost(8),
    )(cols, y, d, *extra)


def branch_kernel(at_ref, p0, p1, p2, p3, p4, top_ref, gf_ref, low_ref, t_ref, e_ref, n_ref, a_ref):
    at = at_ref[0]
    pick = at_ref[1]
    first = first_half()

    def place(n, x):
        y = pltpu.roll(x, 64, 1)
        t_ref[n] = jnp.where(first, x, y)
        e_ref[n] = jnp.where(first, y, x)

    place(at, p0[...])
    place(at ^ 1, p1[...])
    near = (0, 1, 3, 2)
    for i in range(2):
        place(at ^ near[2 + i], p2[i])
    for i in range(4):
        place(at ^ 4 ^ near[i], p3[i])
    for i in range(8):
        place(at ^ (12, 8)[i // 4] ^ near[i % 4], p4[i])
    n_ref[0] = top_ref[...]
    for m in range(8):
        n_ref[8 + m] = t_ref[2 * m] + t_ref[2 * m + 1]
    ups = {}
    for p in range(2, 16):
        h, l = split(e_ref[p])
        ups[p] = rows(h, l).T[0:64]
    for level in (2, 1, 0):
        parents = range(2**level, 2 ** (level + 1))
        children = [c for p in parents for c in (2 * p, 2 * p + 1)]
        prods = []
        for c in children:
            h, l = split(e_ref[c])
            prods.append(mm(left_of(n_ref[c]), rows(h, h, l, l)))
        terms = []
        for c, prod in zip(children, prods):
            h, l = split(prod)
            terms.append(mm(lanes(ups[c], ups[c]), rows(h, h, l, l)))
        for n, p in enumerate(parents):
            n_ref[p] = terms[2 * n] + terms[2 * n + 1]

    both = jnp.where(first, n_ref[pick], n_ref[1])
    lane = lax.broadcasted_iota(jnp.int32, (64, 128), 1)

    def load(k, _):
        a_ref[k] = jnp.take_along_axis(both, (lane & 64) + k, axis=1)
        return 0

    lax.fori_loop(0, 64, load, 0, unroll=8)
    chol_lanes(a_ref)

    def store(k, out):
        return jnp.where((lane & 63) == k, a_ref[k], out)

    out = lax.fori_loop(0, 64, store, jnp.zeros((64, 128), F32), unroll=8)
    gf_ref[0] = out.T[0:64]
    low_ref[...] = jnp.where(first, pltpu.roll(out, 64, 1), out)


def branch(at, parts, top):
    return pl.pallas_call(
        branch_kernel,
        out_shape=(
            jax.ShapeDtypeStruct((1, 64, 64), F32),
            jax.ShapeDtypeStruct((64, 128), F32),
        ),
        in_specs=[SMEM] + [VMEM] * 6,
        out_specs=(VMEM, VMEM),
        scratch_shapes=[
            pltpu.VMEM((16, 64, 128), F32),
            pltpu.VMEM((16, 64, 128), F32),
            pltpu.VMEM((16, 64, 128), F32),
            pltpu.VMEM((64, 64, 128), F32),
        ],
        compiler_params=params(8),
        cost_estimate=cost(5),
        name="branch",
    )(at, *parts, top)


def far_kernel(cols_ref, f_ref, l0, l1, l2, l3, o_ref, l_ref, c_ref):
    for s, part in enumerate((l0[...], l1[...], l2[0], l2[1], l3[2], l3[3], l3[0], l3[1])):
        h, l = split(part[:, 0:64])
        l_ref[s] = rows(h, h, l)
    lh, ll = split(l0[...].T[0:64])
    left = lanes(lh, ll, lh)
    halves = []
    for g in range(2):
        for s in range(8):
            x = f_ref[8 * s : 8 * s + 8, 8 * g : 8 * g + 8, :]
            c_ref[8 * g : 8 * g + 8, 8 * s : 8 * s + 8, :] = jnp.swapaxes(x, 0, 1)
        for f in range(8 * g, 8 * g + 8):
            ch, cl = split(c_ref[f])
            halves.append(mm(left, rows(ch, ch, cl)))
    outs = []
    for f in range(16):
        hh, hl = split(halves[f])
        outs.append(mm(lanes(hh, hl, hh), l_ref[cols_ref[f]]))
    for f in range(16):
        c_ref[f] = outs[f]
    for g in range(2):
        for s in range(8):
            x = c_ref[8 * g : 8 * g + 8, 8 * s : 8 * s + 8, :]
            o_ref[8 * s : 8 * s + 8, 8 * g : 8 * g + 8, :] = jnp.swapaxes(x, 0, 1)


def far(cols, coupling, lowers):
    return pl.pallas_call(
        far_kernel,
        out_shape=jax.ShapeDtypeStruct(coupling.shape, F32),
        in_specs=[SMEM] + [VMEM] * 5,
        out_specs=VMEM,
        scratch_shapes=[pltpu.VMEM((8, 192, 64), BF16), pltpu.VMEM((16, 64, 64), F32)],
        compiler_params=params(6),
        cost_estimate=cost(3),
        name="far",
    )(cols, coupling, *lowers)


def shifted(value, axis, to):
    return lax.ppermute(value, axis, [(i, to(i)) for i in range(lax.axis_size(axis))])


def steps(
    basis_t, nested_transfer_matrices, leaf_coupling, leaf_columns, far_coupling, far_columns
):
    basis_t, nested_transfer_matrices, leaf_coupling = (
        pltpu.with_memory_space_constraint(x, pltpu.HBM)
        for x in (basis_t, nested_transfer_matrices, leaf_coupling)
    )
    both = ("wide", "narrow")
    wide_at = lax.axis_index("wide")
    at = lax.axis_index("narrow")
    gram, top, pay = climb(basis_t, nested_transfer_matrices)
    pay_a = shifted(pay, "narrow", lambda i: i ^ 1)
    head = chol_head(gram)
    pair = jnp.stack([pay, pay_a])
    pay_b = shifted(pair, "narrow", lambda i: i ^ 3)
    mid = chol_mid(head)
    quad = jnp.concatenate([pair, pay_b])
    pay_c = shifted(quad, "narrow", lambda i: i ^ 4)
    low, pack = chol_tail(mid)
    octet = jnp.concatenate([quad, pay_c])
    pay_d = shifted(octet, "narrow", lambda i: i ^ 12)
    count = lax.axis_size(both)
    low_near = lax.ppermute(pack, both, [(i, i ^ 1) for i in range(count)])
    later = [(i, i + 1) for i in range(1, count - 1, 2)]
    low_far = lax.ppermute(pack, both, later + [(j, i) for i, j in later])
    half_a = half_leaf(leaf_coupling, low, 0)
    half_b = half_leaf(leaf_coupling, low, 1)
    ones = 1 + sum((at % 2**k == 2**k - 1).astype(jnp.int32) for k in range(1, 5))
    pick = jnp.where(ones <= 4, (16 + at) >> ones, 0)
    place = jnp.stack([at, pick]).astype(jnp.int32)
    group_factors, own = branch(place, [pay, pay_a, pay_b, pay_c, pay_d], top)
    own_a = shifted(own, "wide", lambda i: i ^ 1)
    factors = prep(at.reshape(1) % 2, low_near, low, low_far)
    two = jnp.stack([own, own_a])
    own_b = shifted(two, "wide", lambda i: i ^ 2)
    cols = leaf_columns - (lax.axis_index(both) * 64 - 64)
    out = full_leaf(cols, half_a, factors, 0)
    four = jnp.concatenate([two, own_b])
    own_c = shifted(four, "wide", lambda i: i ^ 6)
    leaf_coupled = full_leaf(cols, half_b, factors, 1, out)
    far_out = far(
        wide_at ^ far_columns,
        jnp.transpose(far_coupling, (0, 2, 1)),
        [own, own_a, own_b, own_c],
    )
    return leaf_coupled, jnp.transpose(far_out, (0, 2, 1)), group_factors


def solution(mesh):
    spread = P(None, None, ("wide", "narrow"))
    split_first = P(("wide", "narrow"), None, None)
    ids = P(("wide", "narrow"))
    return jax.shard_map(
        steps,
        mesh=mesh,
        in_specs=(split_first, spread, spread, ids, spread, ids),
        out_specs=(spread, spread, split_first),
        check_vma=False,
    )
```

```python
import functools

import jax
import jax.numpy as jnp
from jax import lax
from jax.experimental import pallas as pl
from jax.experimental.pallas import tpu as pltpu
from jax.sharding import PartitionSpec as P

F32 = jnp.float32
BF16 = jnp.bfloat16
ANY = pl.BlockSpec(memory_space=pl.ANY)
VMEM = pl.BlockSpec(memory_space=pltpu.VMEM)
SMEM = pl.BlockSpec(memory_space=pltpu.SMEM)


def params(mib):
    return pltpu.CompilerParams(vmem_limit_bytes=mib * 2**20)


def cost(us):
    return pl.CostEstimate(flops=int(us * 1.15e9), bytes_accessed=4096, transcendentals=0)


def split(x):
    hi = x.astype(BF16)
    lo = (x - hi.astype(F32)).astype(BF16)
    return hi, lo


def mm(a, b):
    return lax.dot_general(a, b, (((1,), (0,)), ((), ())), preferred_element_type=F32)


def mm_nt(a, b):
    return lax.dot_general(a, b, (((1,), (1,)), ((), ())), preferred_element_type=F32)


def mm_tn(a, b):
    return lax.dot_general(a, b, (((0,), (0,)), ((), ())), preferred_element_type=F32)


def lanes(*parts):
    return jnp.concatenate(parts, axis=1)


def rows(*parts):
    return jnp.concatenate(parts, axis=0)


def first_half(shape=(64, 128)):
    return lax.broadcasted_iota(jnp.int32, shape, 1) % 128 < 64


def mixed(m):
    h = m.astype(BF16).astype(F32)
    return jnp.where(first_half(m.shape), h, m - h).astype(BF16)


def left_of(m):
    v = mixed(m)
    return lanes(v, v)


def right_of(m):
    return lanes(*split(m))


def twice(m):
    return rows(m, m)


LEAVES = 32
HALF = 8
PAIRS = 64


def climb_kernel(
    b_hbm, t_hbm, g_ref, top_ref, pay_ref, b_ref, t_ref, u_ref, e_ref, w_ref, sem
):
    t_copies = [
        pltpu.make_async_copy(
            t_hbm.at[pl.ds(16 * n, 16)], t_ref.at[pl.ds(16 * n, 16)], sem.at[n]
        )
        for n in range(4)
    ]
    b_copies = [
        pltpu.make_async_copy(
            b_hbm.at[pl.ds(32 * n, 32)], b_ref.at[pl.ds(32 * n, 32)], sem.at[4 + n]
        )
        for n in range(2)
    ]
    for copy in t_copies + b_copies:
        copy.start()
    first = first_half()

    def turn(s, _):
        for r in range(8):
            x = t_ref[s * 8 + r]
            u_ref[r] = rows(x, x).T
        for g in range(16):
            x = u_ref[:, 8 * g : 8 * g + 8, :]
            e_ref[8 * g : 8 * g + 8, pl.ds(pl.multiple_of(s * 8, 8), 8), :] = jnp.swapaxes(x, 0, 1)
        return 0

    for n in range(4):
        t_copies[n].wait()
        lax.fori_loop(2 * n, 2 * n + 2, turn, 0)

    row = lax.broadcasted_iota(jnp.int32, (64, 128), 0)
    col = lax.broadcasted_iota(jnp.int32, (64, 128), 1)
    w_ref[1, 0:64] = (row == col % 64).astype(BF16)
    w_ref[1, 64:128] = jnp.zeros((64, 128), BF16)

    def right_rows(h):
        w = w_ref[h]
        return rows(w[0:64], w[0:64], w[64:128], w[64:128])

    def down(clusters):
        zs = [
            mm(rows(left_of(e_ref[2 * p]), left_of(e_ref[2 * p + 1])), right_rows(p))
            for p in clusters
        ]
        for p, z in zip(clusters, zs):
            for c in range(2):
                w_ref[2 * p + c] = rows(*split(z[64 * c : 64 * c + 64]))

    def downs(s, _):
        down([s * 8 + j for j in range(8)])
        return 0

    for level in range(3):
        down(range(2**level, 2 ** (level + 1)))
    for level in range(3, 6):
        n = 2**level
        lax.fori_loop(n // 8, n // 4, downs, 0)
    for copy in b_copies:
        copy.wait()

    def leaves(s, acc):
        count = LEAVES // 2
        qs = [s * count + j for j in range(count)]
        ts = qs + [q + 32 for q in qs]
        bs = [b_ref[t] for t in ts]
        grams = [mm_nt(b, twice(b)) for b in bs]
        for j, q in enumerate(qs):
            g_ref[q] = jnp.where(first, grams[j], grams[count + j])
        prods = [mm(left_of(g), right_rows(64 + t)) for g, t in zip(grams, ts)]
        for p, t in zip(prods, ts):
            ph, pl_ = split(p)
            w = w_ref[64 + t][:, 0:64]
            acc = acc + mm_tn(rows(w, w), rows(ph, ph, pl_, pl_))
        return acc

    top = lax.fori_loop(0, 64 // LEAVES, leaves, jnp.zeros((64, 128), F32))
    top_ref[...] = top
    h, l = split(e_ref[1])
    prod = mm(left_of(top), rows(h, h, l, l))
    ph, pl_ = split(prod)
    up = rows(h, l).T[0:64]
    term = mm(lanes(up, up), rows(ph, ph, pl_, pl_))
    pay_ref[...] = jnp.where(first, term, e_ref[0])


def climb(basis, transfers):
    return pl.pallas_call(
        climb_kernel,
        out_shape=(
            jax.ShapeDtypeStruct((32, 64, 128), F32),
            jax.ShapeDtypeStruct((64, 128), F32),
            jax.ShapeDtypeStruct((64, 128), F32),
        ),
        in_specs=[pl.BlockSpec(memory_space=pltpu.HBM)] * 2,
        out_specs=(VMEM,) * 3,
        scratch_shapes=[
            pltpu.VMEM((64, 64, 256), BF16),
            pltpu.VMEM((64, 64, 128), F32),
            pltpu.VMEM((8, 128, 128), F32),
            pltpu.VMEM((128, 64, 128), F32),
            pltpu.VMEM((128, 128, 128), BF16),
            pltpu.SemaphoreType.DMA((6,)),
        ],
        compiler_params=params(20),
        cost_estimate=cost(10),
        name="climb",
    )(basis, transfers)


def chol_lanes(a_ref, panels=range(8), count=64, panel=8):
    sub = lax.broadcasted_iota(jnp.int32, (8, 128), 0)
    for p in panels:
        base = p * panel
        if p > 0:
            for it in range(p, count // 8):

                def body(k, accs):
                    lv = a_ref[k, it * 8 : it * 8 + 8, :]
                    return tuple(
                        accs[j] - lv * a_ref[k, pl.ds(base + j, 8, stride=0), :]
                        for j in range(panel)
                    )

                accs = tuple(
                    a_ref[base + j, it * 8 : it * 8 + 8, :] for j in range(panel)
                )
                accs = lax.fori_loop(0, base, body, accs, unroll=8)
                for j in range(panel):
                    a_ref[base + j, it * 8 : it * 8 + 8, :] = accs[j]
        d = [a_ref[base + j, base : base + 8, :] for j in range(8)]
        invs = []
        for j in range(8):
            piv = jnp.broadcast_to(d[j][j : j + 1, :], (8, 128))
            inv = lax.rsqrt(piv)
            invs.append(inv)
            d[j] = jnp.where(sub >= j, d[j] * inv, 0.0)
            for m in range(j + 1, 8):
                d[m] = d[m] - d[j] * jnp.broadcast_to(d[j][m : m + 1, :], (8, 128))
            a_ref[base + j, base : base + 8, :] = d[j]
            if base > 0:
                a_ref[base + j, 0:base, :] = jnp.zeros((base, 128), F32)
        bc = {}
        for j in range(8):
            for m in range(j + 1, 8):
                bc[j, m] = jnp.broadcast_to(d[j][m : m + 1, :], (8, 128))
        for it in range(p + 1, count // 8):
            v = [a_ref[base + j, it * 8 : it * 8 + 8, :] for j in range(8)]
            for j in range(8):
                v[j] = v[j] * invs[j]
                for m in range(j + 1, 8):
                    v[m] = v[m] - v[j] * bc[j, m]
                a_ref[base + j, it * 8 : it * 8 + 8, :] = v[j]


EARLY = 2


def chol_head_kernel(g_ref, a_ref, u_ref):
    def load(s, _):
        at = pl.ds(pl.multiple_of(s * 8, 8), 8)
        for g in range(4):
            u_ref[:, 8 * g : 8 * g + 8, :] = jnp.swapaxes(g_ref[8 * g : 8 * g + 8, at, :], 0, 1)
        for r in range(8):
            x = u_ref[r, 0:32, :]
            y = pltpu.roll(x, 64, 1)
            a_ref[s * 8 + r] = rows(x, y, x, y).T[0:64]
        return 0

    lax.fori_loop(0, 8, load, 0)
    chol_lanes(a_ref, range(EARLY))


def chol_head(gram):
    return pl.pallas_call(
        chol_head_kernel,
        out_shape=jax.ShapeDtypeStruct((64, 64, 128), F32),
        in_specs=[VMEM],
        out_specs=VMEM,
        scratch_shapes=[pltpu.VMEM((8, 64, 128), F32)],
        compiler_params=params(8),
        cost_estimate=cost(4),
        name="chol_head",
    )(gram)


def chol_mid_kernel(i_ref, a_ref):
    a_ref[...] = i_ref[...]
    chol_lanes(a_ref, range(EARLY, 8))


def chol_mid(part):
    return pl.pallas_call(
        chol_mid_kernel,
        out_shape=jax.ShapeDtypeStruct((64, 64, 128), F32),
        in_specs=[VMEM],
        out_specs=VMEM,
        compiler_params=params(8),
        cost_estimate=cost(3),
        name="chol_mid",
    )(part)


def chol_tail_kernel(a_ref, low_ref, pack_ref, u_ref, v_ref):
    below = lax.broadcasted_iota(jnp.int32, (32, 128), 0)

    def paired(x):
        return rows(x, pltpu.roll(x, 96, 1)).T[0:32]

    def gather(s):
        at = pl.ds(pl.multiple_of(s * 8, 8), 8)
        for g in range(8):
            u_ref[:, 8 * g : 8 * g + 8, :] = jnp.swapaxes(a_ref[8 * g : 8 * g + 8, at, :], 0, 1)

    def spread(ref, to, s):
        at = pl.ds(pl.multiple_of(s * 8, 8), 8)
        for g in range(4):
            to[8 * g : 8 * g + 8, at, :] = jnp.swapaxes(ref[:, 8 * g : 8 * g + 8, :], 0, 1)

    def upper(s, _):
        gather(s)
        for r in range(8):
            v_ref[r] = paired(u_ref[r])
        spread(v_ref, low_ref, s)
        return 0

    def lower(s, _):
        gather(s + 4)
        for r in range(8):
            v_ref[r] = paired(u_ref[r])
        spread(v_ref, low_ref, s + 4)
        for r in range(8):
            a = s * 8 + r
            free = jnp.where(below <= a, u_ref[r, 32:64, :], a_ref[a, 0:32, :])
            v_ref[r] = paired(rows(u_ref[r, 0:32, :], free))
        spread(v_ref, pack_ref, s)
        return 0

    lax.fori_loop(0, 4, upper, 0)
    lax.fori_loop(0, 4, lower, 0)
    diagonal = rows(*[a_ref[b, b : b + 1, :] for b in range(32)])
    pack_ref[32] = paired(rows(jnp.zeros((32, 128), F32), diagonal))


def chol_tail(part):
    return pl.pallas_call(
        chol_tail_kernel,
        out_shape=(
            jax.ShapeDtypeStruct((32, 64, 128), F32),
            jax.ShapeDtypeStruct((33, 32, 128), F32),
        ),
        in_specs=[VMEM],
        out_specs=(VMEM, VMEM),
        scratch_shapes=[
            pltpu.VMEM((8, 64, 128), F32),
            pltpu.VMEM((8, 32, 128), F32),
        ],
        compiler_params=params(10),
        cost_estimate=cost(5),
        name="chol_tail",
    )(part)


def half_kernel(c_hbm, low_ref, y_ref, c_ref, s_ref, u_ref, sem, part):
    copies = [
        [
            pltpu.make_async_copy(
                c_hbm.at[pl.ds(16 * n, 16), :, pl.ds((part + 2 * c) * 128, 128)],
                c_ref.at[c, pl.ds(16 * n, 16)],
                sem.at[n, c],
            )
            for c in range(2)
        ]
        for n in range(4)
    ]
    for group in copies:
        for copy in group:
            copy.start()

    def turn(s, _):
        for r in range(8):
            u_ref[r] = rows(c_ref[0, s * 8 + r], c_ref[1, s * 8 + r]).T
        at = pl.ds(pl.multiple_of(s * 8, 8), 8)
        for g in range(16):
            s_ref[8 * g : 8 * g + 8, at, :] = jnp.swapaxes(u_ref[:, 8 * g : 8 * g + 8, :], 0, 1)
        return 0

    for n in range(4):
        for copy in copies[n]:
            copy.wait()
        lax.fori_loop(2 * n, 2 * n + 2, turn, 0)
    first = first_half((64, 256))

    def leaf(s, _):
        ts = [s * HALF + j for j in range(HALF)]
        lefts = []
        for t in ts:
            lh, ll = split(low_ref[16 * part + t])
            lefts.append(rows(lh, ll, lh).T)
        at = [(j, n) for j in range(HALF) for n in range(0, 8, 2)]
        zs = []
        for j, n in at:
            wh, wl = split(lanes(s_ref[ts[j] * 8 + n], s_ref[ts[j] * 8 + n + 1]))
            zs.append(mm(lefts[j], rows(wh, wh, wl)))
        for (j, n), z in zip(at, zs):
            yh, yl = split(jnp.where(first, z[0:64], z[64:128]))
            for m in range(2):
                b = ts[j] * 8 + n + m
                y_ref[b, :, 0:128] = yh[:, m * 128 : m * 128 + 128]
                y_ref[b, :, 128:256] = yl[:, m * 128 : m * 128 + 128]
        return 0

    lax.fori_loop(0, 16 // HALF, leaf, 0)


def half_leaf(coupling, low, part):
    return pl.pallas_call(
        functools.partial(half_kernel, part=part),
        out_shape=jax.ShapeDtypeStruct((128, 64, 256), BF16),
        in_specs=[pl.BlockSpec(memory_space=pltpu.HBM), VMEM],
        out_specs=VMEM,
        scratch_shapes=[
            pltpu.VMEM((2, 64, 64, 128), F32),
            pltpu.VMEM((128, 64, 128), F32),
            pltpu.VMEM((8, 128, 128), F32),
            pltpu.SemaphoreType.DMA((4, 2)),
        ],
        compiler_params=params(18),
        cost_estimate=cost(6),
    )(coupling, low)


def prep_kernel(odd_ref, near_ref, own_ref, far_ref, d_ref):
    first = first_half()
    odd = odd_ref[0]

    def plain(q, _):
        x = own_ref[q]
        y = pltpu.roll(x, 64, 1)
        d_ref[64 + q] = right_of(jnp.where(first, x, y))
        d_ref[96 + q] = right_of(jnp.where(first, y, x))
        return 0

    lax.fori_loop(0, 32, plain, 0, unroll=8)
    half = first[0:32]
    row = lax.broadcasted_iota(jnp.int32, (32, 128), 0)
    col = lax.broadcasted_iota(jnp.int32, (32, 128), 1) % 64 - 32
    for base, ref in ((128 - 128 * odd, near_ref), (128 * odd, far_ref)):

        def packed(s, _, ref=ref, base=base):
            qs = [s * 4 + j for j in range(4)]
            ups = []
            for q in qs:
                diagonal = ref[32, pl.ds(q, 32, stride=0), :]
                rest = jnp.where(col == row, diagonal, 0.0)
                ups.append(jnp.where(col > row, ref[q], rest))
            turned = rows(*ups).T
            shifts = [
                [turned[64 * c + 32 : 64 * c + 64]]
                + [
                    pltpu.roll(turned[64 * c + 32 : 64 * c + 64], 32 * n, 1)
                    for n in range(1, 4)
                ]
                for c in range(2)
            ]
            for j, q in enumerate(qs):
                x = jnp.where(col <= row, ref[q], 0.0)
                y = pltpu.roll(x, 64, 1)
                for c in range(2):
                    at = shifts[c]
                    top = jnp.where(half, at[(4 - j) % 4], at[(6 - j) % 4])
                    top = jnp.where(col < 0, top, 0.0)
                    low = jnp.where(half, x, y) if c == 0 else jnp.where(half, y, x)
                    d_ref[base + 32 * c + q] = right_of(rows(top, low))
            return 0

        lax.fori_loop(0, 8, packed, 0, unroll=2)


def prep(odd, near, own, far):
    return pl.pallas_call(
        prep_kernel,
        out_shape=jax.ShapeDtypeStruct((192, 64, 256), BF16),
        in_specs=[SMEM] + [VMEM] * 3,
        out_specs=VMEM,
        compiler_params=params(16),
        cost_estimate=cost(3),
        name="prep",
    )(odd, near, own, far)


def full_kernel(cols_ref, y_ref, d_ref, *refs, part):
    out_ref, s_ref, u_ref, o_ref, sem = refs[-5:]
    lane = lax.broadcasted_iota(jnp.int32, (64, 256), 1)
    keep = ((lane % 128) < 64).astype(BF16)
    drop = ((lane % 128) >= 64).astype(BF16)

    def pair(s, _):
        ps = [s * PAIRS + j for j in range(PAIRS)]
        zs = []
        for p in ps:
            sa = cols_ref[part * 128 + p]
            sb = cols_ref[part * 128 + 256 + p]
            r = rows(d_ref[sa] * keep, d_ref[sb] * drop)
            y = y_ref[p]
            zs.append(mm(rows(y[:, 0:128], y[:, 128:256]), r))
        for p, z in zip(ps, zs):
            s_ref[p] = z[0:64, 0:128] + z[0:64, 128:256] + z[64:128, 0:128]
        return 0

    lax.fori_loop(0, 128 // PAIRS, pair, 0)

    def send(n):
        return [
            pltpu.make_async_copy(
                o_ref.at[c, pl.ds(16 * n, 16)],
                out_ref.at[pl.ds(16 * n, 16), :, pl.ds((part + 2 * c) * 128, 128)],
                sem.at[n, c],
            )
            for c in range(2)
        ]

    def turn(s, _):
        at = pl.ds(pl.multiple_of(s * 8, 8), 8)
        for g in range(16):
            u_ref[:, 8 * g : 8 * g + 8, :] = jnp.swapaxes(s_ref[8 * g : 8 * g + 8, at, :], 0, 1)
        for r in range(8):
            x = u_ref[r].T
            o_ref[0, s * 8 + r] = x[0:64]
            o_ref[1, s * 8 + r] = x[64:128]
        return 0

    for n in range(4):
        lax.fori_loop(2 * n, 2 * n + 2, turn, 0)
        for copy in send(n):
            copy.start()
    for n in range(4):
        for copy in send(n):
            copy.wait()


def full_leaf(cols, y, d, part, into=None):
    extra = [] if into is None else [into]
    return pl.pallas_call(
        functools.partial(full_kernel, part=part),
        out_shape=jax.ShapeDtypeStruct((64, 64, 512), F32),
        in_specs=[SMEM, VMEM, VMEM] + [pl.BlockSpec(memory_space=pltpu.HBM)] * len(extra),
        out_specs=pl.BlockSpec(memory_space=pltpu.HBM),
        scratch_shapes=[
            pltpu.VMEM((128, 64, 128), F32),
            pltpu.VMEM((8, 128, 128), F32),
            pltpu.VMEM((2, 64, 64, 128), F32),
            pltpu.SemaphoreType.DMA((4, 2)),
        ],
        input_output_aliases={} if into is None else {3: 0},
        compiler_params=params(22),
        cost_estimate=cost(8),
    )(cols, y, d, *extra)


def branch_kernel(at_ref, p0, p1, p2, p3, p4, top_ref, gf_ref, low_ref, t_ref, e_ref, n_ref, a_ref):
    at = at_ref[0]
    pick = at_ref[1]
    first = first_half()

    def place(n, x):
        y = pltpu.roll(x, 64, 1)
        t_ref[n] = jnp.where(first, x, y)
        e_ref[n] = jnp.where(first, y, x)

    place(at, p0[...])
    place(at ^ 1, p1[...])
    near = (0, 1, 3, 2)
    for i in range(2):
        place(at ^ near[2 + i], p2[i])
    for i in range(4):
        place(at ^ 4 ^ near[i], p3[i])
    for i in range(8):
        place(at ^ (12, 8)[i // 4] ^ near[i % 4], p4[i])
    n_ref[0] = top_ref[...]
    for m in range(8):
        n_ref[8 + m] = t_ref[2 * m] + t_ref[2 * m + 1]
    ups = {}
    for p in range(2, 16):
        h, l = split(e_ref[p])
        ups[p] = rows(h, l).T[0:64]
    for level in (2, 1, 0):
        parents = range(2**level, 2 ** (level + 1))
        children = [c for p in parents for c in (2 * p, 2 * p + 1)]
        prods = []
        for c in children:
            h, l = split(e_ref[c])
            prods.append(mm(left_of(n_ref[c]), rows(h, h, l, l)))
        terms = []
        for c, prod in zip(children, prods):
            h, l = split(prod)
            terms.append(mm(lanes(ups[c], ups[c]), rows(h, h, l, l)))
        for n, p in enumerate(parents):
            n_ref[p] = terms[2 * n] + terms[2 * n + 1]

    both = jnp.where(first, n_ref[pick], n_ref[1])
    lane = lax.broadcasted_iota(jnp.int32, (64, 128), 1)

    def load(k, _):
        a_ref[k] = jnp.take_along_axis(both, (lane & 64) + k, axis=1)
        return 0

    lax.fori_loop(0, 64, load, 0, unroll=8)
    chol_lanes(a_ref)

    def store(k, out):
        return jnp.where((lane & 63) == k, a_ref[k], out)

    out = lax.fori_loop(0, 64, store, jnp.zeros((64, 128), F32), unroll=8)
    gf_ref[0] = out.T[0:64]
    low_ref[...] = jnp.where(first, pltpu.roll(out, 64, 1), out)


def branch(at, parts, top):
    return pl.pallas_call(
        branch_kernel,
        out_shape=(
            jax.ShapeDtypeStruct((1, 64, 64), F32),
            jax.ShapeDtypeStruct((64, 128), F32),
        ),
        in_specs=[SMEM] + [VMEM] * 6,
        out_specs=(VMEM, VMEM),
        scratch_shapes=[
            pltpu.VMEM((16, 64, 128), F32),
            pltpu.VMEM((16, 64, 128), F32),
            pltpu.VMEM((16, 64, 128), F32),
            pltpu.VMEM((64, 64, 128), F32),
        ],
        compiler_params=params(8),
        cost_estimate=cost(5),
        name="branch",
    )(at, *parts, top)


def far_kernel(cols_ref, f_ref, l0, l1, l2, l3, o_ref, l_ref, c_ref):
    for s, part in enumerate((l0[...], l1[...], l2[0], l2[1], l3[2], l3[3], l3[0], l3[1])):
        h, l = split(part[:, 0:64])
        l_ref[s] = rows(h, h, l)
    lh, ll = split(l0[...].T[0:64])
    left = lanes(lh, ll, lh)
    halves = []
    for g in range(2):
        for s in range(8):
            x = f_ref[8 * s : 8 * s + 8, 8 * g : 8 * g + 8, :]
            c_ref[8 * g : 8 * g + 8, 8 * s : 8 * s + 8, :] = jnp.swapaxes(x, 0, 1)
        for f in range(8 * g, 8 * g + 8):
            ch, cl = split(c_ref[f])
            halves.append(mm(left, rows(ch, ch, cl)))
    outs = []
    for f in range(16):
        hh, hl = split(halves[f])
        outs.append(mm(lanes(hh, hl, hh), l_ref[cols_ref[f]]))
    for f in range(16):
        c_ref[f] = outs[f]
    for g in range(2):
        for s in range(8):
            x = c_ref[8 * g : 8 * g + 8, 8 * s : 8 * s + 8, :]
            o_ref[8 * s : 8 * s + 8, 8 * g : 8 * g + 8, :] = jnp.swapaxes(x, 0, 1)


def far(cols, coupling, lowers):
    return pl.pallas_call(
        far_kernel,
        out_shape=jax.ShapeDtypeStruct(coupling.shape, F32),
        in_specs=[SMEM] + [VMEM] * 5,
        out_specs=VMEM,
        scratch_shapes=[pltpu.VMEM((8, 192, 64), BF16), pltpu.VMEM((16, 64, 64), F32)],
        compiler_params=params(6),
        cost_estimate=cost(3),
        name="far",
    )(cols, coupling, *lowers)


def shifted(value, axis, to):
    return lax.ppermute(value, axis, [(i, to(i)) for i in range(lax.axis_size(axis))])


def steps(
    basis_t, nested_transfer_matrices, leaf_coupling, leaf_columns, far_coupling, far_columns
):
    basis_t, nested_transfer_matrices, leaf_coupling = (
        pltpu.with_memory_space_constraint(x, pltpu.HBM)
        for x in (basis_t, nested_transfer_matrices, leaf_coupling)
    )
    both = ("wide", "narrow")
    wide_at = lax.axis_index("wide")
    at = lax.axis_index("narrow")
    gram, top, pay = climb(basis_t, nested_transfer_matrices)
    pay_a = shifted(pay, "narrow", lambda i: i ^ 1)
    head = chol_head(gram)
    pair = jnp.stack([pay, pay_a])
    pay_b = shifted(pair, "narrow", lambda i: i ^ 3)
    mid = chol_mid(head)
    quad = jnp.concatenate([pair, pay_b])
    pay_c = shifted(quad, "narrow", lambda i: i ^ 4)
    low, pack = chol_tail(mid)
    octet = jnp.concatenate([quad, pay_c])
    pay_d = shifted(octet, "narrow", lambda i: i ^ 12)
    count = lax.axis_size(both)
    low_near = lax.ppermute(pack, both, [(i, i ^ 1) for i in range(count)])
    later = [(i, i + 1) for i in range(1, count - 1, 2)]
    low_far = lax.ppermute(pack, both, later + [(j, i) for i, j in later])
    half_a = half_leaf(leaf_coupling, low, 0)
    half_b = half_leaf(leaf_coupling, low, 1)
    ones = 1 + sum((at % 2**k == 2**k - 1).astype(jnp.int32) for k in range(1, 5))
    pick = jnp.where(ones <= 4, (16 + at) >> ones, 0)
    place = jnp.stack([at, pick]).astype(jnp.int32)
    group_factors, own = branch(place, [pay, pay_a, pay_b, pay_c, pay_d], top)
    own_a = shifted(own, "wide", lambda i: i ^ 1)
    factors = prep(at.reshape(1) % 2, low_near, low, low_far)
    two = jnp.stack([own, own_a])
    own_b = shifted(two, "wide", lambda i: i ^ 2)
    cols = leaf_columns - (lax.axis_index(both) * 64 - 64)
    out = full_leaf(cols, half_a, factors, 0)
    four = jnp.concatenate([two, own_b])
    own_c = shifted(four, "wide", lambda i: i ^ 6)
    leaf_coupled = full_leaf(cols, half_b, factors, 1, out)
    far_out = far(
        wide_at ^ far_columns,
        jnp.transpose(far_coupling, (0, 2, 1)),
        [own, own_a, own_b, own_c],
    )
    return leaf_coupled, jnp.transpose(far_out, (0, 2, 1)), group_factors


def solution(mesh):
    spread = P(None, None, ("wide", "narrow"))
    split_first = P(("wide", "narrow"), None, None)
    ids = P(("wide", "narrow"))
    return jax.shard_map(
        steps,
        mesh=mesh,
        in_specs=(split_first, spread, spread, ids, spread, ids),
        out_specs=(spread, spread, split_first),
        check_vma=False,
    )
```
